256 devices in a mesh: blk: 32 (over x, z), leaf: 4 (over y), samp: 2 (over core).
Axes of the slice: x: 4, y: 4, z: 8, core: 2. Of those that a mesh axis runs over, the one named last changes fastest.
Arguments:
- points: float32 [3, 32768], P(None, ('blk', 'leaf')), may hold values from 0 to 64, as said below
- neighbors: int32 [128, 8], P(('blk', 'leaf')), may hold values from -1 to 127, as said below
- omega: float32 [512, 32768], P(None, ('blk', 'leaf')), may hold values from -6 to 6
- observed: float32 [32768], P(('blk', 'leaf')), may hold values from -6 to 6
- prior_draws: float32 [64, 32768], P('samp', ('blk', 'leaf')), may hold values from -6 to 6
Outputs:
- weights: float32 [64, 32768], P('samp', ('blk', 'leaf'))
- residual: float32 [64, 32768], P('samp', ('blk', 'leaf'))
The draws below stay inside these ranges and needn't reach their ends.
Inputs may be any that keep to these rules, and one draw needn't show every extreme that they name: Block g's points lie in the unit cell with integer corner (cx, cy, cz), where cx // 2 = g // 4 and 0 <= cy, cz < 3. `neighbors`: row g lists in ascending order every block h whose unit cell touches g's (cells at most one apart in every coordinate, the first taken periodic of period 2 * 32), which includes every block with a point within distance 1 of a point of g, followed by -1 in the unused slots; the relation is symmetric, and every listed block has a slab index h // 4 equal to or cyclically next to g // 4.
All inputs are finite; a program needn't handle non-finite values.
Results may differ from the reference program's by a relative error of at most 0.0003.
Values sent between devices are 32-bit elements; how exact they have to be, the bound alone decides.
A program may use at most 64 MiB of HBM per device.

```python
import jax
import jax.numpy as jnp
from jax import lax

PB = 256
S = 512
SAMPLES = 64
ITERS = 2
CELLS = 3
BPS = 4
NB = 8
NBLOCKS = 128
NPTS = 32768
N_BLK = 32


def cell_table(key):
    folded = jax.random.fold_in(key, 7)
    draw_x, draw_y, draw_z = jax.random.split(folded, 3)
    block_ids = jnp.arange(NBLOCKS, dtype=jnp.int32)
    slab_ids = block_ids // BPS
    cell_x = 2 * slab_ids + jax.random.randint(draw_x, (NBLOCKS,), 0, 2, dtype=jnp.int32)
    cell_y = jax.random.randint(draw_y, (NBLOCKS,), 0, CELLS, dtype=jnp.int32)
    cell_z = jax.random.randint(draw_z, (NBLOCKS,), 0, CELLS, dtype=jnp.int32)
    return (cell_x, cell_y, cell_z)


def draw_points(key, part):
    cell_x, cell_y, cell_z = cell_table(key)
    offsets = jax.random.uniform(jax.random.fold_in(key, 11), (3, NBLOCKS, PB), jnp.float32)
    corner = jnp.stack([cell_x, cell_y, cell_z]).astype(jnp.float32)
    return (corner[:, :, None] + offsets).reshape(3, NPTS)


def draw_neighbors(key, part):
    cell_x, cell_y, cell_z = cell_table(key)
    block_ids = jnp.arange(NBLOCKS, dtype=jnp.int32)
    slab_ids = block_ids // BPS
    shifts = jnp.arange(3, dtype=jnp.int32) - 1
    within = jnp.arange(BPS, dtype=jnp.int32)
    candidates = jnp.mod(slab_ids[:, None, None] + shifts[None, :, None], N_BLK) * BPS + within[None, None, :]
    candidates = candidates.reshape(NBLOCKS, 3 * BPS)
    gap_x = jnp.mod(cell_x[candidates] - cell_x[:, None], 2 * N_BLK)
    adjacent = (gap_x <= 1) | (gap_x >= 2 * N_BLK - 1)
    adjacent = adjacent & (jnp.abs(cell_y[candidates] - cell_y[:, None]) <= 1)
    adjacent = adjacent & (jnp.abs(cell_z[candidates] - cell_z[:, None]) <= 1)
    sort_keys = jnp.where(adjacent, candidates, NBLOCKS)
    ordered = jnp.sort(sort_keys, axis=1)[:, :NB]
    return jnp.where(ordered == NBLOCKS, -1, ordered).astype(jnp.int32)


def block_scale(own_key, shape, cuts, smallest, largest):
    gain, own = 1.0, jax.random.fold_in(own_key, 6)
    for position, parts in cuts:
        steps = jnp.exp(jax.random.uniform(jax.random.fold_in(own, position), (parts,), jnp.float32, smallest / len(cuts), largest / len(cuts)))
        gain = gain * jnp.repeat(steps, shape[position] // parts).reshape([-1 if axis == position else 1 for axis in range(len(shape))])
    return gain


def gaussian(own_key, shape, deviation, reach, cuts=(), held_as=jnp.bfloat16):
    loudness = block_scale(own_key, shape, cuts, -0.22, 0.18) if cuts else 1.0
    entries = jax.random.normal(own_key, shape, jnp.float32) * deviation * loudness
    return jnp.minimum(jnp.maximum(entries, -reach), reach).astype(held_as)


def setup_inputs(seed: int = 0) -> dict:
    keys = jax.random.split(jax.random.key(seed), 6)
    return {
        "points": draw_points(jax.random.fold_in(keys[5], 71), 0),
        "neighbors": draw_neighbors(jax.random.fold_in(keys[5], 71), 0),
        "omega": gaussian(keys[2], (S, NPTS), 1.0, 6.0, ((1, 128),), jnp.float32),
        "observed": gaussian(keys[3], (NPTS,), 1.0, 6.0, ((0, 128),), jnp.float32),
        "prior_draws": gaussian(keys[4], (SAMPLES, NPTS), 1.0, 6.0, ((0, 2), (1, 128)), jnp.float32),
    }


support_radius = 0.8
noise_variance = 1.0
sketch_shift = 1.0

def wendland(row_points, column_points, period):
    offset = row_points[None, :, :, None] - column_points[:, :, None, :]
    half_period = 0.5 * period
    along_x = jnp.mod(offset[:, 0] + half_period, period) - half_period
    squared = along_x * along_x + offset[:, 1] * offset[:, 1] + offset[:, 2] * offset[:, 2]
    radius = jnp.sqrt(squared) / support_radius
    remain = jnp.maximum(1.0 - radius, 0.0)
    return remain ** 4 * (4.0 * radius + 1.0)

def apply_kernel(values, points, neighbors):
    width = values.shape[0]
    point_blocks = points.reshape(3, NBLOCKS, PB).transpose(1, 0, 2)
    value_blocks = values.reshape(width, NBLOCKS, PB)
    period = 2.0 * N_BLK

    def block_rows(packed):
        row_points, listed = packed
        usable = listed >= 0
        safe_ids = jnp.where(usable, listed, 0).astype(jnp.int32)
        kernel_tile = wendland(row_points, point_blocks[safe_ids], period)
        kernel_tile = kernel_tile * usable[:, None, None].astype(kernel_tile.dtype)
        picked = jnp.take(value_blocks, safe_ids, axis=1)
        return jnp.einsum('cnj,nij->ci', picked, kernel_tile, precision=lax.Precision.HIGHEST)
    applied = lax.map(block_rows, (point_blocks, neighbors))
    return applied.transpose(1, 0, 2).reshape(width, NPTS)

def high_dot(left, right):
    return jnp.dot(left, right, precision=lax.Precision.HIGHEST, preferred_element_type=left.dtype)

def inverse_apply(vectors, basis, wood_factor):
    projected = high_dot(basis, vectors.T)
    first_solve = lax.linalg.triangular_solve(wood_factor, projected, left_side=True, lower=True)
    solved = lax.linalg.triangular_solve(wood_factor, first_solve, left_side=True, lower=True, transpose_a=True)
    return (vectors - high_dot(solved.T, basis)) / noise_variance

def reference(points, neighbors, omega, observed, prior_draws):
    sketch = apply_kernel(omega, points, neighbors) + sketch_shift * omega
    core_gram = high_dot(omega, sketch.T)
    core_gram = 0.5 * (core_gram + core_gram.T)
    factor = jnp.linalg.cholesky(core_gram)
    basis = lax.linalg.triangular_solve(factor, sketch, left_side=True, lower=True)
    basis_gram = high_dot(basis, basis.T)
    woodbury = noise_variance * jnp.eye(S, dtype=basis.dtype) + 0.5 * (basis_gram + basis_gram.T)
    wood_factor = jnp.linalg.cholesky(woodbury)
    rhs = observed[None, :] - prior_draws
    weights = jnp.zeros_like(rhs)
    residual = rhs
    precond = inverse_apply(residual, basis, wood_factor)
    direction = precond
    inner_now = lax.optimization_barrier(jnp.sum(residual * precond, axis=1))
    for step_index in range(ITERS):
        image = apply_kernel(direction, points, neighbors) + noise_variance * direction
        step_size = inner_now / lax.optimization_barrier(jnp.sum(direction * image, axis=1))
        weights = weights + step_size[:, None] * direction
        residual = residual - step_size[:, None] * image
        if step_index + 1 < ITERS:
            precond = inverse_apply(residual, basis, wood_factor)
            inner_next = lax.optimization_barrier(jnp.sum(residual * precond, axis=1))
            direction = precond + (inner_next / inner_now)[:, None] * direction
            inner_now = inner_next
    return (weights, residual)
```

```python
import jax
import jax.numpy as jnp
from jax import lax
from jax.sharding import PartitionSpec as P

PB = 256
ITERS = 2


support_radius = 0.8
noise_variance = 1.0
sketch_shift = 1.0

ALL_AXES = ("blk", "leaf", "samp")


def shifted_2(block, axis, distance):
    devices = range(lax.axis_size(axis))
    route = [((i - distance) % len(devices), i) for i in devices]
    return lax.ppermute(block, axis, route)


def wendland(row_points, column_points, period):
    offset = row_points[None, :, :, None] - column_points[:, :, None, :]
    half_period = 0.5 * period
    along_x = jnp.mod(offset[:, 0] + half_period, period) - half_period
    squared = along_x * along_x + offset[:, 1] * offset[:, 1] + offset[:, 2] * offset[:, 2]
    radius = jnp.sqrt(squared) / support_radius
    remain = jnp.maximum(1.0 - radius, 0.0)
    return remain**4 * (4.0 * radius + 1.0)


def high_dot(left, right):
    return jnp.dot(left, right, precision=lax.Precision.HIGHEST, preferred_element_type=jnp.float32)


def shifted(values, offset_by):
    return shifted_2(values, "blk", offset_by)


def beside_all(values):
    slab_values = lax.all_gather(values, "leaf", axis=1, tiled=True)
    return jnp.concatenate([shifted(slab_values, 1), slab_values, shifted(slab_values, -1)], axis=1)


def lower_solve(factor, values):
    return lax.linalg.triangular_solve(factor, values, left_side=True, lower=True)


def local(points, neighbors, omega, observed, prior_draws):
    blk_dev = neighbors.shape[0]
    cycle_count = lax.axis_size("blk")
    slab_blocks = blk_dev * lax.axis_size("leaf")
    period = 2.0 * cycle_count
    own_slab = lax.axis_index("blk")
    n_samp = lax.axis_size("samp")
    samp_idx = lax.axis_index("samp")
    usable = neighbors >= 0
    relative = jnp.mod(neighbors // slab_blocks - own_slab + 1, cycle_count)
    chosen = jnp.where(usable, relative * slab_blocks + jnp.mod(neighbors, slab_blocks), 0)
    usable_weight = usable.astype(jnp.float32)
    reach_points = beside_all(points)
    reach_blocks = reach_points.reshape(3, 3 * slab_blocks, PB).transpose(1, 0, 2)
    row_blocks = points.reshape(3, blk_dev, PB).transpose(1, 0, 2)

    kernel_tile = wendland(row_blocks[0], reach_blocks[chosen[0]], period)
    kernel_tile = kernel_tile * usable_weight[0][:, None, None]

    def apply_kernel(values):
        width = values.shape[0]
        reach = beside_all(values).reshape(width, 3 * slab_blocks, PB)
        picked = jnp.take(reach, chosen[0], axis=1)
        return jnp.einsum("cnj,nij->ci", picked, kernel_tile, precision=lax.Precision.HIGHEST)

    def slot(x):
        zeros = jnp.zeros((n_samp,) + x.shape, x.dtype)
        return lax.dynamic_update_index_in_dim(zeros, x, samp_idx, 0)

    def unslot(xs):
        return lax.dynamic_index_in_dim(xs, samp_idx, 0, keepdims=False)

    def total_per_samp(values):
        return jax.tree.map(unslot, lax.psum(jax.tree.map(slot, values), ALL_AXES))

    sketch = apply_kernel(omega) + sketch_shift * omega
    rhs = observed[None, :] - prior_draws
    half = PB // n_samp
    omega_half = lax.dynamic_slice_in_dim(omega, samp_idx * half, half, axis=1)
    sketch_half = lax.dynamic_slice_in_dim(sketch, samp_idx * half, half, axis=1)
    core_part = high_dot(omega_half, sketch_half.T)
    square_part = high_dot(sketch_half, sketch_half.T)
    rhs_part = slot(high_dot(sketch, rhs.T))
    core_gram, square_gram, rhs_proj = lax.psum((core_part, square_part, rhs_part), ALL_AXES)
    rhs_proj = unslot(rhs_proj)

    core_gram = 0.5 * (core_gram + core_gram.T)
    factor = jnp.linalg.cholesky(core_gram)
    basis = lower_solve(factor, sketch)
    half_solved = lower_solve(factor, square_gram)
    basis_gram = lower_solve(factor, half_solved.T)
    woodbury = noise_variance * jnp.eye(basis.shape[0], dtype=jnp.float32) + 0.5 * (
        basis_gram + basis_gram.T
    )
    wood_factor = jnp.linalg.cholesky(woodbury)

    def precond_from(vectors, projected):
        first_solve = lower_solve(wood_factor, projected)
        solved = lax.linalg.triangular_solve(
            wood_factor, first_solve, left_side=True, lower=True, transpose_a=True
        )
        return (vectors - high_dot(solved.T, basis)) / noise_variance

    residual = rhs
    projected = lower_solve(factor, rhs_proj)
    precond = precond_from(residual, projected)
    direction = precond
    weights = jnp.zeros_like(rhs)

    image = apply_kernel(direction) + noise_variance * direction
    inner_now, curvature, image_proj = total_per_samp(
        (
            jnp.sum(residual * precond, axis=1),
            jnp.sum(direction * image, axis=1),
            high_dot(basis, image.T),
        )
    )
    step_size = inner_now / curvature
    weights = weights + step_size[:, None] * direction
    residual = residual - step_size[:, None] * image
    projected = projected - step_size[None, :] * image_proj
    precond = precond_from(residual, projected)
    inner_next = total_per_samp(jnp.sum(residual * precond, axis=1))
    direction = precond + (inner_next / inner_now)[:, None] * direction
    inner_now = inner_next

    image = apply_kernel(direction) + noise_variance * direction
    curvature = total_per_samp(jnp.sum(direction * image, axis=1))
    step_size = inner_now / curvature
    weights = weights + step_size[:, None] * direction
    residual = residual - step_size[:, None] * image
    return (weights, residual)


def solution(mesh):
    in_specs = (
        P(None, ("blk", "leaf")),
        P(("blk", "leaf"), None),
        P(None, ("blk", "leaf")),
        P(("blk", "leaf")),
        P("samp", ("blk", "leaf")),
    )
    out_specs = (P("samp", ("blk", "leaf")), P("samp", ("blk", "leaf")))
    return jax.shard_map(local, mesh=mesh, in_specs=in_specs, out_specs=out_specs, check_vma=False)
```

```python
import jax
import jax.numpy as jnp
from jax import lax
from jax.sharding import PartitionSpec as P

PB = 256
ITERS = 2


support_radius = 0.8
noise_variance = 1.0
sketch_shift = 1.0

ALL_AXES = ("blk", "leaf", "samp")


def shifted_2(block, axis, distance):
    devices = range(lax.axis_size(axis))
    route = [((i - distance) % len(devices), i) for i in devices]
    return lax.ppermute(block, axis, route)


def wendland(row_points, column_points, period):
    offset = row_points[None, :, :, None] - column_points[:, :, None, :]
    half_period = 0.5 * period
    along_x = jnp.mod(offset[:, 0] + half_period, period) - half_period
    squared = along_x * along_x + offset[:, 1] * offset[:, 1] + offset[:, 2] * offset[:, 2]
    radius = jnp.sqrt(squared) / support_radius
    remain = jnp.maximum(1.0 - radius, 0.0)
    return remain**4 * (4.0 * radius + 1.0)


def high_dot(left, right):
    return jnp.dot(left, right, precision=lax.Precision.HIGHEST, preferred_element_type=jnp.float32)


def shifted(values, offset_by):
    return shifted_2(values, "blk", offset_by)


def beside_all(values):
    slab_values = lax.all_gather(values, "leaf", axis=1, tiled=True)
    return jnp.concatenate([shifted(slab_values, 1), slab_values, shifted(slab_values, -1)], axis=1)


def lower_solve(factor, values):
    return lax.linalg.triangular_solve(factor, values, left_side=True, lower=True)


def local(points, neighbors, omega, observed, prior_draws):
    blk_dev = neighbors.shape[0]
    cycle_count = lax.axis_size("blk")
    slab_blocks = blk_dev * lax.axis_size("leaf")
    period = 2.0 * cycle_count
    own_slab = lax.axis_index("blk")
    n_samp = lax.axis_size("samp")
    samp_idx = lax.axis_index("samp")
    usable = neighbors >= 0
    relative = jnp.mod(neighbors // slab_blocks - own_slab + 1, cycle_count)
    chosen = jnp.where(usable, relative * slab_blocks + jnp.mod(neighbors, slab_blocks), 0)
    usable_weight = usable.astype(jnp.float32)
    reach_points = beside_all(points)
    reach_blocks = reach_points.reshape(3, 3 * slab_blocks, PB).transpose(1, 0, 2)
    row_blocks = points.reshape(3, blk_dev, PB).transpose(1, 0, 2)

    kernel_tile = wendland(row_blocks[0], reach_blocks[chosen[0]], period)
    kernel_tile = kernel_tile * usable_weight[0][:, None, None]

    def apply_kernel(values):
        width = values.shape[0]
        reach = beside_all(values).reshape(width, 3 * slab_blocks, PB)
        picked = jnp.take(reach, chosen[0], axis=1)
        return jnp.einsum("cnj,nij->ci", picked, kernel_tile, precision=lax.Precision.HIGHEST)

    def slot(x):
        zeros = jnp.zeros((n_samp,) + x.shape, x.dtype)
        return lax.dynamic_update_index_in_dim(zeros, x, samp_idx, 0)

    def unslot(xs):
        return lax.dynamic_index_in_dim(xs, samp_idx, 0, keepdims=False)

    def total_per_samp(values):
        return jax.tree.map(unslot, lax.psum(jax.tree.map(slot, values), ALL_AXES))

    sketch = apply_kernel(omega) + sketch_shift * omega
    rhs = observed[None, :] - prior_draws
    half = PB // n_samp
    omega_half = lax.dynamic_slice_in_dim(omega, samp_idx * half, half, axis=1)
    sketch_half = lax.dynamic_slice_in_dim(sketch, samp_idx * half, half, axis=1)
    core_part = high_dot(omega_half, sketch_half.T)
    square_part = high_dot(sketch_half, sketch_half.T)
    joint_part = 0.5 * (core_part + core_part.T) + 0.5 * (square_part + square_part.T)
    rhs_part = slot(high_dot(sketch, rhs.T))
    joint_gram, rhs_proj = lax.psum((joint_part, rhs_part), ALL_AXES)
    rhs_proj = unslot(rhs_proj)

    joint_factor = jnp.linalg.cholesky(joint_gram)

    def precond_from(vectors, projected):
        first_solve = lower_solve(joint_factor, projected)
        solved = lax.linalg.triangular_solve(
            joint_factor, first_solve, left_side=True, lower=True, transpose_a=True
        )
        return (vectors - high_dot(solved.T, sketch)) / noise_variance

    residual = rhs
    projected = rhs_proj
    precond = precond_from(residual, projected)
    direction = precond
    weights = jnp.zeros_like(rhs)

    image = apply_kernel(direction) + noise_variance * direction
    inner_now, curvature, image_proj = total_per_samp(
        (
            jnp.sum(residual * precond, axis=1),
            jnp.sum(direction * image, axis=1),
            high_dot(sketch, image.T),
        )
    )
    step_size = inner_now / curvature
    weights = weights + step_size[:, None] * direction
    residual = residual - step_size[:, None] * image
    projected = projected - step_size[None, :] * image_proj
    precond = precond_from(residual, projected)
    inner_next = total_per_samp(jnp.sum(residual * precond, axis=1))
    direction = precond + (inner_next / inner_now)[:, None] * direction
    inner_now = inner_next

    image = apply_kernel(direction) + noise_variance * direction
    curvature = total_per_samp(jnp.sum(direction * image, axis=1))
    step_size = inner_now / curvature
    weights = weights + step_size[:, None] * direction
    residual = residual - step_size[:, None] * image
    return (weights, residual)


def solution(mesh):
    in_specs = (
        P(None, ("blk", "leaf")),
        P(("blk", "leaf"), None),
        P(None, ("blk", "leaf")),
        P(("blk", "leaf")),
        P("samp", ("blk", "leaf")),
    )
    out_specs = (P("samp", ("blk", "leaf")), P("samp", ("blk", "leaf")))
    return jax.shard_map(local, mesh=mesh, in_specs=in_specs, out_specs=out_specs, check_vma=False)
```

```python
import jax
import jax.numpy as jnp
from jax import lax
from jax.sharding import PartitionSpec as P
from jax.experimental import pallas as pl
from jax.experimental.pallas import tpu as pltpu

PB = 256
ITERS = 2


support_radius = 0.8
noise_variance = 1.0
sketch_shift = 1.0

ALL_AXES = ("blk", "leaf", "samp")


def shifted_2(block, axis, distance):
    devices = range(lax.axis_size(axis))
    route = [((i - distance) % len(devices), i) for i in devices]
    return lax.ppermute(block, axis, route)


def wendland(row_points, column_points, period):
    offset = row_points[None, :, :, None] - column_points[:, :, None, :]
    half_period = 0.5 * period
    along_x = jnp.mod(offset[:, 0] + half_period, period) - half_period
    squared = along_x * along_x + offset[:, 1] * offset[:, 1] + offset[:, 2] * offset[:, 2]
    radius = jnp.sqrt(squared) / support_radius
    remain = jnp.maximum(1.0 - radius, 0.0)
    return remain**4 * (4.0 * radius + 1.0)


def high_dot(left, right):
    return jnp.dot(left, right, precision=lax.Precision.HIGHEST, preferred_element_type=jnp.float32)


def shifted(values, offset_by):
    return shifted_2(values, "blk", offset_by)


def beside_all(values):
    slab_values = lax.all_gather(values, "leaf", axis=1, tiled=True)
    return jnp.concatenate([shifted(slab_values, 1), slab_values, shifted(slab_values, -1)], axis=1)


def blk_split(n_blk):
    if n_blk % 8 == 0 and n_blk > 8:
        return (8, n_blk // 8)
    return (n_blk, 1)


def reduce_phases():
    inner, outer = blk_split(lax.axis_size("blk"))
    phases = [("leaf", lax.axis_size("leaf"), 1), ("blk", inner, 1)]
    if outer > 1:
        phases.append(("blk", outer, inner))
    return tuple(p for p in phases if p[1] > 1)


def group_peer(axis, n, stride, k):
    idx = lax.axis_index(axis)
    own = (idx // stride) % n
    return own, idx + ((own + k) % n - own) * stride


def sum_kernel(phases, x_ref, o_ref, recv, send_sem, recv_sem):
    barrier = pltpu.get_barrier_semaphore()
    greeted = 0
    for axis, n, stride in phases:
        for k in range(1, n):
            _, peer = group_peer(axis, n, stride, k)
            pl.semaphore_signal(
                barrier, 1, device_id={axis: peer}, device_id_type=pl.DeviceIdType.MESH
            )
            greeted += 1
    pl.semaphore_wait(barrier, greeted)
    acc = x_ref[...]
    for p, (axis, n, stride) in enumerate(phases):
        recv[p, 0] = acc
        copies = []
        for k in range(1, n):
            own, peer = group_peer(axis, n, stride, k)
            copy = pltpu.make_async_remote_copy(
                src_ref=x_ref if p == 0 else recv.at[p, 0],
                dst_ref=recv.at[p, k],
                send_sem=send_sem.at[p, k],
                recv_sem=recv_sem.at[p, k],
                device_id={axis: peer},
                device_id_type=pl.DeviceIdType.MESH,
            )
            copy.start()
            copies.append(copy)
        for copy in copies:
            copy.wait()
        own, _ = group_peer(axis, n, stride, 0)
        terms = [recv[p, (own - j) % n] for j in range(n)]
        acc = terms[0]
        for term in terms[1:]:
            acc = acc + term
    o_ref[...] = acc


def group_sum(values, collective_id):
    phases = reduce_phases()
    rows = values.shape[0]
    widest = max(n for _, n, _ in phases)
    return pl.pallas_call(
        lambda *refs: sum_kernel(phases, *refs),
        out_shape=jax.ShapeDtypeStruct(values.shape, jnp.float32),
        in_specs=[pl.BlockSpec(memory_space=pltpu.VMEM)],
        out_specs=pl.BlockSpec(memory_space=pltpu.VMEM),
        scratch_shapes=[
            pltpu.VMEM((len(phases), widest, rows, 128), jnp.float32),
            pltpu.SemaphoreType.DMA((len(phases), widest)),
            pltpu.SemaphoreType.DMA((len(phases), widest)),
        ],
        compiler_params=pltpu.CompilerParams(collective_id=collective_id, has_side_effects=True),
    )(values)


def lower_solve(factor, values):
    return lax.linalg.triangular_solve(factor, values, left_side=True, lower=True)


def local(points, neighbors, omega, observed, prior_draws):
    blk_dev = neighbors.shape[0]
    cycle_count = lax.axis_size("blk")
    slab_blocks = blk_dev * lax.axis_size("leaf")
    period = 2.0 * cycle_count
    own_slab = lax.axis_index("blk")
    n_samp = lax.axis_size("samp")
    samp_idx = lax.axis_index("samp")
    usable = neighbors >= 0
    relative = jnp.mod(neighbors // slab_blocks - own_slab + 1, cycle_count)
    chosen = jnp.where(usable, relative * slab_blocks + jnp.mod(neighbors, slab_blocks), 0)
    usable_weight = usable.astype(jnp.float32)
    reach_points = beside_all(points)
    reach_blocks = reach_points.reshape(3, 3 * slab_blocks, PB).transpose(1, 0, 2)
    row_blocks = points.reshape(3, blk_dev, PB).transpose(1, 0, 2)

    kernel_tile = wendland(row_blocks[0], reach_blocks[chosen[0]], period)
    kernel_tile = kernel_tile * usable_weight[0][:, None, None]

    def apply_kernel(values):
        width = values.shape[0]
        reach = beside_all(values).reshape(width, 3 * slab_blocks, PB)
        picked = jnp.take(reach, chosen[0], axis=1)
        return jnp.einsum("cnj,nij->ci", picked, kernel_tile, precision=lax.Precision.HIGHEST)

    def slot(x):
        zeros = jnp.zeros((n_samp,) + x.shape, x.dtype)
        return lax.dynamic_update_index_in_dim(zeros, x, samp_idx, 0)

    def unslot(xs):
        return lax.dynamic_index_in_dim(xs, samp_idx, 0, keepdims=False)

    def total_per_samp(values):
        return jax.tree.map(unslot, lax.psum(jax.tree.map(slot, values), ALL_AXES))

    sketch = apply_kernel(omega) + sketch_shift * omega
    rhs = observed[None, :] - prior_draws
    half = PB // n_samp
    omega_half = lax.dynamic_slice_in_dim(omega, samp_idx * half, half, axis=1)
    sketch_half = lax.dynamic_slice_in_dim(sketch, samp_idx * half, half, axis=1)
    core_part = high_dot(omega_half, sketch_half.T)
    square_part = high_dot(sketch_half, sketch_half.T)
    joint_part = 0.5 * (core_part + core_part.T) + 0.5 * (square_part + square_part.T)
    rhs_part = slot(high_dot(sketch, rhs.T))
    joint_gram, rhs_proj = lax.psum((joint_part, rhs_part), ALL_AXES)
    rhs_proj = unslot(rhs_proj)

    joint_factor = jnp.linalg.cholesky(joint_gram)

    def precond_from(vectors, projected):
        first_solve = lower_solve(joint_factor, projected)
        solved = lax.linalg.triangular_solve(
            joint_factor, first_solve, left_side=True, lower=True, transpose_a=True
        )
        return (vectors - high_dot(solved.T, sketch)) / noise_variance

    residual = rhs
    projected = rhs_proj
    precond = precond_from(residual, projected)
    direction = precond
    weights = jnp.zeros_like(rhs)

    width = rhs.shape[0]
    sketch_rows = sketch.shape[0]

    def pack_scalars(*vectors):
        rows = jnp.stack(vectors)
        return jnp.pad(rows, ((0, 8 - rows.shape[0]), (0, 128 - width)))

    image = apply_kernel(direction) + noise_variance * direction
    image_proj = high_dot(sketch, image.T).reshape(sketch_rows * width // 128, 128)
    packed = jnp.concatenate(
        [
            image_proj,
            pack_scalars(
                jnp.sum(residual * precond, axis=1), jnp.sum(direction * image, axis=1)
            ),
        ]
    )
    packed = group_sum(packed, 0)
    image_proj = packed[:-8].reshape(sketch_rows, width)
    inner_now = packed[-8, :width]
    curvature = packed[-7, :width]
    step_size = inner_now / curvature
    weights = weights + step_size[:, None] * direction
    residual = residual - step_size[:, None] * image
    projected = projected - step_size[None, :] * image_proj
    precond = precond_from(residual, projected)
    inner_next = group_sum(pack_scalars(jnp.sum(residual * precond, axis=1)), 1)[0, :width]
    direction = precond + (inner_next / inner_now)[:, None] * direction
    inner_now = inner_next

    image = apply_kernel(direction) + noise_variance * direction
    curvature = group_sum(pack_scalars(jnp.sum(direction * image, axis=1)), 1)[0, :width]
    step_size = inner_now / curvature
    weights = weights + step_size[:, None] * direction
    residual = residual - step_size[:, None] * image
    return (weights, residual)


def solution(mesh):
    in_specs = (
        P(None, ("blk", "leaf")),
        P(("blk", "leaf"), None),
        P(None, ("blk", "leaf")),
        P(("blk", "leaf")),
        P("samp", ("blk", "leaf")),
    )
    out_specs = (P("samp", ("blk", "leaf")), P("samp", ("blk", "leaf")))
    return jax.shard_map(local, mesh=mesh, in_specs=in_specs, out_specs=out_specs, check_vma=False)
```

```python
import jax
import jax.numpy as jnp
from jax import lax
from jax.sharding import PartitionSpec as P
from jax.experimental import pallas as pl
from jax.experimental.pallas import tpu as pltpu

PB = 256
ITERS = 2


support_radius = 0.8
noise_variance = 1.0
sketch_shift = 1.0

ALL_AXES = ("blk", "leaf", "samp")


def shifted_2(block, axis, distance):
    devices = range(lax.axis_size(axis))
    route = [((i - distance) % len(devices), i) for i in devices]
    return lax.ppermute(block, axis, route)


def wendland(row_points, column_points, period):
    offset = row_points[None, :, :, None] - column_points[:, :, None, :]
    half_period = 0.5 * period
    along_x = jnp.mod(offset[:, 0] + half_period, period) - half_period
    squared = along_x * along_x + offset[:, 1] * offset[:, 1] + offset[:, 2] * offset[:, 2]
    radius = jnp.sqrt(squared) / support_radius
    remain = jnp.maximum(1.0 - radius, 0.0)
    return remain**4 * (4.0 * radius + 1.0)


def high_dot(left, right):
    return jnp.dot(left, right, precision=lax.Precision.HIGHEST, preferred_element_type=jnp.float32)


def shifted(values, offset_by):
    return shifted_2(values, "blk", offset_by)


def beside_all(values):
    slab_values = lax.all_gather(values, "leaf", axis=1, tiled=True)
    return jnp.concatenate([shifted(slab_values, 1), slab_values, shifted(slab_values, -1)], axis=1)


def blk_split(n_blk):
    if n_blk % 8 == 0 and n_blk > 8:
        return (8, n_blk // 8)
    return (n_blk, 1)


def reduce_phases():
    inner, outer = blk_split(lax.axis_size("blk"))
    phases = [("leaf", lax.axis_size("leaf"), 1), ("blk", inner, 1)]
    if outer > 1:
        phases.append(("blk", outer, inner))
    return tuple(p for p in phases if p[1] > 1)


def group_peer(axis, n, stride, k):
    idx = lax.axis_index(axis)
    own = (idx // stride) % n
    return own, idx + ((own + k) % n - own) * stride


def sum_kernel(phases, x_ref, o_ref, recv, send_sem, recv_sem):
    barrier = pltpu.get_barrier_semaphore()
    greeted = 0
    for axis, n, stride in phases:
        for k in range(1, n):
            _, peer = group_peer(axis, n, stride, k)
            pl.semaphore_signal(
                barrier, 1, device_id={axis: peer}, device_id_type=pl.DeviceIdType.MESH
            )
            greeted += 1
    pl.semaphore_wait(barrier, greeted)
    acc = x_ref[...]
    for p, (axis, n, stride) in enumerate(phases):
        recv[p, 0] = acc
        copies = []
        for k in range(1, n):
            own, peer = group_peer(axis, n, stride, k)
            copy = pltpu.make_async_remote_copy(
                src_ref=x_ref if p == 0 else recv.at[p, 0],
                dst_ref=recv.at[p, k],
                send_sem=send_sem.at[p, k],
                recv_sem=recv_sem.at[p, k],
                device_id={axis: peer},
                device_id_type=pl.DeviceIdType.MESH,
            )
            copy.start()
            copies.append(copy)
        for copy in copies:
            copy.wait()
        own, _ = group_peer(axis, n, stride, 0)
        terms = [recv[p, (own - j) % n] for j in range(n)]
        acc = terms[0]
        for term in terms[1:]:
            acc = acc + term
    o_ref[...] = acc


def group_sum(values, collective_id):
    phases = reduce_phases()
    rows = values.shape[0]
    widest = max(n for _, n, _ in phases)
    return pl.pallas_call(
        lambda *refs: sum_kernel(phases, *refs),
        out_shape=jax.ShapeDtypeStruct(values.shape, jnp.float32),
        in_specs=[pl.BlockSpec(memory_space=pltpu.VMEM)],
        out_specs=pl.BlockSpec(memory_space=pltpu.VMEM),
        scratch_shapes=[
            pltpu.VMEM((len(phases), widest, rows, 128), jnp.float32),
            pltpu.SemaphoreType.DMA((len(phases), widest)),
            pltpu.SemaphoreType.DMA((len(phases), widest)),
        ],
        compiler_params=pltpu.CompilerParams(collective_id=collective_id, has_side_effects=True),
    )(values)


def gram_kernel(phases, x_ref, o_ref, *scratch):
    count = len(phases)
    recvs = scratch[:count]
    sums = scratch[count : 2 * count - 1]
    full = scratch[2 * count - 1]
    rs_send, rs_recv, ag_send, ag_recv = scratch[2 * count :]
    barrier = pltpu.get_barrier_semaphore()
    greeted = 0
    for axis, n, stride in phases:
        for k in range(1, n):
            _, peer = group_peer(axis, n, stride, k)
            pl.semaphore_signal(
                barrier, 1, device_id={axis: peer}, device_id_type=pl.DeviceIdType.MESH
            )
            greeted += 1
    pl.semaphore_wait(barrier, greeted)
    source = x_ref
    length = x_ref.shape[0]
    offset = 0
    for p, (axis, n, stride) in enumerate(phases):
        own, _ = group_peer(axis, n, stride, 0)
        part = length // n
        recv = recvs[p]
        recv[0] = source[pl.ds(pl.multiple_of(own * part, 8), part)]
        copies = []
        for k in range(1, n):
            _, peer = group_peer(axis, n, stride, k)
            chunk = (own + k) % n
            copy = pltpu.make_async_remote_copy(
                src_ref=source.at[pl.ds(pl.multiple_of(chunk * part, 8), part)],
                dst_ref=recv.at[k],
                send_sem=rs_send.at[p, k],
                recv_sem=rs_recv.at[p, k],
                device_id={axis: peer},
                device_id_type=pl.DeviceIdType.MESH,
            )
            copy.start()
            copies.append(copy)
        for copy in copies:
            copy.wait()
        acc = recv[own % n]
        for j in range(1, n):
            acc = acc + recv[(own - j) % n]
        offset = offset + own * part
        length = part
        if p < count - 1:
            sums[p][...] = acc
            source = sums[p]
        else:
            full[pl.ds(pl.multiple_of(offset, 8), part)] = acc
    for p in reversed(range(count)):
        axis, n, stride = phases[p]
        own, _ = group_peer(axis, n, stride, 0)
        here = full.at[pl.ds(pl.multiple_of(offset, 8), length)]
        copies = []
        for k in range(1, n):
            _, peer = group_peer(axis, n, stride, k)
            copy = pltpu.make_async_remote_copy(
                src_ref=here,
                dst_ref=here,
                send_sem=ag_send.at[p, k],
                recv_sem=ag_recv.at[p, k],
                device_id={axis: peer},
                device_id_type=pl.DeviceIdType.MESH,
            )
            copy.start()
            copies.append(copy)
        for copy in copies:
            copy.wait()
        offset = offset - own * length
        length = length * n
    o_ref[...] = full[...]


def gram_sum(values, collective_id):
    phases = (("samp", lax.axis_size("samp"), 1),) + reduce_phases()
    phases = tuple(p for p in phases if p[1] > 1)
    rows = values.shape[0]
    widest = max(n for _, n, _ in phases)
    recvs, sums = [], []
    length = rows
    for p, (_, n, _) in enumerate(phases):
        length //= n
        recvs.append(pltpu.VMEM((n, length, 128), jnp.float32))
        if p < len(phases) - 1:
            sums.append(pltpu.VMEM((length, 128), jnp.float32))
    semaphores = [pltpu.SemaphoreType.DMA((len(phases), widest)) for _ in range(4)]
    return pl.pallas_call(
        lambda *refs: gram_kernel(phases, *refs),
        out_shape=jax.ShapeDtypeStruct(values.shape, jnp.float32),
        in_specs=[pl.BlockSpec(memory_space=pltpu.VMEM)],
        out_specs=pl.BlockSpec(memory_space=pltpu.VMEM),
        scratch_shapes=recvs + sums + [pltpu.VMEM((rows, 128), jnp.float32)] + semaphores,
        compiler_params=pltpu.CompilerParams(collective_id=collective_id, has_side_effects=True),
    )(values)


def lower_solve(factor, values):
    return lax.linalg.triangular_solve(factor, values, left_side=True, lower=True)


def local(points, neighbors, omega, observed, prior_draws):
    blk_dev = neighbors.shape[0]
    cycle_count = lax.axis_size("blk")
    slab_blocks = blk_dev * lax.axis_size("leaf")
    period = 2.0 * cycle_count
    own_slab = lax.axis_index("blk")
    n_samp = lax.axis_size("samp")
    samp_idx = lax.axis_index("samp")
    usable = neighbors >= 0
    relative = jnp.mod(neighbors // slab_blocks - own_slab + 1, cycle_count)
    chosen = jnp.where(usable, relative * slab_blocks + jnp.mod(neighbors, slab_blocks), 0)
    usable_weight = usable.astype(jnp.float32)
    reach_points = beside_all(points)
    reach_blocks = reach_points.reshape(3, 3 * slab_blocks, PB).transpose(1, 0, 2)
    row_blocks = points.reshape(3, blk_dev, PB).transpose(1, 0, 2)

    kernel_tile = wendland(row_blocks[0], reach_blocks[chosen[0]], period)
    kernel_tile = kernel_tile * usable_weight[0][:, None, None]

    def apply_kernel(values):
        width = values.shape[0]
        reach = beside_all(values).reshape(width, 3 * slab_blocks, PB)
        picked = jnp.take(reach, chosen[0], axis=1)
        return jnp.einsum("cnj,nij->ci", picked, kernel_tile, precision=lax.Precision.HIGHEST)

    def slot(x):
        zeros = jnp.zeros((n_samp,) + x.shape, x.dtype)
        return lax.dynamic_update_index_in_dim(zeros, x, samp_idx, 0)

    def unslot(xs):
        return lax.dynamic_index_in_dim(xs, samp_idx, 0, keepdims=False)

    def total_per_samp(values):
        return jax.tree.map(unslot, lax.psum(jax.tree.map(slot, values), ALL_AXES))

    sketch = apply_kernel(omega) + sketch_shift * omega
    rhs = observed[None, :] - prior_draws
    half = PB // n_samp
    omega_half = lax.dynamic_slice_in_dim(omega, samp_idx * half, half, axis=1)
    sketch_half = lax.dynamic_slice_in_dim(sketch, samp_idx * half, half, axis=1)
    core_part = high_dot(omega_half, sketch_half.T)
    square_part = high_dot(sketch_half, sketch_half.T)
    joint_part = 0.5 * (core_part + core_part.T) + 0.5 * (square_part + square_part.T)
    rhs_proj = total_per_samp(high_dot(sketch, rhs.T))
    gram_rows = joint_part.shape[0]
    joint_gram = gram_sum(joint_part.reshape(gram_rows * gram_rows // 128, 128), 2)
    joint_gram = joint_gram.reshape(gram_rows, gram_rows)

    joint_factor = jnp.linalg.cholesky(joint_gram)

    def precond_from(vectors, projected):
        first_solve = lower_solve(joint_factor, projected)
        solved = lax.linalg.triangular_solve(
            joint_factor, first_solve, left_side=True, lower=True, transpose_a=True
        )
        return (vectors - high_dot(solved.T, sketch)) / noise_variance

    residual = rhs
    projected = rhs_proj
    precond = precond_from(residual, projected)
    direction = precond
    weights = jnp.zeros_like(rhs)

    width = rhs.shape[0]
    sketch_rows = sketch.shape[0]

    def pack_scalars(*vectors):
        rows = jnp.stack(vectors)
        return jnp.pad(rows, ((0, 8 - rows.shape[0]), (0, 128 - width)))

    image = apply_kernel(direction) + noise_variance * direction
    image_proj = high_dot(sketch, image.T).reshape(sketch_rows * width // 128, 128)
    packed = jnp.concatenate(
        [
            image_proj,
            pack_scalars(
                jnp.sum(residual * precond, axis=1), jnp.sum(direction * image, axis=1)
            ),
        ]
    )
    packed = group_sum(packed, 0)
    image_proj = packed[:-8].reshape(sketch_rows, width)
    inner_now = packed[-8, :width]
    curvature = packed[-7, :width]
    step_size = inner_now / curvature
    weights = weights + step_size[:, None] * direction
    residual = residual - step_size[:, None] * image
    projected = projected - step_size[None, :] * image_proj
    precond = precond_from(residual, projected)
    inner_next = group_sum(pack_scalars(jnp.sum(residual * precond, axis=1)), 1)[0, :width]
    direction = precond + (inner_next / inner_now)[:, None] * direction
    inner_now = inner_next

    image = apply_kernel(direction) + noise_variance * direction
    curvature = group_sum(pack_scalars(jnp.sum(direction * image, axis=1)), 1)[0, :width]
    step_size = inner_now / curvature
    weights = weights + step_size[:, None] * direction
    residual = residual - step_size[:, None] * image
    return (weights, residual)


def solution(mesh):
    in_specs = (
        P(None, ("blk", "leaf")),
        P(("blk", "leaf"), None),
        P(None, ("blk", "leaf")),
        P(("blk", "leaf")),
        P("samp", ("blk", "leaf")),
    )
    out_specs = (P("samp", ("blk", "leaf")), P("samp", ("blk", "leaf")))
    return jax.shard_map(local, mesh=mesh, in_specs=in_specs, out_specs=out_specs, check_vma=False)
```

```python
import jax
import jax.numpy as jnp
from jax import lax
from jax.sharding import PartitionSpec as P
from jax.experimental import pallas as pl
from jax.experimental.pallas import tpu as pltpu

PB = 256
ITERS = 2


support_radius = 0.8
noise_variance = 1.0
sketch_shift = 1.0

ALL_AXES = ("blk", "leaf", "samp")


def shifted_2(block, axis, distance):
    devices = range(lax.axis_size(axis))
    route = [((i - distance) % len(devices), i) for i in devices]
    return lax.ppermute(block, axis, route)


def wendland(row_points, column_points, period):
    offset = row_points[None, :, :, None] - column_points[:, :, None, :]
    half_period = 0.5 * period
    along_x = jnp.mod(offset[:, 0] + half_period, period) - half_period
    squared = along_x * along_x + offset[:, 1] * offset[:, 1] + offset[:, 2] * offset[:, 2]
    radius = jnp.sqrt(squared) / support_radius
    remain = jnp.maximum(1.0 - radius, 0.0)
    return remain**4 * (4.0 * radius + 1.0)


def high_dot(left, right):
    return jnp.dot(left, right, precision=lax.Precision.HIGHEST, preferred_element_type=jnp.float32)


def shifted(values, offset_by):
    return shifted_2(values, "blk", offset_by)


def beside_all(values):
    slab_values = lax.all_gather(values, "leaf", axis=1, tiled=True)
    return jnp.concatenate([shifted(slab_values, 1), slab_values, shifted(slab_values, -1)], axis=1)


def blk_split(n_blk):
    if n_blk % 8 == 0 and n_blk > 8:
        return (8, n_blk // 8)
    return (n_blk, 1)


def reduce_phases():
    inner, outer = blk_split(lax.axis_size("blk"))
    phases = [("leaf", lax.axis_size("leaf"), 1), ("blk", inner, 1)]
    if outer > 1:
        phases.append(("blk", outer, inner))
    return tuple(p for p in phases if p[1] > 1)


def group_peer(axis, n, stride, k):
    idx = lax.axis_index(axis)
    own = (idx // stride) % n
    return own, idx + ((own + k) % n - own) * stride


def sum_kernel(phases, x_ref, o_ref, recv, send_sem, recv_sem):
    barrier = pltpu.get_barrier_semaphore()
    greeted = 0
    for axis, n, stride in phases:
        for k in range(1, n):
            _, peer = group_peer(axis, n, stride, k)
            pl.semaphore_signal(
                barrier, 1, device_id={axis: peer}, device_id_type=pl.DeviceIdType.MESH
            )
            greeted += 1
    pl.semaphore_wait(barrier, greeted)
    acc = x_ref[...]
    for p, (axis, n, stride) in enumerate(phases):
        recv[p, 0] = acc
        copies = []
        for k in range(1, n):
            own, peer = group_peer(axis, n, stride, k)
            copy = pltpu.make_async_remote_copy(
                src_ref=x_ref if p == 0 else recv.at[p, 0],
                dst_ref=recv.at[p, k],
                send_sem=send_sem.at[p, k],
                recv_sem=recv_sem.at[p, k],
                device_id={axis: peer},
                device_id_type=pl.DeviceIdType.MESH,
            )
            copy.start()
            copies.append(copy)
        for copy in copies:
            copy.wait()
        own, _ = group_peer(axis, n, stride, 0)
        terms = [recv[p, (own - j) % n] for j in range(n)]
        acc = terms[0]
        for term in terms[1:]:
            acc = acc + term
    o_ref[...] = acc


def group_sum(values, collective_id):
    phases = reduce_phases()
    rows = values.shape[0]
    widest = max(n for _, n, _ in phases)
    return pl.pallas_call(
        lambda *refs: sum_kernel(phases, *refs),
        out_shape=jax.ShapeDtypeStruct(values.shape, jnp.float32),
        in_specs=[pl.BlockSpec(memory_space=pltpu.VMEM)],
        out_specs=pl.BlockSpec(memory_space=pltpu.VMEM),
        scratch_shapes=[
            pltpu.VMEM((len(phases), widest, rows, 128), jnp.float32),
            pltpu.SemaphoreType.DMA((len(phases), widest)),
            pltpu.SemaphoreType.DMA((len(phases), widest)),
        ],
        compiler_params=pltpu.CompilerParams(collective_id=collective_id, has_side_effects=True),
    )(values)


def gram_kernel(phases, x_ref, o_ref, *scratch):
    count = len(phases)
    recvs = scratch[:count]
    sums = scratch[count : 2 * count - 1]
    full = scratch[2 * count - 1]
    rs_send, rs_recv, ag_send, ag_recv = scratch[2 * count :]
    barrier = pltpu.get_barrier_semaphore()
    greeted = 0
    for axis, n, stride in phases:
        for k in range(1, n):
            _, peer = group_peer(axis, n, stride, k)
            pl.semaphore_signal(
                barrier, 1, device_id={axis: peer}, device_id_type=pl.DeviceIdType.MESH
            )
            greeted += 1
    pl.semaphore_wait(barrier, greeted)
    source = x_ref
    length = x_ref.shape[0]
    offset = 0
    for p, (axis, n, stride) in enumerate(phases):
        own, _ = group_peer(axis, n, stride, 0)
        part = length // n
        recv = recvs[p]
        recv[0] = source[pl.ds(pl.multiple_of(own * part, 8), part)]
        copies = []
        for k in range(1, n):
            _, peer = group_peer(axis, n, stride, k)
            chunk = (own + k) % n
            copy = pltpu.make_async_remote_copy(
                src_ref=source.at[pl.ds(pl.multiple_of(chunk * part, 8), part)],
                dst_ref=recv.at[k],
                send_sem=rs_send.at[p, k],
                recv_sem=rs_recv.at[p, k],
                device_id={axis: peer},
                device_id_type=pl.DeviceIdType.MESH,
            )
            copy.start()
            copies.append(copy)
        for copy in copies:
            copy.wait()
        acc = recv[own % n]
        for j in range(1, n):
            acc = acc + recv[(own - j) % n]
        offset = offset + own * part
        length = part
        if p < count - 1:
            sums[p][...] = acc
            source = sums[p]
        else:
            full[pl.ds(pl.multiple_of(offset, 8), part)] = acc
    for p in reversed(range(count)):
        axis, n, stride = phases[p]
        own, _ = group_peer(axis, n, stride, 0)
        here = full.at[pl.ds(pl.multiple_of(offset, 8), length)]
        copies = []
        for k in range(1, n):
            _, peer = group_peer(axis, n, stride, k)
            copy = pltpu.make_async_remote_copy(
                src_ref=here,
                dst_ref=here,
                send_sem=ag_send.at[p, k],
                recv_sem=ag_recv.at[p, k],
                device_id={axis: peer},
                device_id_type=pl.DeviceIdType.MESH,
            )
            copy.start()
            copies.append(copy)
        for copy in copies:
            copy.wait()
        offset = offset - own * length
        length = length * n
    o_ref[...] = full[...]


def gram_sum(values, collective_id):
    phases = (("samp", lax.axis_size("samp"), 1),) + reduce_phases()
    phases = tuple(p for p in phases if p[1] > 1)
    rows = values.shape[0]
    widest = max(n for _, n, _ in phases)
    recvs, sums = [], []
    length = rows
    for p, (_, n, _) in enumerate(phases):
        length //= n
        recvs.append(pltpu.VMEM((n, length, 128), jnp.float32))
        if p < len(phases) - 1:
            sums.append(pltpu.VMEM((length, 128), jnp.float32))
    semaphores = [pltpu.SemaphoreType.DMA((len(phases), widest)) for _ in range(4)]
    return pl.pallas_call(
        lambda *refs: gram_kernel(phases, *refs),
        out_shape=jax.ShapeDtypeStruct(values.shape, jnp.float32),
        in_specs=[pl.BlockSpec(memory_space=pltpu.VMEM)],
        out_specs=pl.BlockSpec(memory_space=pltpu.VMEM),
        scratch_shapes=recvs + sums + [pltpu.VMEM((rows, 128), jnp.float32)] + semaphores,
        compiler_params=pltpu.CompilerParams(collective_id=collective_id, has_side_effects=True),
    )(values)


def lower_solve(factor, values):
    return lax.linalg.triangular_solve(factor, values, left_side=True, lower=True)


def local(points, neighbors, omega, observed, prior_draws):
    blk_dev = neighbors.shape[0]
    cycle_count = lax.axis_size("blk")
    slab_blocks = blk_dev * lax.axis_size("leaf")
    period = 2.0 * cycle_count
    own_slab = lax.axis_index("blk")
    n_samp = lax.axis_size("samp")
    samp_idx = lax.axis_index("samp")
    usable = neighbors >= 0
    relative = jnp.mod(neighbors // slab_blocks - own_slab + 1, cycle_count)
    chosen = jnp.where(usable, relative * slab_blocks + jnp.mod(neighbors, slab_blocks), 0)
    usable_weight = usable.astype(jnp.float32)
    reach_points = beside_all(points)
    reach_blocks = reach_points.reshape(3, 3 * slab_blocks, PB).transpose(1, 0, 2)
    row_blocks = points.reshape(3, blk_dev, PB).transpose(1, 0, 2)

    kernel_tile = wendland(row_blocks[0], reach_blocks[chosen[0]], period)
    kernel_tile = kernel_tile * usable_weight[0][:, None, None]

    def apply_kernel(values):
        width = values.shape[0]
        reach = beside_all(values).reshape(width, 3 * slab_blocks, PB)
        picked = jnp.take(reach, chosen[0], axis=1)
        return jnp.einsum("cnj,nij->ci", picked, kernel_tile, precision=lax.Precision.HIGHEST)

    def slot(x):
        zeros = jnp.zeros((n_samp,) + x.shape, x.dtype)
        return lax.dynamic_update_index_in_dim(zeros, x, samp_idx, 0)

    def unslot(xs):
        return lax.dynamic_index_in_dim(xs, samp_idx, 0, keepdims=False)

    def total_per_samp(values):
        return jax.tree.map(unslot, lax.psum(jax.tree.map(slot, values), ALL_AXES))

    sketch = apply_kernel(omega) + sketch_shift * omega
    rhs = observed[None, :] - prior_draws
    half = PB // n_samp
    omega_half = lax.dynamic_slice_in_dim(omega, samp_idx * half, half, axis=1)
    sketch_half = lax.dynamic_slice_in_dim(sketch, samp_idx * half, half, axis=1)
    core_part = high_dot(omega_half, sketch_half.T)
    square_part = high_dot(sketch_half, sketch_half.T)
    joint_part = 0.5 * (core_part + core_part.T) + 0.5 * (square_part + square_part.T)
    gram_rows = joint_part.shape[0]
    joint_gram = gram_sum(joint_part.reshape(gram_rows * gram_rows // 128, 128), 2)
    joint_gram = joint_gram.reshape(gram_rows, gram_rows)
    width = rhs.shape[0]
    rhs_proj = high_dot(sketch, rhs.T).reshape(gram_rows * width // 128, 128)
    rhs_proj = group_sum(rhs_proj, 3).reshape(gram_rows, width)

    joint_factor = jnp.linalg.cholesky(joint_gram)

    def precond_from(vectors, projected):
        first_solve = lower_solve(joint_factor, projected)
        solved = lax.linalg.triangular_solve(
            joint_factor, first_solve, left_side=True, lower=True, transpose_a=True
        )
        return (vectors - high_dot(solved.T, sketch)) / noise_variance

    residual = rhs
    projected = rhs_proj
    precond = precond_from(residual, projected)
    direction = precond
    weights = jnp.zeros_like(rhs)

    sketch_rows = sketch.shape[0]

    def pack_scalars(*vectors):
        rows = jnp.stack(vectors)
        return jnp.pad(rows, ((0, 8 - rows.shape[0]), (0, 128 - width)))

    image = apply_kernel(direction) + noise_variance * direction
    image_proj = high_dot(sketch, image.T).reshape(sketch_rows * width // 128, 128)
    packed = jnp.concatenate(
        [
            image_proj,
            pack_scalars(
                jnp.sum(residual * precond, axis=1), jnp.sum(direction * image, axis=1)
            ),
        ]
    )
    packed = group_sum(packed, 0)
    image_proj = packed[:-8].reshape(sketch_rows, width)
    inner_now = packed[-8, :width]
    curvature = packed[-7, :width]
    step_size = inner_now / curvature
    weights = weights + step_size[:, None] * direction
    residual = residual - step_size[:, None] * image
    projected = projected - step_size[None, :] * image_proj
    precond = precond_from(residual, projected)
    inner_next = group_sum(pack_scalars(jnp.sum(residual * precond, axis=1)), 1)[0, :width]
    direction = precond + (inner_next / inner_now)[:, None] * direction
    inner_now = inner_next

    image = apply_kernel(direction) + noise_variance * direction
    curvature = group_sum(pack_scalars(jnp.sum(direction * image, axis=1)), 1)[0, :width]
    step_size = inner_now / curvature
    weights = weights + step_size[:, None] * direction
    residual = residual - step_size[:, None] * image
    return (weights, residual)


def solution(mesh):
    in_specs = (
        P(None, ("blk", "leaf")),
        P(("blk", "leaf"), None),
        P(None, ("blk", "leaf")),
        P(("blk", "leaf")),
        P("samp", ("blk", "leaf")),
    )
    out_specs = (P("samp", ("blk", "leaf")), P("samp", ("blk", "leaf")))
    return jax.shard_map(local, mesh=mesh, in_specs=in_specs, out_specs=out_specs, check_vma=False)
```

```python
import jax
import jax.numpy as jnp
from jax import lax
from jax.sharding import PartitionSpec as P
from jax.experimental import pallas as pl
from jax.experimental.pallas import tpu as pltpu

PB = 256
ITERS = 2


support_radius = 0.8
noise_variance = 1.0
sketch_shift = 1.0

ALL_AXES = ("blk", "leaf", "samp")


def shifted_2(block, axis, distance):
    devices = range(lax.axis_size(axis))
    route = [((i - distance) % len(devices), i) for i in devices]
    return lax.ppermute(block, axis, route)


def wendland(row_points, column_points, period):
    offset = row_points[None, :, :, None] - column_points[:, :, None, :]
    half_period = 0.5 * period
    along_x = jnp.mod(offset[:, 0] + half_period, period) - half_period
    squared = along_x * along_x + offset[:, 1] * offset[:, 1] + offset[:, 2] * offset[:, 2]
    radius = jnp.sqrt(squared) / support_radius
    remain = jnp.maximum(1.0 - radius, 0.0)
    return remain**4 * (4.0 * radius + 1.0)


def high_dot(left, right):
    return jnp.dot(left, right, precision=lax.Precision.HIGHEST, preferred_element_type=jnp.float32)


def shifted(values, offset_by):
    return shifted_2(values, "blk", offset_by)


def beside_all(values):
    slab_values = lax.all_gather(values, "leaf", axis=1, tiled=True)
    return jnp.concatenate([shifted(slab_values, 1), slab_values, shifted(slab_values, -1)], axis=1)


def blk_split(n_blk):
    if n_blk % 8 == 0 and n_blk > 8:
        return (8, n_blk // 8)
    return (n_blk, 1)


def reduce_phases():
    inner, outer = blk_split(lax.axis_size("blk"))
    phases = [("leaf", lax.axis_size("leaf"), 1), ("blk", inner, 1)]
    if outer > 1:
        phases.append(("blk", outer, inner))
    return tuple(p for p in phases if p[1] > 1)


def group_peer(axis, n, stride, k):
    idx = lax.axis_index(axis)
    own = (idx // stride) % n
    return own, idx + ((own + k) % n - own) * stride


def sum_kernel(phases, x_ref, o_ref, recv, send_sem, recv_sem):
    barrier = pltpu.get_barrier_semaphore()
    greeted = 0
    for axis, n, stride in phases:
        for k in range(1, n):
            _, peer = group_peer(axis, n, stride, k)
            pl.semaphore_signal(
                barrier, 1, device_id={axis: peer}, device_id_type=pl.DeviceIdType.MESH
            )
            greeted += 1
    pl.semaphore_wait(barrier, greeted)
    acc = x_ref[...]
    for p, (axis, n, stride) in enumerate(phases):
        recv[p, 0] = acc
        copies = []
        for k in range(1, n):
            own, peer = group_peer(axis, n, stride, k)
            copy = pltpu.make_async_remote_copy(
                src_ref=x_ref if p == 0 else recv.at[p, 0],
                dst_ref=recv.at[p, k],
                send_sem=send_sem.at[p, k],
                recv_sem=recv_sem.at[p, k],
                device_id={axis: peer},
                device_id_type=pl.DeviceIdType.MESH,
            )
            copy.start()
            copies.append(copy)
        for copy in copies:
            copy.wait()
        own, _ = group_peer(axis, n, stride, 0)
        terms = [recv[p, (own - j) % n] for j in range(n)]
        acc = terms[0]
        for term in terms[1:]:
            acc = acc + term
    o_ref[...] = acc


def group_sum(values, collective_id):
    phases = reduce_phases()
    rows = values.shape[0]
    widest = max(n for _, n, _ in phases)
    return pl.pallas_call(
        lambda *refs: sum_kernel(phases, *refs),
        out_shape=jax.ShapeDtypeStruct(values.shape, jnp.float32),
        in_specs=[pl.BlockSpec(memory_space=pltpu.VMEM)],
        out_specs=pl.BlockSpec(memory_space=pltpu.VMEM),
        scratch_shapes=[
            pltpu.VMEM((len(phases), widest, rows, 128), jnp.float32),
            pltpu.SemaphoreType.DMA((len(phases), widest)),
            pltpu.SemaphoreType.DMA((len(phases), widest)),
        ],
        compiler_params=pltpu.CompilerParams(collective_id=collective_id, has_side_effects=True),
    )(values)


def gram_kernel(phases, x_ref, o_ref, *scratch):
    count = len(phases)
    recvs = scratch[:count]
    sums = scratch[count : 2 * count - 1]
    full = scratch[2 * count - 1]
    rs_send, rs_recv, ag_send, ag_recv = scratch[2 * count :]
    barrier = pltpu.get_barrier_semaphore()
    greeted = 0
    for axis, n, stride in phases:
        for k in range(1, n):
            _, peer = group_peer(axis, n, stride, k)
            pl.semaphore_signal(
                barrier, 1, device_id={axis: peer}, device_id_type=pl.DeviceIdType.MESH
            )
            greeted += 1
    pl.semaphore_wait(barrier, greeted)
    source = x_ref
    length = x_ref.shape[0]
    offset = 0
    for p, (axis, n, stride) in enumerate(phases):
        own, _ = group_peer(axis, n, stride, 0)
        part = length // n
        recv = recvs[p]
        recv[0] = source[pl.ds(pl.multiple_of(own * part, 8), part)]
        copies = []
        for k in range(1, n):
            _, peer = group_peer(axis, n, stride, k)
            chunk = (own + k) % n
            copy = pltpu.make_async_remote_copy(
                src_ref=source.at[pl.ds(pl.multiple_of(chunk * part, 8), part)],
                dst_ref=recv.at[k],
                send_sem=rs_send.at[p, k],
                recv_sem=rs_recv.at[p, k],
                device_id={axis: peer},
                device_id_type=pl.DeviceIdType.MESH,
            )
            copy.start()
            copies.append(copy)
        for copy in copies:
            copy.wait()
        acc = recv[own % n]
        for j in range(1, n):
            acc = acc + recv[(own - j) % n]
        offset = offset + own * part
        length = part
        if p < count - 1:
            sums[p][...] = acc
            source = sums[p]
        else:
            full[pl.ds(pl.multiple_of(offset, 8), part)] = acc
    for p in reversed(range(count)):
        axis, n, stride = phases[p]
        own, _ = group_peer(axis, n, stride, 0)
        here = full.at[pl.ds(pl.multiple_of(offset, 8), length)]
        copies = []
        for k in range(1, n):
            _, peer = group_peer(axis, n, stride, k)
            copy = pltpu.make_async_remote_copy(
                src_ref=here,
                dst_ref=here,
                send_sem=ag_send.at[p, k],
                recv_sem=ag_recv.at[p, k],
                device_id={axis: peer},
                device_id_type=pl.DeviceIdType.MESH,
            )
            copy.start()
            copies.append(copy)
        for copy in copies:
            copy.wait()
        offset = offset - own * length
        length = length * n
    o_ref[...] = full[...]


def gram_sum(values, collective_id):
    phases = (("samp", lax.axis_size("samp"), 1),) + reduce_phases()
    phases = tuple(p for p in phases if p[1] > 1)
    rows = values.shape[0]
    widest = max(n for _, n, _ in phases)
    recvs, sums = [], []
    length = rows
    for p, (_, n, _) in enumerate(phases):
        length //= n
        recvs.append(pltpu.VMEM((n, length, 128), jnp.float32))
        if p < len(phases) - 1:
            sums.append(pltpu.VMEM((length, 128), jnp.float32))
    semaphores = [pltpu.SemaphoreType.DMA((len(phases), widest)) for _ in range(4)]
    return pl.pallas_call(
        lambda *refs: gram_kernel(phases, *refs),
        out_shape=jax.ShapeDtypeStruct(values.shape, jnp.float32),
        in_specs=[pl.BlockSpec(memory_space=pltpu.VMEM)],
        out_specs=pl.BlockSpec(memory_space=pltpu.VMEM),
        scratch_shapes=recvs + sums + [pltpu.VMEM((rows, 128), jnp.float32)] + semaphores,
        compiler_params=pltpu.CompilerParams(collective_id=collective_id, has_side_effects=True),
    )(values)


def halo_kernel(n_blk, n_leaf, x_ref, o_ref, land, send_sem, recv_sem):
    own_blk = lax.axis_index("blk")
    own_leaf = lax.axis_index("leaf")
    targets = []
    for d in (-1, 1):
        for leaf in range(n_leaf):
            targets.append(((own_blk + d + n_blk) % n_blk, leaf, (1 - d) * n_leaf + own_leaf))
    for k in range(1, n_leaf):
        targets.append((own_blk, (own_leaf + k) % n_leaf, n_leaf + own_leaf))
    barrier = pltpu.get_barrier_semaphore()
    for blk, leaf, _ in targets:
        pl.semaphore_signal(
            barrier,
            1,
            device_id={"blk": blk, "leaf": leaf},
            device_id_type=pl.DeviceIdType.MESH,
        )
    pl.semaphore_wait(barrier, len(targets))
    copies = []
    for i, (blk, leaf, segment) in enumerate(targets):
        copy = pltpu.make_async_remote_copy(
            src_ref=x_ref,
            dst_ref=land.at[segment],
            send_sem=send_sem.at[i],
            recv_sem=recv_sem.at[segment],
            device_id={"blk": blk, "leaf": leaf},
            device_id_type=pl.DeviceIdType.MESH,
        )
        copy.start()
        copies.append(copy)
    land[n_leaf + own_leaf] = x_ref[...]
    incoming = [((own_blk - 1 + n_blk) % n_blk, s, s) for s in range(n_leaf)]
    incoming += [((own_blk + 1) % n_blk, s, 2 * n_leaf + s) for s in range(n_leaf)]
    for k in range(1, n_leaf):
        leaf = (own_leaf + k) % n_leaf
        incoming.append((own_blk, leaf, n_leaf + leaf))
    for copy in copies:
        copy.wait_send()
    for blk, leaf, segment in incoming:
        pltpu.make_async_remote_copy(
            src_ref=x_ref,
            dst_ref=land.at[segment],
            send_sem=send_sem.at[0],
            recv_sem=recv_sem.at[segment],
            device_id={"blk": blk, "leaf": leaf},
            device_id_type=pl.DeviceIdType.MESH,
        ).wait_recv()
    o_ref[...] = land[...]


def halo_gather(values, collective_id):
    n_blk = lax.axis_size("blk")
    n_leaf = lax.axis_size("leaf")
    segments = 3 * n_leaf
    return pl.pallas_call(
        lambda *refs: halo_kernel(n_blk, n_leaf, *refs),
        out_shape=jax.ShapeDtypeStruct((segments,) + values.shape, jnp.float32),
        in_specs=[pl.BlockSpec(memory_space=pltpu.VMEM)],
        out_specs=pl.BlockSpec(memory_space=pltpu.VMEM),
        scratch_shapes=[
            pltpu.VMEM((segments,) + values.shape, jnp.float32),
            pltpu.SemaphoreType.DMA((segments,)),
            pltpu.SemaphoreType.DMA((segments,)),
        ],
        compiler_params=pltpu.CompilerParams(collective_id=collective_id, has_side_effects=True),
    )(values)


def lower_solve(factor, values):
    return lax.linalg.triangular_solve(factor, values, left_side=True, lower=True)


def local(points, neighbors, omega, observed, prior_draws):
    blk_dev = neighbors.shape[0]
    cycle_count = lax.axis_size("blk")
    slab_blocks = blk_dev * lax.axis_size("leaf")
    period = 2.0 * cycle_count
    own_slab = lax.axis_index("blk")
    n_samp = lax.axis_size("samp")
    samp_idx = lax.axis_index("samp")
    usable = neighbors >= 0
    relative = jnp.mod(neighbors // slab_blocks - own_slab + 1, cycle_count)
    chosen = jnp.where(usable, relative * slab_blocks + jnp.mod(neighbors, slab_blocks), 0)
    usable_weight = usable.astype(jnp.float32)
    reach_blocks = halo_gather(points, 4)
    row_blocks = points.reshape(3, blk_dev, PB).transpose(1, 0, 2)

    kernel_tile = wendland(row_blocks[0], reach_blocks[chosen[0]], period)
    kernel_tile = kernel_tile * usable_weight[0][:, None, None]

    def apply_kernel(values):
        width = values.shape[0]
        reach = halo_gather(values, 5 if width == omega.shape[0] else 6)
        picked = jnp.take(reach, chosen[0], axis=0)
        return jnp.einsum("ncj,nij->ci", picked, kernel_tile, precision=lax.Precision.HIGHEST)

    def slot(x):
        zeros = jnp.zeros((n_samp,) + x.shape, x.dtype)
        return lax.dynamic_update_index_in_dim(zeros, x, samp_idx, 0)

    def unslot(xs):
        return lax.dynamic_index_in_dim(xs, samp_idx, 0, keepdims=False)

    def total_per_samp(values):
        return jax.tree.map(unslot, lax.psum(jax.tree.map(slot, values), ALL_AXES))

    sketch = apply_kernel(omega) + sketch_shift * omega
    rhs = observed[None, :] - prior_draws
    half = PB // n_samp
    omega_half = lax.dynamic_slice_in_dim(omega, samp_idx * half, half, axis=1)
    sketch_half = lax.dynamic_slice_in_dim(sketch, samp_idx * half, half, axis=1)
    core_part = high_dot(omega_half, sketch_half.T)
    square_part = high_dot(sketch_half, sketch_half.T)
    joint_part = 0.5 * (core_part + core_part.T) + 0.5 * (square_part + square_part.T)
    gram_rows = joint_part.shape[0]
    joint_gram = gram_sum(joint_part.reshape(gram_rows * gram_rows // 128, 128), 2)
    joint_gram = joint_gram.reshape(gram_rows, gram_rows)
    width = rhs.shape[0]
    rhs_proj = high_dot(sketch, rhs.T).reshape(gram_rows * width // 128, 128)
    rhs_proj = group_sum(rhs_proj, 3).reshape(gram_rows, width)

    joint_factor = jnp.linalg.cholesky(joint_gram)

    def precond_from(vectors, projected):
        first_solve = lower_solve(joint_factor, projected)
        solved = lax.linalg.triangular_solve(
            joint_factor, first_solve, left_side=True, lower=True, transpose_a=True
        )
        return (vectors - high_dot(solved.T, sketch)) / noise_variance

    residual = rhs
    projected = rhs_proj
    precond = precond_from(residual, projected)
    direction = precond
    weights = jnp.zeros_like(rhs)

    sketch_rows = sketch.shape[0]

    def pack_scalars(*vectors):
        rows = jnp.stack(vectors)
        return jnp.pad(rows, ((0, 8 - rows.shape[0]), (0, 128 - width)))

    image = apply_kernel(direction) + noise_variance * direction
    image_proj = high_dot(sketch, image.T).reshape(sketch_rows * width // 128, 128)
    packed = jnp.concatenate(
        [
            image_proj,
            pack_scalars(
                jnp.sum(residual * precond, axis=1), jnp.sum(direction * image, axis=1)
            ),
        ]
    )
    packed = group_sum(packed, 0)
    image_proj = packed[:-8].reshape(sketch_rows, width)
    inner_now = packed[-8, :width]
    curvature = packed[-7, :width]
    step_size = inner_now / curvature
    weights = weights + step_size[:, None] * direction
    residual = residual - step_size[:, None] * image
    projected = projected - step_size[None, :] * image_proj
    precond = precond_from(residual, projected)
    inner_next = group_sum(pack_scalars(jnp.sum(residual * precond, axis=1)), 1)[0, :width]
    direction = precond + (inner_next / inner_now)[:, None] * direction
    inner_now = inner_next

    image = apply_kernel(direction) + noise_variance * direction
    curvature = group_sum(pack_scalars(jnp.sum(direction * image, axis=1)), 1)[0, :width]
    step_size = inner_now / curvature
    weights = weights + step_size[:, None] * direction
    residual = residual - step_size[:, None] * image
    return (weights, residual)


def solution(mesh):
    in_specs = (
        P(None, ("blk", "leaf")),
        P(("blk", "leaf"), None),
        P(None, ("blk", "leaf")),
        P(("blk", "leaf")),
        P("samp", ("blk", "leaf")),
    )
    out_specs = (P("samp", ("blk", "leaf")), P("samp", ("blk", "leaf")))
    return jax.shard_map(local, mesh=mesh, in_specs=in_specs, out_specs=out_specs, check_vma=False)
```

```python
import jax
import jax.numpy as jnp
from jax import lax
from jax.sharding import PartitionSpec as P
from jax.experimental import pallas as pl
from jax.experimental.pallas import tpu as pltpu

PB = 256
ITERS = 2


support_radius = 0.8
noise_variance = 1.0
sketch_shift = 1.0

ALL_AXES = ("blk", "leaf", "samp")


def shifted_2(block, axis, distance):
    devices = range(lax.axis_size(axis))
    route = [((i - distance) % len(devices), i) for i in devices]
    return lax.ppermute(block, axis, route)


def wendland(row_points, column_points, period):
    offset = row_points[None, :, :, None] - column_points[:, :, None, :]
    half_period = 0.5 * period
    along_x = jnp.mod(offset[:, 0] + half_period, period) - half_period
    squared = along_x * along_x + offset[:, 1] * offset[:, 1] + offset[:, 2] * offset[:, 2]
    radius = jnp.sqrt(squared) / support_radius
    remain = jnp.maximum(1.0 - radius, 0.0)
    return remain**4 * (4.0 * radius + 1.0)


def high_dot(left, right):
    return jnp.dot(left, right, precision=lax.Precision.HIGHEST, preferred_element_type=jnp.float32)


def shifted(values, offset_by):
    return shifted_2(values, "blk", offset_by)


def beside_all(values):
    slab_values = lax.all_gather(values, "leaf", axis=1, tiled=True)
    return jnp.concatenate([shifted(slab_values, 1), slab_values, shifted(slab_values, -1)], axis=1)


def blk_split(n_blk):
    if n_blk % 8 == 0 and n_blk > 8:
        return (8, n_blk // 8)
    return (n_blk, 1)


def reduce_phases():
    inner, outer = blk_split(lax.axis_size("blk"))
    phases = [("leaf", lax.axis_size("leaf"), 1), ("blk", inner, 1)]
    if outer > 1:
        phases.append(("blk", outer, inner))
    return tuple(p for p in phases if p[1] > 1)


def group_peer(axis, n, stride, k):
    idx = lax.axis_index(axis)
    own = (idx // stride) % n
    return own, idx + ((own + k) % n - own) * stride


def sum_kernel(phases, x_ref, o_ref, recv, send_sem, recv_sem):
    barrier = pltpu.get_barrier_semaphore()
    greeted = 0
    for axis, n, stride in phases:
        for k in range(1, n):
            _, peer = group_peer(axis, n, stride, k)
            pl.semaphore_signal(
                barrier, 1, device_id={axis: peer}, device_id_type=pl.DeviceIdType.MESH
            )
            greeted += 1
    pl.semaphore_wait(barrier, greeted)
    acc = x_ref[...]
    for p, (axis, n, stride) in enumerate(phases):
        recv[p, 0] = acc
        copies = []
        for k in range(1, n):
            own, peer = group_peer(axis, n, stride, k)
            copy = pltpu.make_async_remote_copy(
                src_ref=x_ref if p == 0 else recv.at[p, 0],
                dst_ref=recv.at[p, k],
                send_sem=send_sem.at[p, k],
                recv_sem=recv_sem.at[p, k],
                device_id={axis: peer},
                device_id_type=pl.DeviceIdType.MESH,
            )
            copy.start()
            copies.append(copy)
        for copy in copies:
            copy.wait()
        own, _ = group_peer(axis, n, stride, 0)
        terms = [recv[p, (own - j) % n] for j in range(n)]
        acc = terms[0]
        for term in terms[1:]:
            acc = acc + term
    o_ref[...] = acc


def group_sum(values, collective_id):
    phases = reduce_phases()
    rows = values.shape[0]
    widest = max(n for _, n, _ in phases)
    return pl.pallas_call(
        lambda *refs: sum_kernel(phases, *refs),
        out_shape=jax.ShapeDtypeStruct(values.shape, jnp.float32),
        in_specs=[pl.BlockSpec(memory_space=pltpu.VMEM)],
        out_specs=pl.BlockSpec(memory_space=pltpu.VMEM),
        scratch_shapes=[
            pltpu.VMEM((len(phases), widest, rows, 128), jnp.float32),
            pltpu.SemaphoreType.DMA((len(phases), widest)),
            pltpu.SemaphoreType.DMA((len(phases), widest)),
        ],
        compiler_params=pltpu.CompilerParams(collective_id=collective_id, has_side_effects=True),
    )(values)


def gram_kernel(phases, x_ref, o_ref, *scratch):
    count = len(phases)
    recvs = scratch[:count]
    sums = scratch[count : 2 * count - 1]
    full = scratch[2 * count - 1]
    rs_send, rs_recv, ag_send, ag_recv = scratch[2 * count :]
    barrier = pltpu.get_barrier_semaphore()
    greeted = 0
    for axis, n, stride in phases:
        for k in range(1, n):
            _, peer = group_peer(axis, n, stride, k)
            pl.semaphore_signal(
                barrier, 1, device_id={axis: peer}, device_id_type=pl.DeviceIdType.MESH
            )
            greeted += 1
    pl.semaphore_wait(barrier, greeted)
    source = x_ref
    length = x_ref.shape[0]
    offset = 0
    for p, (axis, n, stride) in enumerate(phases):
        own, _ = group_peer(axis, n, stride, 0)
        part = length // n
        recv = recvs[p]
        recv[0] = source[pl.ds(pl.multiple_of(own * part, 8), part)]
        copies = []
        for k in range(1, n):
            _, peer = group_peer(axis, n, stride, k)
            chunk = (own + k) % n
            copy = pltpu.make_async_remote_copy(
                src_ref=source.at[pl.ds(pl.multiple_of(chunk * part, 8), part)],
                dst_ref=recv.at[k],
                send_sem=rs_send.at[p, k],
                recv_sem=rs_recv.at[p, k],
                device_id={axis: peer},
                device_id_type=pl.DeviceIdType.MESH,
            )
            copy.start()
            copies.append(copy)
        for copy in copies:
            copy.wait()
        acc = recv[own % n]
        for j in range(1, n):
            acc = acc + recv[(own - j) % n]
        offset = offset + own * part
        length = part
        if p < count - 1:
            sums[p][...] = acc
            source = sums[p]
        else:
            full[pl.ds(pl.multiple_of(offset, 8), part)] = acc
    for p in reversed(range(count)):
        axis, n, stride = phases[p]
        own, _ = group_peer(axis, n, stride, 0)
        here = full.at[pl.ds(pl.multiple_of(offset, 8), length)]
        copies = []
        for k in range(1, n):
            _, peer = group_peer(axis, n, stride, k)
            copy = pltpu.make_async_remote_copy(
                src_ref=here,
                dst_ref=here,
                send_sem=ag_send.at[p, k],
                recv_sem=ag_recv.at[p, k],
                device_id={axis: peer},
                device_id_type=pl.DeviceIdType.MESH,
            )
            copy.start()
            copies.append(copy)
        for copy in copies:
            copy.wait()
        offset = offset - own * length
        length = length * n
    o_ref[...] = full[...]


def gram_sum(values, collective_id):
    phases = (("samp", lax.axis_size("samp"), 1),) + reduce_phases()
    phases = tuple(p for p in phases if p[1] > 1)
    rows = values.shape[0]
    widest = max(n for _, n, _ in phases)
    recvs, sums = [], []
    length = rows
    for p, (_, n, _) in enumerate(phases):
        length //= n
        recvs.append(pltpu.VMEM((n, length, 128), jnp.float32))
        if p < len(phases) - 1:
            sums.append(pltpu.VMEM((length, 128), jnp.float32))
    semaphores = [pltpu.SemaphoreType.DMA((len(phases), widest)) for _ in range(4)]
    return pl.pallas_call(
        lambda *refs: gram_kernel(phases, *refs),
        out_shape=jax.ShapeDtypeStruct(values.shape, jnp.float32),
        in_specs=[pl.BlockSpec(memory_space=pltpu.VMEM)],
        out_specs=pl.BlockSpec(memory_space=pltpu.VMEM),
        scratch_shapes=recvs + sums + [pltpu.VMEM((rows, 128), jnp.float32)] + semaphores,
        compiler_params=pltpu.CompilerParams(collective_id=collective_id, has_side_effects=True),
    )(values)


def halo_kernel(n_blk, n_leaf, x_ref, o_ref, land, send_sem, recv_sem):
    own_blk = lax.axis_index("blk")
    own_leaf = lax.axis_index("leaf")
    targets = []
    for d in (-1, 1):
        for leaf in range(n_leaf):
            targets.append(((own_blk + d + n_blk) % n_blk, leaf, (1 - d) * n_leaf + own_leaf))
    for k in range(1, n_leaf):
        targets.append((own_blk, (own_leaf + k) % n_leaf, n_leaf + own_leaf))
    barrier = pltpu.get_barrier_semaphore()
    for blk, leaf, _ in targets:
        pl.semaphore_signal(
            barrier,
            1,
            device_id={"blk": blk, "leaf": leaf},
            device_id_type=pl.DeviceIdType.MESH,
        )
    pl.semaphore_wait(barrier, len(targets))
    copies = []
    for i, (blk, leaf, segment) in enumerate(targets):
        copy = pltpu.make_async_remote_copy(
            src_ref=x_ref,
            dst_ref=land.at[segment],
            send_sem=send_sem.at[i],
            recv_sem=recv_sem.at[segment],
            device_id={"blk": blk, "leaf": leaf},
            device_id_type=pl.DeviceIdType.MESH,
        )
        copy.start()
        copies.append(copy)
    land[n_leaf + own_leaf] = x_ref[...]
    incoming = [((own_blk - 1 + n_blk) % n_blk, s, s) for s in range(n_leaf)]
    incoming += [((own_blk + 1) % n_blk, s, 2 * n_leaf + s) for s in range(n_leaf)]
    for k in range(1, n_leaf):
        leaf = (own_leaf + k) % n_leaf
        incoming.append((own_blk, leaf, n_leaf + leaf))
    for copy in copies:
        copy.wait_send()
    for blk, leaf, segment in incoming:
        pltpu.make_async_remote_copy(
            src_ref=x_ref,
            dst_ref=land.at[segment],
            send_sem=send_sem.at[0],
            recv_sem=recv_sem.at[segment],
            device_id={"blk": blk, "leaf": leaf},
            device_id_type=pl.DeviceIdType.MESH,
        ).wait_recv()
    o_ref[...] = land[...]


def halo_gather(values, collective_id):
    n_blk = lax.axis_size("blk")
    n_leaf = lax.axis_size("leaf")
    segments = 3 * n_leaf
    return pl.pallas_call(
        lambda *refs: halo_kernel(n_blk, n_leaf, *refs),
        out_shape=jax.ShapeDtypeStruct((segments,) + values.shape, jnp.float32),
        in_specs=[pl.BlockSpec(memory_space=pltpu.VMEM)],
        out_specs=pl.BlockSpec(memory_space=pltpu.VMEM),
        scratch_shapes=[
            pltpu.VMEM((segments,) + values.shape, jnp.float32),
            pltpu.SemaphoreType.DMA((segments,)),
            pltpu.SemaphoreType.DMA((segments,)),
        ],
        compiler_params=pltpu.CompilerParams(collective_id=collective_id, has_side_effects=True),
    )(values)


def lower_solve(factor, values):
    return lax.linalg.triangular_solve(factor, values, left_side=True, lower=True)


def local(points, neighbors, omega, observed, prior_draws):
    blk_dev = neighbors.shape[0]
    cycle_count = lax.axis_size("blk")
    slab_blocks = blk_dev * lax.axis_size("leaf")
    period = 2.0 * cycle_count
    own_slab = lax.axis_index("blk")
    n_samp = lax.axis_size("samp")
    samp_idx = lax.axis_index("samp")
    usable = neighbors >= 0
    relative = jnp.mod(neighbors // slab_blocks - own_slab + 1, cycle_count)
    chosen = jnp.where(usable, relative * slab_blocks + jnp.mod(neighbors, slab_blocks), 0)
    usable_weight = usable.astype(jnp.float32)
    reach_blocks = halo_gather(points, 4)
    row_blocks = points.reshape(3, blk_dev, PB).transpose(1, 0, 2)

    kernel_tile = wendland(row_blocks[0], reach_blocks[chosen[0]], period)
    kernel_tile = kernel_tile * usable_weight[0][:, None, None]

    def apply_kernel(values):
        width = values.shape[0]
        if width == omega.shape[0]:
            reach = beside_all(values).reshape(width, 3 * slab_blocks, PB)
            picked = jnp.take(reach, chosen[0], axis=1)
            return jnp.einsum("cnj,nij->ci", picked, kernel_tile, precision=lax.Precision.HIGHEST)
        reach = halo_gather(values, 6)
        picked = jnp.take(reach, chosen[0], axis=0)
        return jnp.einsum("ncj,nij->ci", picked, kernel_tile, precision=lax.Precision.HIGHEST)

    def slot(x):
        zeros = jnp.zeros((n_samp,) + x.shape, x.dtype)
        return lax.dynamic_update_index_in_dim(zeros, x, samp_idx, 0)

    def unslot(xs):
        return lax.dynamic_index_in_dim(xs, samp_idx, 0, keepdims=False)

    def total_per_samp(values):
        return jax.tree.map(unslot, lax.psum(jax.tree.map(slot, values), ALL_AXES))

    sketch = apply_kernel(omega) + sketch_shift * omega
    rhs = observed[None, :] - prior_draws
    half = PB // n_samp
    omega_half = lax.dynamic_slice_in_dim(omega, samp_idx * half, half, axis=1)
    sketch_half = lax.dynamic_slice_in_dim(sketch, samp_idx * half, half, axis=1)
    core_part = high_dot(omega_half, sketch_half.T)
    square_part = high_dot(sketch_half, sketch_half.T)
    joint_part = 0.5 * (core_part + core_part.T) + 0.5 * (square_part + square_part.T)
    gram_rows = joint_part.shape[0]
    joint_gram = gram_sum(joint_part.reshape(gram_rows * gram_rows // 128, 128), 2)
    joint_gram = joint_gram.reshape(gram_rows, gram_rows)
    width = rhs.shape[0]
    rhs_proj = high_dot(sketch, rhs.T).reshape(gram_rows * width // 128, 128)
    rhs_proj = group_sum(rhs_proj, 3).reshape(gram_rows, width)

    joint_factor = jnp.linalg.cholesky(joint_gram)

    def precond_from(vectors, projected):
        first_solve = lower_solve(joint_factor, projected)
        solved = lax.linalg.triangular_solve(
            joint_factor, first_solve, left_side=True, lower=True, transpose_a=True
        )
        return (vectors - high_dot(solved.T, sketch)) / noise_variance

    residual = rhs
    projected = rhs_proj
    precond = precond_from(residual, projected)
    direction = precond
    weights = jnp.zeros_like(rhs)

    sketch_rows = sketch.shape[0]

    def pack_scalars(*vectors):
        rows = jnp.stack(vectors)
        return jnp.pad(rows, ((0, 8 - rows.shape[0]), (0, 128 - width)))

    image = apply_kernel(direction) + noise_variance * direction
    image_proj = high_dot(sketch, image.T).reshape(sketch_rows * width // 128, 128)
    packed = jnp.concatenate(
        [
            image_proj,
            pack_scalars(
                jnp.sum(residual * precond, axis=1), jnp.sum(direction * image, axis=1)
            ),
        ]
    )
    packed = group_sum(packed, 0)
    image_proj = packed[:-8].reshape(sketch_rows, width)
    inner_now = packed[-8, :width]
    curvature = packed[-7, :width]
    step_size = inner_now / curvature
    weights = weights + step_size[:, None] * direction
    residual = residual - step_size[:, None] * image
    projected = projected - step_size[None, :] * image_proj
    precond = precond_from(residual, projected)
    inner_next = group_sum(pack_scalars(jnp.sum(residual * precond, axis=1)), 1)[0, :width]
    direction = precond + (inner_next / inner_now)[:, None] * direction
    inner_now = inner_next

    image = apply_kernel(direction) + noise_variance * direction
    curvature = group_sum(pack_scalars(jnp.sum(direction * image, axis=1)), 1)[0, :width]
    step_size = inner_now / curvature
    weights = weights + step_size[:, None] * direction
    residual = residual - step_size[:, None] * image
    return (weights, residual)


def solution(mesh):
    in_specs = (
        P(None, ("blk", "leaf")),
        P(("blk", "leaf"), None),
        P(None, ("blk", "leaf")),
        P(("blk", "leaf")),
        P("samp", ("blk", "leaf")),
    )
    out_specs = (P("samp", ("blk", "leaf")), P("samp", ("blk", "leaf")))
    return jax.shard_map(local, mesh=mesh, in_specs=in_specs, out_specs=out_specs, check_vma=False)
```

```python
import jax
import jax.numpy as jnp
from jax import lax
from jax.sharding import PartitionSpec as P
from jax.experimental import pallas as pl
from jax.experimental.pallas import tpu as pltpu

PB = 256
ITERS = 2


support_radius = 0.8
noise_variance = 1.0
sketch_shift = 1.0

ALL_AXES = ("blk", "leaf", "samp")


def shifted_2(block, axis, distance):
    devices = range(lax.axis_size(axis))
    route = [((i - distance) % len(devices), i) for i in devices]
    return lax.ppermute(block, axis, route)


def wendland(row_points, column_points, period):
    offset = row_points[None, :, :, None] - column_points[:, :, None, :]
    half_period = 0.5 * period
    along_x = jnp.mod(offset[:, 0] + half_period, period) - half_period
    squared = along_x * along_x + offset[:, 1] * offset[:, 1] + offset[:, 2] * offset[:, 2]
    radius = jnp.sqrt(squared) / support_radius
    remain = jnp.maximum(1.0 - radius, 0.0)
    return remain**4 * (4.0 * radius + 1.0)


def high_dot(left, right):
    return jnp.dot(left, right, precision=lax.Precision.HIGHEST, preferred_element_type=jnp.float32)


def shifted(values, offset_by):
    return shifted_2(values, "blk", offset_by)


def beside_all(values):
    slab_values = lax.all_gather(values, "leaf", axis=1, tiled=True)
    return jnp.concatenate([shifted(slab_values, 1), slab_values, shifted(slab_values, -1)], axis=1)


def blk_split(n_blk):
    if n_blk % 8 == 0 and n_blk > 8:
        return (8, n_blk // 8)
    return (n_blk, 1)


def reduce_phases():
    inner, outer = blk_split(lax.axis_size("blk"))
    phases = [("leaf", lax.axis_size("leaf"), 1), ("blk", inner, 1)]
    if outer > 1:
        phases.append(("blk", outer, inner))
    return tuple(p for p in phases if p[1] > 1)


def group_peer(axis, n, stride, k):
    idx = lax.axis_index(axis)
    own = (idx // stride) % n
    return own, idx + ((own + k) % n - own) * stride


def sum_kernel(phases, x_ref, o_ref, recv, send_sem, recv_sem):
    barrier = pltpu.get_barrier_semaphore()
    greeted = 0
    for axis, n, stride in phases:
        for k in range(1, n):
            _, peer = group_peer(axis, n, stride, k)
            pl.semaphore_signal(
                barrier, 1, device_id={axis: peer}, device_id_type=pl.DeviceIdType.MESH
            )
            greeted += 1
    pl.semaphore_wait(barrier, greeted)
    acc = x_ref[...]
    for p, (axis, n, stride) in enumerate(phases):
        recv[p, 0] = acc
        copies = []
        for k in range(1, n):
            own, peer = group_peer(axis, n, stride, k)
            copy = pltpu.make_async_remote_copy(
                src_ref=x_ref if p == 0 else recv.at[p, 0],
                dst_ref=recv.at[p, k],
                send_sem=send_sem.at[p, k],
                recv_sem=recv_sem.at[p, k],
                device_id={axis: peer},
                device_id_type=pl.DeviceIdType.MESH,
            )
            copy.start()
            copies.append(copy)
        for copy in copies:
            copy.wait()
        own, _ = group_peer(axis, n, stride, 0)
        terms = [recv[p, (own - j) % n] for j in range(n)]
        acc = terms[0]
        for term in terms[1:]:
            acc = acc + term
    o_ref[...] = acc


def group_sum(values, collective_id):
    phases = reduce_phases()
    rows = values.shape[0]
    widest = max(n for _, n, _ in phases)
    return pl.pallas_call(
        lambda *refs: sum_kernel(phases, *refs),
        out_shape=jax.ShapeDtypeStruct(values.shape, jnp.float32),
        in_specs=[pl.BlockSpec(memory_space=pltpu.VMEM)],
        out_specs=pl.BlockSpec(memory_space=pltpu.VMEM),
        scratch_shapes=[
            pltpu.VMEM((len(phases), widest, rows, 128), jnp.float32),
            pltpu.SemaphoreType.DMA((len(phases), widest)),
            pltpu.SemaphoreType.DMA((len(phases), widest)),
        ],
        compiler_params=pltpu.CompilerParams(collective_id=collective_id, has_side_effects=True),
    )(values)


def gram_kernel(phases, x_ref, o_ref, *scratch):
    count = len(phases)
    recvs = scratch[:count]
    sums = scratch[count : 2 * count - 1]
    full = scratch[2 * count - 1]
    rs_send, rs_recv, ag_send, ag_recv = scratch[2 * count :]
    barrier = pltpu.get_barrier_semaphore()
    greeted = 0
    for axis, n, stride in phases:
        for k in range(1, n):
            _, peer = group_peer(axis, n, stride, k)
            pl.semaphore_signal(
                barrier, 1, device_id={axis: peer}, device_id_type=pl.DeviceIdType.MESH
            )
            greeted += 1
    pl.semaphore_wait(barrier, greeted)
    source = x_ref
    length = x_ref.shape[0]
    offset = 0
    for p, (axis, n, stride) in enumerate(phases):
        own, _ = group_peer(axis, n, stride, 0)
        part = length // n
        recv = recvs[p]
        recv[0] = source[pl.ds(pl.multiple_of(own * part, 8), part)]
        copies = []
        for k in range(1, n):
            _, peer = group_peer(axis, n, stride, k)
            chunk = (own + k) % n
            copy = pltpu.make_async_remote_copy(
                src_ref=source.at[pl.ds(pl.multiple_of(chunk * part, 8), part)],
                dst_ref=recv.at[k],
                send_sem=rs_send.at[p, k],
                recv_sem=rs_recv.at[p, k],
                device_id={axis: peer},
                device_id_type=pl.DeviceIdType.MESH,
            )
            copy.start()
            copies.append(copy)
        for copy in copies:
            copy.wait()
        acc = recv[own % n]
        for j in range(1, n):
            acc = acc + recv[(own - j) % n]
        offset = offset + own * part
        length = part
        if p < count - 1:
            sums[p][...] = acc
            source = sums[p]
        else:
            full[pl.ds(pl.multiple_of(offset, 8), part)] = acc
    for p in reversed(range(count)):
        axis, n, stride = phases[p]
        own, _ = group_peer(axis, n, stride, 0)
        here = full.at[pl.ds(pl.multiple_of(offset, 8), length)]
        copies = []
        for k in range(1, n):
            _, peer = group_peer(axis, n, stride, k)
            copy = pltpu.make_async_remote_copy(
                src_ref=here,
                dst_ref=here,
                send_sem=ag_send.at[p, k],
                recv_sem=ag_recv.at[p, k],
                device_id={axis: peer},
                device_id_type=pl.DeviceIdType.MESH,
            )
            copy.start()
            copies.append(copy)
        for copy in copies:
            copy.wait()
        offset = offset - own * length
        length = length * n
    o_ref[...] = full[...]


def gram_sum(values, collective_id):
    phases = (("samp", lax.axis_size("samp"), 1),) + reduce_phases()
    phases = tuple(p for p in phases if p[1] > 1)
    rows = values.shape[0]
    widest = max(n for _, n, _ in phases)
    recvs, sums = [], []
    length = rows
    for p, (_, n, _) in enumerate(phases):
        length //= n
        recvs.append(pltpu.VMEM((n, length, 128), jnp.float32))
        if p < len(phases) - 1:
            sums.append(pltpu.VMEM((length, 128), jnp.float32))
    semaphores = [pltpu.SemaphoreType.DMA((len(phases), widest)) for _ in range(4)]
    return pl.pallas_call(
        lambda *refs: gram_kernel(phases, *refs),
        out_shape=jax.ShapeDtypeStruct(values.shape, jnp.float32),
        in_specs=[pl.BlockSpec(memory_space=pltpu.VMEM)],
        out_specs=pl.BlockSpec(memory_space=pltpu.VMEM),
        scratch_shapes=recvs + sums + [pltpu.VMEM((rows, 128), jnp.float32)] + semaphores,
        compiler_params=pltpu.CompilerParams(collective_id=collective_id, has_side_effects=True),
    )(values)


def halo_kernel(n_blk, n_leaf, x_ref, o_ref, land, send_sem, recv_sem):
    own_blk = lax.axis_index("blk")
    own_leaf = lax.axis_index("leaf")
    targets = []
    for d in (-1, 1):
        for leaf in range(n_leaf):
            targets.append(((own_blk + d + n_blk) % n_blk, leaf, (1 - d) * n_leaf + own_leaf))
    for k in range(1, n_leaf):
        targets.append((own_blk, (own_leaf + k) % n_leaf, n_leaf + own_leaf))
    barrier = pltpu.get_barrier_semaphore()
    for blk, leaf, _ in targets:
        pl.semaphore_signal(
            barrier,
            1,
            device_id={"blk": blk, "leaf": leaf},
            device_id_type=pl.DeviceIdType.MESH,
        )
    pl.semaphore_wait(barrier, len(targets))
    copies = []
    for i, (blk, leaf, segment) in enumerate(targets):
        copy = pltpu.make_async_remote_copy(
            src_ref=x_ref,
            dst_ref=land.at[segment],
            send_sem=send_sem.at[i],
            recv_sem=recv_sem.at[segment],
            device_id={"blk": blk, "leaf": leaf},
            device_id_type=pl.DeviceIdType.MESH,
        )
        copy.start()
        copies.append(copy)
    land[n_leaf + own_leaf] = x_ref[...]
    incoming = [((own_blk - 1 + n_blk) % n_blk, s, s) for s in range(n_leaf)]
    incoming += [((own_blk + 1) % n_blk, s, 2 * n_leaf + s) for s in range(n_leaf)]
    for k in range(1, n_leaf):
        leaf = (own_leaf + k) % n_leaf
        incoming.append((own_blk, leaf, n_leaf + leaf))
    for copy in copies:
        copy.wait_send()
    for blk, leaf, segment in incoming:
        pltpu.make_async_remote_copy(
            src_ref=x_ref,
            dst_ref=land.at[segment],
            send_sem=send_sem.at[0],
            recv_sem=recv_sem.at[segment],
            device_id={"blk": blk, "leaf": leaf},
            device_id_type=pl.DeviceIdType.MESH,
        ).wait_recv()
    o_ref[...] = land[...]


def halo_gather(values, collective_id):
    n_blk = lax.axis_size("blk")
    n_leaf = lax.axis_size("leaf")
    segments = 3 * n_leaf
    return pl.pallas_call(
        lambda *refs: halo_kernel(n_blk, n_leaf, *refs),
        out_shape=jax.ShapeDtypeStruct((segments,) + values.shape, jnp.float32),
        in_specs=[pl.BlockSpec(memory_space=pltpu.VMEM)],
        out_specs=pl.BlockSpec(memory_space=pltpu.VMEM),
        scratch_shapes=[
            pltpu.VMEM((segments,) + values.shape, jnp.float32),
            pltpu.SemaphoreType.DMA((segments,)),
            pltpu.SemaphoreType.DMA((segments,)),
        ],
        compiler_params=pltpu.CompilerParams(collective_id=collective_id, has_side_effects=True),
    )(values)


def lower_solve(factor, values):
    return lax.linalg.triangular_solve(factor, values, left_side=True, lower=True)


def local(points, neighbors, omega, observed, prior_draws):
    blk_dev = neighbors.shape[0]
    cycle_count = lax.axis_size("blk")
    slab_blocks = blk_dev * lax.axis_size("leaf")
    period = 2.0 * cycle_count
    own_slab = lax.axis_index("blk")
    n_samp = lax.axis_size("samp")
    samp_idx = lax.axis_index("samp")
    usable = neighbors >= 0
    relative = jnp.mod(neighbors // slab_blocks - own_slab + 1, cycle_count)
    chosen = jnp.where(usable, relative * slab_blocks + jnp.mod(neighbors, slab_blocks), 0)
    usable_weight = usable.astype(jnp.float32)
    reach_blocks = halo_gather(points, 4)
    row_blocks = points.reshape(3, blk_dev, PB).transpose(1, 0, 2)

    segments = 3 * slab_blocks
    listed = jnp.zeros((segments,), jnp.float32).at[chosen[0]].max(usable_weight[0])
    kernel_tile = wendland(row_blocks[0], reach_blocks, period) * listed[:, None, None]

    def apply_kernel(values):
        width = values.shape[0]
        if width == omega.shape[0]:
            slab_values = lax.all_gather(values, "leaf", axis=1, tiled=True)
            parts = (shifted(slab_values, 1), slab_values, shifted(slab_values, -1))
            out = None
            for i, part in enumerate(parts):
                tile = kernel_tile[i * slab_blocks : (i + 1) * slab_blocks]
                term = jnp.einsum(
                    "cnj,nij->ci",
                    part.reshape(width, slab_blocks, PB),
                    tile,
                    precision=lax.Precision.HIGHEST,
                )
                out = term if out is None else out + term
            return out
        reach = halo_gather(values, 6)
        return jnp.einsum("ncj,nij->ci", reach, kernel_tile, precision=lax.Precision.HIGHEST)

    def slot(x):
        zeros = jnp.zeros((n_samp,) + x.shape, x.dtype)
        return lax.dynamic_update_index_in_dim(zeros, x, samp_idx, 0)

    def unslot(xs):
        return lax.dynamic_index_in_dim(xs, samp_idx, 0, keepdims=False)

    def total_per_samp(values):
        return jax.tree.map(unslot, lax.psum(jax.tree.map(slot, values), ALL_AXES))

    sketch = apply_kernel(omega) + sketch_shift * omega
    rhs = observed[None, :] - prior_draws
    half = PB // n_samp
    omega_half = lax.dynamic_slice_in_dim(omega, samp_idx * half, half, axis=1)
    sketch_half = lax.dynamic_slice_in_dim(sketch, samp_idx * half, half, axis=1)
    core_part = high_dot(omega_half, sketch_half.T)
    square_part = high_dot(sketch_half, sketch_half.T)
    joint_part = 0.5 * (core_part + core_part.T) + 0.5 * (square_part + square_part.T)
    gram_rows = joint_part.shape[0]
    joint_gram = gram_sum(joint_part.reshape(gram_rows * gram_rows // 128, 128), 2)
    joint_gram = joint_gram.reshape(gram_rows, gram_rows)
    width = rhs.shape[0]
    rhs_proj = high_dot(sketch, rhs.T).reshape(gram_rows * width // 128, 128)
    rhs_proj = group_sum(rhs_proj, 3).reshape(gram_rows, width)

    joint_factor = jnp.linalg.cholesky(joint_gram)

    def precond_from(vectors, projected):
        first_solve = lower_solve(joint_factor, projected)
        solved = lax.linalg.triangular_solve(
            joint_factor, first_solve, left_side=True, lower=True, transpose_a=True
        )
        return (vectors - high_dot(solved.T, sketch)) / noise_variance

    residual = rhs
    projected = rhs_proj
    precond = precond_from(residual, projected)
    direction = precond
    weights = jnp.zeros_like(rhs)

    sketch_rows = sketch.shape[0]

    def pack_scalars(*vectors):
        rows = jnp.stack(vectors)
        return jnp.pad(rows, ((0, 8 - rows.shape[0]), (0, 128 - width)))

    image = apply_kernel(direction) + noise_variance * direction
    image_proj = high_dot(sketch, image.T).reshape(sketch_rows * width // 128, 128)
    packed = jnp.concatenate(
        [
            image_proj,
            pack_scalars(
                jnp.sum(residual * precond, axis=1), jnp.sum(direction * image, axis=1)
            ),
        ]
    )
    packed = group_sum(packed, 0)
    image_proj = packed[:-8].reshape(sketch_rows, width)
    inner_now = packed[-8, :width]
    curvature = packed[-7, :width]
    step_size = inner_now / curvature
    weights = weights + step_size[:, None] * direction
    residual = residual - step_size[:, None] * image
    projected = projected - step_size[None, :] * image_proj
    precond = precond_from(residual, projected)
    inner_next = group_sum(pack_scalars(jnp.sum(residual * precond, axis=1)), 1)[0, :width]
    direction = precond + (inner_next / inner_now)[:, None] * direction
    inner_now = inner_next

    image = apply_kernel(direction) + noise_variance * direction
    curvature = group_sum(pack_scalars(jnp.sum(direction * image, axis=1)), 1)[0, :width]
    step_size = inner_now / curvature
    weights = weights + step_size[:, None] * direction
    residual = residual - step_size[:, None] * image
    return (weights, residual)


def solution(mesh):
    in_specs = (
        P(None, ("blk", "leaf")),
        P(("blk", "leaf"), None),
        P(None, ("blk", "leaf")),
        P(("blk", "leaf")),
        P("samp", ("blk", "leaf")),
    )
    out_specs = (P("samp", ("blk", "leaf")), P("samp", ("blk", "leaf")))
    return jax.shard_map(local, mesh=mesh, in_specs=in_specs, out_specs=out_specs, check_vma=False)
```

```python
import jax
import jax.numpy as jnp
from jax import lax
from jax.sharding import PartitionSpec as P
from jax.experimental import pallas as pl
from jax.experimental.pallas import tpu as pltpu

PB = 256
ITERS = 2


support_radius = 0.8
noise_variance = 1.0
sketch_shift = 1.0

ALL_AXES = ("blk", "leaf", "samp")


def shifted_2(block, axis, distance):
    devices = range(lax.axis_size(axis))
    route = [((i - distance) % len(devices), i) for i in devices]
    return lax.ppermute(block, axis, route)


def wendland(row_points, column_points, period):
    offset = row_points[None, :, :, None] - column_points[:, :, None, :]
    half_period = 0.5 * period
    along_x = jnp.mod(offset[:, 0] + half_period, period) - half_period
    squared = along_x * along_x + offset[:, 1] * offset[:, 1] + offset[:, 2] * offset[:, 2]
    radius = jnp.sqrt(squared) / support_radius
    remain = jnp.maximum(1.0 - radius, 0.0)
    return remain**4 * (4.0 * radius + 1.0)


def high_dot(left, right):
    return jnp.dot(left, right, precision=lax.Precision.HIGHEST, preferred_element_type=jnp.float32)


def shifted(values, offset_by):
    return shifted_2(values, "blk", offset_by)


def beside_all(values):
    slab_values = lax.all_gather(values, "leaf", axis=1, tiled=True)
    return jnp.concatenate([shifted(slab_values, 1), slab_values, shifted(slab_values, -1)], axis=1)


def blk_split(n_blk):
    if n_blk % 8 == 0 and n_blk > 8:
        return (8, n_blk // 8)
    return (n_blk, 1)


def reduce_phases():
    inner, outer = blk_split(lax.axis_size("blk"))
    phases = [("leaf", lax.axis_size("leaf"), 1), ("blk", inner, 1)]
    if outer > 1:
        phases.append(("blk", outer, inner))
    return tuple(p for p in phases if p[1] > 1)


def group_peer(axis, n, stride, k):
    idx = lax.axis_index(axis)
    own = (idx // stride) % n
    return own, idx + ((own + k) % n - own) * stride


def sum_kernel(phases, x_ref, o_ref, recv, send_sem, recv_sem):
    barrier = pltpu.get_barrier_semaphore()
    greeted = 0
    for axis, n, stride in phases:
        for k in range(1, n):
            _, peer = group_peer(axis, n, stride, k)
            pl.semaphore_signal(
                barrier, 1, device_id={axis: peer}, device_id_type=pl.DeviceIdType.MESH
            )
            greeted += 1
    pl.semaphore_wait(barrier, greeted)
    acc = x_ref[...]
    for p, (axis, n, stride) in enumerate(phases):
        recv[p, 0] = acc
        copies = []
        for k in range(1, n):
            own, peer = group_peer(axis, n, stride, k)
            copy = pltpu.make_async_remote_copy(
                src_ref=x_ref if p == 0 else recv.at[p, 0],
                dst_ref=recv.at[p, k],
                send_sem=send_sem.at[p, k],
                recv_sem=recv_sem.at[p, k],
                device_id={axis: peer},
                device_id_type=pl.DeviceIdType.MESH,
            )
            copy.start()
            copies.append(copy)
        for copy in copies:
            copy.wait()
        own, _ = group_peer(axis, n, stride, 0)
        terms = [recv[p, (own - j) % n] for j in range(n)]
        acc = terms[0]
        for term in terms[1:]:
            acc = acc + term
    o_ref[...] = acc


def group_sum(values, collective_id):
    phases = reduce_phases()
    rows = values.shape[0]
    widest = max(n for _, n, _ in phases)
    return pl.pallas_call(
        lambda *refs: sum_kernel(phases, *refs),
        out_shape=jax.ShapeDtypeStruct(values.shape, jnp.float32),
        in_specs=[pl.BlockSpec(memory_space=pltpu.VMEM)],
        out_specs=pl.BlockSpec(memory_space=pltpu.VMEM),
        scratch_shapes=[
            pltpu.VMEM((len(phases), widest, rows, 128), jnp.float32),
            pltpu.SemaphoreType.DMA((len(phases), widest)),
            pltpu.SemaphoreType.DMA((len(phases), widest)),
        ],
        compiler_params=pltpu.CompilerParams(collective_id=collective_id, has_side_effects=True),
    )(values)


def gram_kernel(phases, x_ref, o_ref, *scratch):
    count = len(phases)
    recvs = scratch[:count]
    sums = scratch[count : 2 * count - 1]
    full = scratch[2 * count - 1]
    rs_send, rs_recv, ag_send, ag_recv = scratch[2 * count :]
    barrier = pltpu.get_barrier_semaphore()
    greeted = 0
    for axis, n, stride in phases:
        for k in range(1, n):
            _, peer = group_peer(axis, n, stride, k)
            pl.semaphore_signal(
                barrier, 1, device_id={axis: peer}, device_id_type=pl.DeviceIdType.MESH
            )
            greeted += 1
    pl.semaphore_wait(barrier, greeted)
    source = x_ref
    length = x_ref.shape[0]
    offset = 0
    for p, (axis, n, stride) in enumerate(phases):
        own, _ = group_peer(axis, n, stride, 0)
        part = length // n
        recv = recvs[p]
        recv[0] = source[pl.ds(pl.multiple_of(own * part, 8), part)]
        copies = []
        for k in range(1, n):
            _, peer = group_peer(axis, n, stride, k)
            chunk = (own + k) % n
            copy = pltpu.make_async_remote_copy(
                src_ref=source.at[pl.ds(pl.multiple_of(chunk * part, 8), part)],
                dst_ref=recv.at[k],
                send_sem=rs_send.at[p, k],
                recv_sem=rs_recv.at[p, k],
                device_id={axis: peer},
                device_id_type=pl.DeviceIdType.MESH,
            )
            copy.start()
            copies.append(copy)
        for copy in copies:
            copy.wait()
        acc = recv[own % n]
        for j in range(1, n):
            acc = acc + recv[(own - j) % n]
        offset = offset + own * part
        length = part
        if p < count - 1:
            sums[p][...] = acc
            source = sums[p]
        else:
            full[pl.ds(pl.multiple_of(offset, 8), part)] = acc
    for p in reversed(range(count)):
        axis, n, stride = phases[p]
        own, _ = group_peer(axis, n, stride, 0)
        here = full.at[pl.ds(pl.multiple_of(offset, 8), length)]
        copies = []
        for k in range(1, n):
            _, peer = group_peer(axis, n, stride, k)
            copy = pltpu.make_async_remote_copy(
                src_ref=here,
                dst_ref=here,
                send_sem=ag_send.at[p, k],
                recv_sem=ag_recv.at[p, k],
                device_id={axis: peer},
                device_id_type=pl.DeviceIdType.MESH,
            )
            copy.start()
            copies.append(copy)
        for copy in copies:
            copy.wait()
        offset = offset - own * length
        length = length * n
    o_ref[...] = full[...]


def gram_sum(values, collective_id):
    phases = (("samp", lax.axis_size("samp"), 1),) + reduce_phases()
    phases = tuple(p for p in phases if p[1] > 1)
    rows = values.shape[0]
    widest = max(n for _, n, _ in phases)
    recvs, sums = [], []
    length = rows
    for p, (_, n, _) in enumerate(phases):
        length //= n
        recvs.append(pltpu.VMEM((n, length, 128), jnp.float32))
        if p < len(phases) - 1:
            sums.append(pltpu.VMEM((length, 128), jnp.float32))
    semaphores = [pltpu.SemaphoreType.DMA((len(phases), widest)) for _ in range(4)]
    return pl.pallas_call(
        lambda *refs: gram_kernel(phases, *refs),
        out_shape=jax.ShapeDtypeStruct(values.shape, jnp.float32),
        in_specs=[pl.BlockSpec(memory_space=pltpu.VMEM)],
        out_specs=pl.BlockSpec(memory_space=pltpu.VMEM),
        scratch_shapes=recvs + sums + [pltpu.VMEM((rows, 128), jnp.float32)] + semaphores,
        compiler_params=pltpu.CompilerParams(collective_id=collective_id, has_side_effects=True),
    )(values)


def halo_kernel(n_blk, n_leaf, x_ref, o_ref, land, send_sem, recv_sem):
    own_blk = lax.axis_index("blk")
    own_leaf = lax.axis_index("leaf")
    targets = []
    for d in (-1, 1):
        for leaf in range(n_leaf):
            targets.append(((own_blk + d + n_blk) % n_blk, leaf, (1 - d) * n_leaf + own_leaf))
    for k in range(1, n_leaf):
        targets.append((own_blk, (own_leaf + k) % n_leaf, n_leaf + own_leaf))
    barrier = pltpu.get_barrier_semaphore()
    for blk, leaf, _ in targets:
        pl.semaphore_signal(
            barrier,
            1,
            device_id={"blk": blk, "leaf": leaf},
            device_id_type=pl.DeviceIdType.MESH,
        )
    pl.semaphore_wait(barrier, len(targets))
    copies = []
    for i, (blk, leaf, segment) in enumerate(targets):
        copy = pltpu.make_async_remote_copy(
            src_ref=x_ref,
            dst_ref=land.at[segment],
            send_sem=send_sem.at[i],
            recv_sem=recv_sem.at[segment],
            device_id={"blk": blk, "leaf": leaf},
            device_id_type=pl.DeviceIdType.MESH,
        )
        copy.start()
        copies.append(copy)
    land[n_leaf + own_leaf] = x_ref[...]
    incoming = [((own_blk - 1 + n_blk) % n_blk, s, s) for s in range(n_leaf)]
    incoming += [((own_blk + 1) % n_blk, s, 2 * n_leaf + s) for s in range(n_leaf)]
    for k in range(1, n_leaf):
        leaf = (own_leaf + k) % n_leaf
        incoming.append((own_blk, leaf, n_leaf + leaf))
    for copy in copies:
        copy.wait_send()
    for blk, leaf, segment in incoming:
        pltpu.make_async_remote_copy(
            src_ref=x_ref,
            dst_ref=land.at[segment],
            send_sem=send_sem.at[0],
            recv_sem=recv_sem.at[segment],
            device_id={"blk": blk, "leaf": leaf},
            device_id_type=pl.DeviceIdType.MESH,
        ).wait_recv()
    o_ref[...] = land[...]


def halo_gather(values, collective_id):
    n_blk = lax.axis_size("blk")
    n_leaf = lax.axis_size("leaf")
    segments = 3 * n_leaf
    return pl.pallas_call(
        lambda *refs: halo_kernel(n_blk, n_leaf, *refs),
        out_shape=jax.ShapeDtypeStruct((segments,) + values.shape, jnp.float32),
        in_specs=[pl.BlockSpec(memory_space=pltpu.VMEM)],
        out_specs=pl.BlockSpec(memory_space=pltpu.VMEM),
        scratch_shapes=[
            pltpu.VMEM((segments,) + values.shape, jnp.float32),
            pltpu.SemaphoreType.DMA((segments,)),
            pltpu.SemaphoreType.DMA((segments,)),
        ],
        compiler_params=pltpu.CompilerParams(collective_id=collective_id, has_side_effects=True),
    )(values)


def lower_solve(factor, values):
    return lax.linalg.triangular_solve(factor, values, left_side=True, lower=True)


def local(points, neighbors, omega, observed, prior_draws):
    blk_dev = neighbors.shape[0]
    cycle_count = lax.axis_size("blk")
    slab_blocks = blk_dev * lax.axis_size("leaf")
    period = 2.0 * cycle_count
    own_slab = lax.axis_index("blk")
    n_samp = lax.axis_size("samp")
    samp_idx = lax.axis_index("samp")
    usable = neighbors >= 0
    relative = jnp.mod(neighbors // slab_blocks - own_slab + 1, cycle_count)
    chosen = jnp.where(usable, relative * slab_blocks + jnp.mod(neighbors, slab_blocks), 0)
    usable_weight = usable.astype(jnp.float32)
    reach_blocks = halo_gather(points, 4)
    row_blocks = points.reshape(3, blk_dev, PB).transpose(1, 0, 2)

    segments = 3 * slab_blocks
    listed = jnp.zeros((segments,), jnp.float32).at[chosen[0]].max(usable_weight[0])
    kernel_tile = wendland(row_blocks[0], reach_blocks, period) * listed[:, None, None]

    def apply_kernel(values, wide=False):
        width = values.shape[0]
        if wide:
            slab_values = lax.all_gather(values, "leaf", axis=1, tiled=True)
            parts = (shifted(slab_values, 1), slab_values, shifted(slab_values, -1))
            out = None
            for i, part in enumerate(parts):
                tile = kernel_tile[i * slab_blocks : (i + 1) * slab_blocks]
                term = jnp.einsum(
                    "cnj,nij->ci",
                    part.reshape(width, slab_blocks, PB),
                    tile,
                    precision=lax.Precision.HIGHEST,
                )
                out = term if out is None else out + term
            return out
        reach = halo_gather(values, 6)
        return jnp.einsum("ncj,nij->ci", reach, kernel_tile, precision=lax.Precision.HIGHEST)

    def slot(x):
        zeros = jnp.zeros((n_samp,) + x.shape, x.dtype)
        return lax.dynamic_update_index_in_dim(zeros, x, samp_idx, 0)

    def unslot(xs):
        return lax.dynamic_index_in_dim(xs, samp_idx, 0, keepdims=False)

    def total_per_samp(values):
        return jax.tree.map(unslot, lax.psum(jax.tree.map(slot, values), ALL_AXES))

    sketch_rows = omega.shape[0]
    omega_rows = lax.dynamic_slice_in_dim(omega, samp_idx * (sketch_rows // n_samp), sketch_rows // n_samp)
    sketch = apply_kernel(omega_rows, wide=True) + sketch_shift * omega_rows
    sketch = lax.all_gather(sketch, "samp", axis=0, tiled=True)
    rhs = observed[None, :] - prior_draws
    half = PB // n_samp
    omega_half = lax.dynamic_slice_in_dim(omega, samp_idx * half, half, axis=1)
    sketch_half = lax.dynamic_slice_in_dim(sketch, samp_idx * half, half, axis=1)
    core_part = high_dot(omega_half, sketch_half.T)
    square_part = high_dot(sketch_half, sketch_half.T)
    joint_part = 0.5 * (core_part + core_part.T) + 0.5 * (square_part + square_part.T)
    gram_rows = joint_part.shape[0]
    joint_gram = gram_sum(joint_part.reshape(gram_rows * gram_rows // 128, 128), 2)
    joint_gram = joint_gram.reshape(gram_rows, gram_rows)
    width = rhs.shape[0]
    rhs_proj = high_dot(sketch, rhs.T).reshape(gram_rows * width // 128, 128)
    rhs_proj = group_sum(rhs_proj, 3).reshape(gram_rows, width)

    joint_factor = jnp.linalg.cholesky(joint_gram)

    def precond_from(vectors, projected):
        first_solve = lower_solve(joint_factor, projected)
        solved = lax.linalg.triangular_solve(
            joint_factor, first_solve, left_side=True, lower=True, transpose_a=True
        )
        return (vectors - high_dot(solved.T, sketch)) / noise_variance

    residual = rhs
    projected = rhs_proj
    precond = precond_from(residual, projected)
    direction = precond
    weights = jnp.zeros_like(rhs)

    sketch_rows = sketch.shape[0]

    def pack_scalars(*vectors):
        rows = jnp.stack(vectors)
        return jnp.pad(rows, ((0, 8 - rows.shape[0]), (0, 128 - width)))

    image = apply_kernel(direction) + noise_variance * direction
    image_proj = high_dot(sketch, image.T).reshape(sketch_rows * width // 128, 128)
    packed = jnp.concatenate(
        [
            image_proj,
            pack_scalars(
                jnp.sum(residual * precond, axis=1), jnp.sum(direction * image, axis=1)
            ),
        ]
    )
    packed = group_sum(packed, 0)
    image_proj = packed[:-8].reshape(sketch_rows, width)
    inner_now = packed[-8, :width]
    curvature = packed[-7, :width]
    step_size = inner_now / curvature
    weights = weights + step_size[:, None] * direction
    residual = residual - step_size[:, None] * image
    projected = projected - step_size[None, :] * image_proj
    precond = precond_from(residual, projected)
    inner_next = group_sum(pack_scalars(jnp.sum(residual * precond, axis=1)), 1)[0, :width]
    direction = precond + (inner_next / inner_now)[:, None] * direction
    inner_now = inner_next

    image = apply_kernel(direction) + noise_variance * direction
    curvature = group_sum(pack_scalars(jnp.sum(direction * image, axis=1)), 1)[0, :width]
    step_size = inner_now / curvature
    weights = weights + step_size[:, None] * direction
    residual = residual - step_size[:, None] * image
    return (weights, residual)


def solution(mesh):
    in_specs = (
        P(None, ("blk", "leaf")),
        P(("blk", "leaf"), None),
        P(None, ("blk", "leaf")),
        P(("blk", "leaf")),
        P("samp", ("blk", "leaf")),
    )
    out_specs = (P("samp", ("blk", "leaf")), P("samp", ("blk", "leaf")))
    return jax.shard_map(local, mesh=mesh, in_specs=in_specs, out_specs=out_specs, check_vma=False)
```

```python
import jax
import jax.numpy as jnp
from jax import lax
from jax.sharding import PartitionSpec as P
from jax.experimental import pallas as pl
from jax.experimental.pallas import tpu as pltpu

PB = 256
ITERS = 2


support_radius = 0.8
noise_variance = 1.0
sketch_shift = 1.0

ALL_AXES = ("blk", "leaf", "samp")


def shifted_2(block, axis, distance):
    devices = range(lax.axis_size(axis))
    route = [((i - distance) % len(devices), i) for i in devices]
    return lax.ppermute(block, axis, route)


def wendland(row_points, column_points, period):
    offset = row_points[None, :, :, None] - column_points[:, :, None, :]
    half_period = 0.5 * period
    along_x = jnp.mod(offset[:, 0] + half_period, period) - half_period
    squared = along_x * along_x + offset[:, 1] * offset[:, 1] + offset[:, 2] * offset[:, 2]
    radius = jnp.sqrt(squared) / support_radius
    remain = jnp.maximum(1.0 - radius, 0.0)
    return remain**4 * (4.0 * radius + 1.0)


def high_dot(left, right):
    return jnp.dot(left, right, precision=lax.Precision.HIGHEST, preferred_element_type=jnp.float32)


def shifted(values, offset_by):
    return shifted_2(values, "blk", offset_by)


def beside_all(values):
    slab_values = lax.all_gather(values, "leaf", axis=1, tiled=True)
    return jnp.concatenate([shifted(slab_values, 1), slab_values, shifted(slab_values, -1)], axis=1)


def blk_split(n_blk):
    if n_blk % 8 == 0 and n_blk > 8:
        return (8, n_blk // 8)
    return (n_blk, 1)


def reduce_phases():
    inner, outer = blk_split(lax.axis_size("blk"))
    phases = [("leaf", lax.axis_size("leaf"), 1), ("blk", inner, 1)]
    if outer > 1:
        phases.append(("blk", outer, inner))
    return tuple(p for p in phases if p[1] > 1)


def group_peer(axis, n, stride, k):
    idx = lax.axis_index(axis)
    own = (idx // stride) % n
    return own, idx + ((own + k) % n - own) * stride


def sum_kernel(phases, x_ref, o_ref, recv, send_sem, recv_sem):
    barrier = pltpu.get_barrier_semaphore()
    greeted = 0
    for axis, n, stride in phases:
        for k in range(1, n):
            _, peer = group_peer(axis, n, stride, k)
            pl.semaphore_signal(
                barrier, 1, device_id={axis: peer}, device_id_type=pl.DeviceIdType.MESH
            )
            greeted += 1
    pl.semaphore_wait(barrier, greeted)
    acc = x_ref[...]
    for p, (axis, n, stride) in enumerate(phases):
        recv[p, 0] = acc
        copies = []
        for k in range(1, n):
            own, peer = group_peer(axis, n, stride, k)
            copy = pltpu.make_async_remote_copy(
                src_ref=x_ref if p == 0 else recv.at[p, 0],
                dst_ref=recv.at[p, k],
                send_sem=send_sem.at[p, k],
                recv_sem=recv_sem.at[p, k],
                device_id={axis: peer},
                device_id_type=pl.DeviceIdType.MESH,
            )
            copy.start()
            copies.append(copy)
        for copy in copies:
            copy.wait()
        own, _ = group_peer(axis, n, stride, 0)
        terms = [recv[p, (own - j) % n] for j in range(n)]
        acc = terms[0]
        for term in terms[1:]:
            acc = acc + term
    o_ref[...] = acc


def group_sum(values, collective_id):
    phases = reduce_phases()
    rows = values.shape[0]
    widest = max(n for _, n, _ in phases)
    return pl.pallas_call(
        lambda *refs: sum_kernel(phases, *refs),
        out_shape=jax.ShapeDtypeStruct(values.shape, jnp.float32),
        in_specs=[pl.BlockSpec(memory_space=pltpu.VMEM)],
        out_specs=pl.BlockSpec(memory_space=pltpu.VMEM),
        scratch_shapes=[
            pltpu.VMEM((len(phases), widest, rows, 128), jnp.float32),
            pltpu.SemaphoreType.DMA((len(phases), widest)),
            pltpu.SemaphoreType.DMA((len(phases), widest)),
        ],
        compiler_params=pltpu.CompilerParams(collective_id=collective_id, has_side_effects=True),
    )(values)


def gram_kernel(phases, x_ref, y_ref, o_ref, z_ref, *scratch):
    count = len(phases)
    recvs = scratch[:count]
    sums = scratch[count : 2 * count - 1]
    full = scratch[2 * count - 1]
    rs_send, rs_recv, ag_send, ag_recv, side, side_send, side_recv = scratch[2 * count :]
    side_acc = y_ref[...]
    barrier = pltpu.get_barrier_semaphore()
    greeted = 0
    for axis, n, stride in phases:
        for k in range(1, n):
            _, peer = group_peer(axis, n, stride, k)
            pl.semaphore_signal(
                barrier, 1, device_id={axis: peer}, device_id_type=pl.DeviceIdType.MESH
            )
            greeted += 1
    pl.semaphore_wait(barrier, greeted)
    source = x_ref
    length = x_ref.shape[0]
    offset = 0
    for p, (axis, n, stride) in enumerate(phases):
        own, _ = group_peer(axis, n, stride, 0)
        part = length // n
        recv = recvs[p]
        recv[0] = source[pl.ds(pl.multiple_of(own * part, 8), part)]
        copies = []
        if axis != "samp":
            side[p, 0] = side_acc
            for k in range(1, n):
                _, peer = group_peer(axis, n, stride, k)
                copy = pltpu.make_async_remote_copy(
                    src_ref=side.at[p, 0],
                    dst_ref=side.at[p, k],
                    send_sem=side_send.at[p, k],
                    recv_sem=side_recv.at[p, k],
                    device_id={axis: peer},
                    device_id_type=pl.DeviceIdType.MESH,
                )
                copy.start()
                copies.append(copy)
        for k in range(1, n):
            _, peer = group_peer(axis, n, stride, k)
            chunk = (own + k) % n
            copy = pltpu.make_async_remote_copy(
                src_ref=source.at[pl.ds(pl.multiple_of(chunk * part, 8), part)],
                dst_ref=recv.at[k],
                send_sem=rs_send.at[p, k],
                recv_sem=rs_recv.at[p, k],
                device_id={axis: peer},
                device_id_type=pl.DeviceIdType.MESH,
            )
            copy.start()
            copies.append(copy)
        for copy in copies:
            copy.wait()
        acc = recv[own % n]
        for j in range(1, n):
            acc = acc + recv[(own - j) % n]
        if axis != "samp":
            side_acc = side[p, own % n]
            for j in range(1, n):
                side_acc = side_acc + side[p, (own - j) % n]
        offset = offset + own * part
        length = part
        if p < count - 1:
            sums[p][...] = acc
            source = sums[p]
        else:
            full[pl.ds(pl.multiple_of(offset, 8), part)] = acc
    for p in reversed(range(count)):
        axis, n, stride = phases[p]
        own, _ = group_peer(axis, n, stride, 0)
        here = full.at[pl.ds(pl.multiple_of(offset, 8), length)]
        copies = []
        for k in range(1, n):
            _, peer = group_peer(axis, n, stride, k)
            copy = pltpu.make_async_remote_copy(
                src_ref=here,
                dst_ref=here,
                send_sem=ag_send.at[p, k],
                recv_sem=ag_recv.at[p, k],
                device_id={axis: peer},
                device_id_type=pl.DeviceIdType.MESH,
            )
            copy.start()
            copies.append(copy)
        for copy in copies:
            copy.wait()
        offset = offset - own * length
        length = length * n
    o_ref[...] = full[...]
    z_ref[...] = side_acc


def gram_sum(values, side_values, collective_id):
    phases = (("samp", lax.axis_size("samp"), 1),) + reduce_phases()
    phases = tuple(p for p in phases if p[1] > 1)
    rows = values.shape[0]
    widest = max(n for _, n, _ in phases)
    recvs, sums = [], []
    length = rows
    for p, (_, n, _) in enumerate(phases):
        length //= n
        recvs.append(pltpu.VMEM((n, length, 128), jnp.float32))
        if p < len(phases) - 1:
            sums.append(pltpu.VMEM((length, 128), jnp.float32))
    semaphores = [pltpu.SemaphoreType.DMA((len(phases), widest)) for _ in range(4)]
    side_scratch = [
        pltpu.VMEM((len(phases), widest) + side_values.shape, jnp.float32),
        pltpu.SemaphoreType.DMA((len(phases), widest)),
        pltpu.SemaphoreType.DMA((len(phases), widest)),
    ]
    return pl.pallas_call(
        lambda *refs: gram_kernel(phases, *refs),
        out_shape=(
            jax.ShapeDtypeStruct(values.shape, jnp.float32),
            jax.ShapeDtypeStruct(side_values.shape, jnp.float32),
        ),
        in_specs=[pl.BlockSpec(memory_space=pltpu.VMEM)] * 2,
        out_specs=(pl.BlockSpec(memory_space=pltpu.VMEM),) * 2,
        scratch_shapes=recvs + sums + [pltpu.VMEM((rows, 128), jnp.float32)] + semaphores + side_scratch,
        compiler_params=pltpu.CompilerParams(collective_id=collective_id, has_side_effects=True),
    )(values, side_values)


def halo_kernel(n_blk, n_leaf, x_ref, o_ref, land, send_sem, recv_sem):
    own_blk = lax.axis_index("blk")
    own_leaf = lax.axis_index("leaf")
    targets = []
    for d in (-1, 1):
        for leaf in range(n_leaf):
            targets.append(((own_blk + d + n_blk) % n_blk, leaf, (1 - d) * n_leaf + own_leaf))
    for k in range(1, n_leaf):
        targets.append((own_blk, (own_leaf + k) % n_leaf, n_leaf + own_leaf))
    barrier = pltpu.get_barrier_semaphore()
    for blk, leaf, _ in targets:
        pl.semaphore_signal(
            barrier,
            1,
            device_id={"blk": blk, "leaf": leaf},
            device_id_type=pl.DeviceIdType.MESH,
        )
    pl.semaphore_wait(barrier, len(targets))
    copies = []
    for i, (blk, leaf, segment) in enumerate(targets):
        copy = pltpu.make_async_remote_copy(
            src_ref=x_ref,
            dst_ref=land.at[segment],
            send_sem=send_sem.at[i],
            recv_sem=recv_sem.at[segment],
            device_id={"blk": blk, "leaf": leaf},
            device_id_type=pl.DeviceIdType.MESH,
        )
        copy.start()
        copies.append(copy)
    land[n_leaf + own_leaf] = x_ref[...]
    incoming = [((own_blk - 1 + n_blk) % n_blk, s, s) for s in range(n_leaf)]
    incoming += [((own_blk + 1) % n_blk, s, 2 * n_leaf + s) for s in range(n_leaf)]
    for k in range(1, n_leaf):
        leaf = (own_leaf + k) % n_leaf
        incoming.append((own_blk, leaf, n_leaf + leaf))
    for copy in copies:
        copy.wait_send()
    for blk, leaf, segment in incoming:
        pltpu.make_async_remote_copy(
            src_ref=x_ref,
            dst_ref=land.at[segment],
            send_sem=send_sem.at[0],
            recv_sem=recv_sem.at[segment],
            device_id={"blk": blk, "leaf": leaf},
            device_id_type=pl.DeviceIdType.MESH,
        ).wait_recv()
    o_ref[...] = land[...]


def halo_gather(values, collective_id):
    n_blk = lax.axis_size("blk")
    n_leaf = lax.axis_size("leaf")
    segments = 3 * n_leaf
    return pl.pallas_call(
        lambda *refs: halo_kernel(n_blk, n_leaf, *refs),
        out_shape=jax.ShapeDtypeStruct((segments,) + values.shape, jnp.float32),
        in_specs=[pl.BlockSpec(memory_space=pltpu.VMEM)],
        out_specs=pl.BlockSpec(memory_space=pltpu.VMEM),
        scratch_shapes=[
            pltpu.VMEM((segments,) + values.shape, jnp.float32),
            pltpu.SemaphoreType.DMA((segments,)),
            pltpu.SemaphoreType.DMA((segments,)),
        ],
        compiler_params=pltpu.CompilerParams(collective_id=collective_id, has_side_effects=True),
    )(values)


def lower_solve(factor, values):
    return lax.linalg.triangular_solve(factor, values, left_side=True, lower=True)


def local(points, neighbors, omega, observed, prior_draws):
    blk_dev = neighbors.shape[0]
    cycle_count = lax.axis_size("blk")
    slab_blocks = blk_dev * lax.axis_size("leaf")
    period = 2.0 * cycle_count
    own_slab = lax.axis_index("blk")
    n_samp = lax.axis_size("samp")
    samp_idx = lax.axis_index("samp")
    usable = neighbors >= 0
    relative = jnp.mod(neighbors // slab_blocks - own_slab + 1, cycle_count)
    chosen = jnp.where(usable, relative * slab_blocks + jnp.mod(neighbors, slab_blocks), 0)
    usable_weight = usable.astype(jnp.float32)
    reach_blocks = halo_gather(points, 4)
    row_blocks = points.reshape(3, blk_dev, PB).transpose(1, 0, 2)

    segments = 3 * slab_blocks
    listed = jnp.zeros((segments,), jnp.float32).at[chosen[0]].max(usable_weight[0])
    kernel_tile = wendland(row_blocks[0], reach_blocks, period) * listed[:, None, None]

    def apply_kernel(values, wide=False):
        width = values.shape[0]
        if wide:
            slab_values = lax.all_gather(values, "leaf", axis=1, tiled=True)
            parts = (shifted(slab_values, 1), slab_values, shifted(slab_values, -1))
            out = None
            for i, part in enumerate(parts):
                tile = kernel_tile[i * slab_blocks : (i + 1) * slab_blocks]
                term = jnp.einsum(
                    "cnj,nij->ci",
                    part.reshape(width, slab_blocks, PB),
                    tile,
                    precision=lax.Precision.HIGHEST,
                )
                out = term if out is None else out + term
            return out
        reach = halo_gather(values, 6)
        return jnp.einsum("ncj,nij->ci", reach, kernel_tile, precision=lax.Precision.HIGHEST)

    def slot(x):
        zeros = jnp.zeros((n_samp,) + x.shape, x.dtype)
        return lax.dynamic_update_index_in_dim(zeros, x, samp_idx, 0)

    def unslot(xs):
        return lax.dynamic_index_in_dim(xs, samp_idx, 0, keepdims=False)

    def total_per_samp(values):
        return jax.tree.map(unslot, lax.psum(jax.tree.map(slot, values), ALL_AXES))

    sketch_rows = omega.shape[0]
    omega_rows = lax.dynamic_slice_in_dim(omega, samp_idx * (sketch_rows // n_samp), sketch_rows // n_samp)
    sketch = apply_kernel(omega_rows, wide=True) + sketch_shift * omega_rows
    sketch = lax.all_gather(sketch, "samp", axis=0, tiled=True)
    rhs = observed[None, :] - prior_draws
    half = PB // n_samp
    omega_half = lax.dynamic_slice_in_dim(omega, samp_idx * half, half, axis=1)
    sketch_half = lax.dynamic_slice_in_dim(sketch, samp_idx * half, half, axis=1)
    core_part = high_dot(omega_half, sketch_half.T)
    square_part = high_dot(sketch_half, sketch_half.T)
    joint_part = 0.5 * (core_part + core_part.T) + 0.5 * (square_part + square_part.T)
    gram_rows = joint_part.shape[0]
    width = rhs.shape[0]
    rhs_proj = high_dot(sketch, rhs.T).reshape(gram_rows * width // 128, 128)
    joint_gram, rhs_proj = gram_sum(joint_part.reshape(gram_rows * gram_rows // 128, 128), rhs_proj, 2)
    joint_gram = joint_gram.reshape(gram_rows, gram_rows)
    rhs_proj = rhs_proj.reshape(gram_rows, width)

    joint_factor = jnp.linalg.cholesky(joint_gram)

    def precond_from(vectors, projected):
        first_solve = lower_solve(joint_factor, projected)
        solved = lax.linalg.triangular_solve(
            joint_factor, first_solve, left_side=True, lower=True, transpose_a=True
        )
        return (vectors - high_dot(solved.T, sketch)) / noise_variance

    residual = rhs
    projected = rhs_proj
    precond = precond_from(residual, projected)
    direction = precond
    weights = jnp.zeros_like(rhs)

    sketch_rows = sketch.shape[0]

    def pack_scalars(*vectors):
        rows = jnp.stack(vectors)
        return jnp.pad(rows, ((0, 8 - rows.shape[0]), (0, 128 - width)))

    image = apply_kernel(direction) + noise_variance * direction
    image_proj = high_dot(sketch, image.T).reshape(sketch_rows * width // 128, 128)
    packed = jnp.concatenate(
        [
            image_proj,
            pack_scalars(
                jnp.sum(residual * precond, axis=1), jnp.sum(direction * image, axis=1)
            ),
        ]
    )
    packed = group_sum(packed, 0)
    image_proj = packed[:-8].reshape(sketch_rows, width)
    inner_now = packed[-8, :width]
    curvature = packed[-7, :width]
    step_size = inner_now / curvature
    weights = weights + step_size[:, None] * direction
    residual = residual - step_size[:, None] * image
    projected = projected - step_size[None, :] * image_proj
    precond = precond_from(residual, projected)
    inner_next = group_sum(pack_scalars(jnp.sum(residual * precond, axis=1)), 1)[0, :width]
    direction = precond + (inner_next / inner_now)[:, None] * direction
    inner_now = inner_next

    image = apply_kernel(direction) + noise_variance * direction
    curvature = group_sum(pack_scalars(jnp.sum(direction * image, axis=1)), 1)[0, :width]
    step_size = inner_now / curvature
    weights = weights + step_size[:, None] * direction
    residual = residual - step_size[:, None] * image
    return (weights, residual)


def solution(mesh):
    in_specs = (
        P(None, ("blk", "leaf")),
        P(("blk", "leaf"), None),
        P(None, ("blk", "leaf")),
        P(("blk", "leaf")),
        P("samp", ("blk", "leaf")),
    )
    out_specs = (P("samp", ("blk", "leaf")), P("samp", ("blk", "leaf")))
    return jax.shard_map(local, mesh=mesh, in_specs=in_specs, out_specs=out_specs, check_vma=False)
```

```python
import jax
import jax.numpy as jnp
from jax import lax
from jax.sharding import PartitionSpec as P
from jax.experimental import pallas as pl
from jax.experimental.pallas import tpu as pltpu

PB = 256
ITERS = 2


support_radius = 0.8
noise_variance = 1.0
sketch_shift = 1.0

ALL_AXES = ("blk", "leaf", "samp")


def shifted_2(block, axis, distance):
    devices = range(lax.axis_size(axis))
    route = [((i - distance) % len(devices), i) for i in devices]
    return lax.ppermute(block, axis, route)


def wendland(row_points, column_points, period):
    offset = row_points[None, :, :, None] - column_points[:, :, None, :]
    half_period = 0.5 * period
    along_x = jnp.mod(offset[:, 0] + half_period, period) - half_period
    squared = along_x * along_x + offset[:, 1] * offset[:, 1] + offset[:, 2] * offset[:, 2]
    radius = jnp.sqrt(squared) / support_radius
    remain = jnp.maximum(1.0 - radius, 0.0)
    return remain**4 * (4.0 * radius + 1.0)


def high_dot(left, right):
    return jnp.dot(left, right, precision=lax.Precision.HIGHEST, preferred_element_type=jnp.float32)


def shifted(values, offset_by):
    return shifted_2(values, "blk", offset_by)


def beside_all(values):
    slab_values = lax.all_gather(values, "leaf", axis=1, tiled=True)
    return jnp.concatenate([shifted(slab_values, 1), slab_values, shifted(slab_values, -1)], axis=1)


def blk_split(n_blk):
    if n_blk % 8 == 0 and n_blk > 8:
        return (8, n_blk // 8)
    return (n_blk, 1)


def reduce_phases():
    inner, outer = blk_split(lax.axis_size("blk"))
    phases = [("leaf", lax.axis_size("leaf"), 1), ("blk", inner, 1)]
    if outer > 1:
        phases.append(("blk", outer, inner))
    return tuple(p for p in phases if p[1] > 1)


def group_peer(axis, n, stride, k):
    idx = lax.axis_index(axis)
    own = (idx // stride) % n
    return own, idx + ((own + k) % n - own) * stride


def sum_kernel(phases, x_ref, o_ref, recv, send_sem, recv_sem):
    barrier = pltpu.get_barrier_semaphore()
    greeted = 0
    for axis, n, stride in phases:
        for k in range(1, n):
            _, peer = group_peer(axis, n, stride, k)
            pl.semaphore_signal(
                barrier, 1, device_id={axis: peer}, device_id_type=pl.DeviceIdType.MESH
            )
            greeted += 1
    pl.semaphore_wait(barrier, greeted)
    acc = x_ref[...]
    for p, (axis, n, stride) in enumerate(phases):
        recv[p, 0] = acc
        copies = []
        for k in range(1, n):
            own, peer = group_peer(axis, n, stride, k)
            copy = pltpu.make_async_remote_copy(
                src_ref=x_ref if p == 0 else recv.at[p, 0],
                dst_ref=recv.at[p, k],
                send_sem=send_sem.at[p, k],
                recv_sem=recv_sem.at[p, k],
                device_id={axis: peer},
                device_id_type=pl.DeviceIdType.MESH,
            )
            copy.start()
            copies.append(copy)
        for copy in copies:
            copy.wait()
        own, _ = group_peer(axis, n, stride, 0)
        terms = [recv[p, (own - j) % n] for j in range(n)]
        acc = terms[0]
        for term in terms[1:]:
            acc = acc + term
    o_ref[...] = acc


def group_sum(values, collective_id):
    phases = reduce_phases()
    rows = values.shape[0]
    widest = max(n for _, n, _ in phases)
    return pl.pallas_call(
        lambda *refs: sum_kernel(phases, *refs),
        out_shape=jax.ShapeDtypeStruct(values.shape, jnp.float32),
        in_specs=[pl.BlockSpec(memory_space=pltpu.VMEM)],
        out_specs=pl.BlockSpec(memory_space=pltpu.VMEM),
        scratch_shapes=[
            pltpu.VMEM((len(phases), widest, rows, 128), jnp.float32),
            pltpu.SemaphoreType.DMA((len(phases), widest)),
            pltpu.SemaphoreType.DMA((len(phases), widest)),
        ],
        compiler_params=pltpu.CompilerParams(collective_id=collective_id, has_side_effects=True),
    )(values)


def gram_kernel(phases, x_ref, y_ref, o_ref, z_ref, *scratch):
    count = len(phases)
    recvs = scratch[:count]
    sums = scratch[count : 2 * count - 1]
    full = scratch[2 * count - 1]
    rs_send, rs_recv, ag_send, ag_recv, side, side_send, side_recv = scratch[2 * count :]
    side_acc = y_ref[...]
    barrier = pltpu.get_barrier_semaphore()
    greeted = 0
    for axis, n, stride in phases:
        for k in range(1, n):
            _, peer = group_peer(axis, n, stride, k)
            pl.semaphore_signal(
                barrier, 1, device_id={axis: peer}, device_id_type=pl.DeviceIdType.MESH
            )
            greeted += 1
    pl.semaphore_wait(barrier, greeted)
    source = x_ref
    length = x_ref.shape[0]
    offset = 0
    for p, (axis, n, stride) in enumerate(phases):
        own, _ = group_peer(axis, n, stride, 0)
        part = length // n
        recv = recvs[p]
        recv[0] = source[pl.ds(pl.multiple_of(own * part, 8), part)]
        copies = []
        if axis != "samp":
            side[p, 0] = side_acc
            for k in range(1, n):
                _, peer = group_peer(axis, n, stride, k)
                copy = pltpu.make_async_remote_copy(
                    src_ref=side.at[p, 0],
                    dst_ref=side.at[p, k],
                    send_sem=side_send.at[p, k],
                    recv_sem=side_recv.at[p, k],
                    device_id={axis: peer},
                    device_id_type=pl.DeviceIdType.MESH,
                )
                copy.start()
                copies.append(copy)
        for k in range(1, n):
            _, peer = group_peer(axis, n, stride, k)
            chunk = (own + k) % n
            copy = pltpu.make_async_remote_copy(
                src_ref=source.at[pl.ds(pl.multiple_of(chunk * part, 8), part)],
                dst_ref=recv.at[k],
                send_sem=rs_send.at[p, k],
                recv_sem=rs_recv.at[p, k],
                device_id={axis: peer},
                device_id_type=pl.DeviceIdType.MESH,
            )
            copy.start()
            copies.append(copy)
        for copy in copies:
            copy.wait()
        acc = recv[own % n]
        for j in range(1, n):
            acc = acc + recv[(own - j) % n]
        if axis != "samp":
            side_acc = side[p, own % n]
            for j in range(1, n):
                side_acc = side_acc + side[p, (own - j) % n]
        offset = offset + own * part
        length = part
        if p < count - 1:
            sums[p][...] = acc
            source = sums[p]
        else:
            full[pl.ds(pl.multiple_of(offset, 8), part)] = acc
    for p in reversed(range(count)):
        axis, n, stride = phases[p]
        own, _ = group_peer(axis, n, stride, 0)
        here = full.at[pl.ds(pl.multiple_of(offset, 8), length)]
        copies = []
        for k in range(1, n):
            _, peer = group_peer(axis, n, stride, k)
            copy = pltpu.make_async_remote_copy(
                src_ref=here,
                dst_ref=here,
                send_sem=ag_send.at[p, k],
                recv_sem=ag_recv.at[p, k],
                device_id={axis: peer},
                device_id_type=pl.DeviceIdType.MESH,
            )
            copy.start()
            copies.append(copy)
        for copy in copies:
            copy.wait()
        offset = offset - own * length
        length = length * n
    o_ref[...] = full[...]
    z_ref[...] = side_acc


def gram_sum(values, side_values, collective_id):
    phases = (("samp", lax.axis_size("samp"), 1),) + reduce_phases()
    phases = tuple(p for p in phases if p[1] > 1)
    rows = values.shape[0]
    widest = max(n for _, n, _ in phases)
    recvs, sums = [], []
    length = rows
    for p, (_, n, _) in enumerate(phases):
        length //= n
        recvs.append(pltpu.VMEM((n, length, 128), jnp.float32))
        if p < len(phases) - 1:
            sums.append(pltpu.VMEM((length, 128), jnp.float32))
    semaphores = [pltpu.SemaphoreType.DMA((len(phases), widest)) for _ in range(4)]
    side_scratch = [
        pltpu.VMEM((len(phases), widest) + side_values.shape, jnp.float32),
        pltpu.SemaphoreType.DMA((len(phases), widest)),
        pltpu.SemaphoreType.DMA((len(phases), widest)),
    ]
    return pl.pallas_call(
        lambda *refs: gram_kernel(phases, *refs),
        out_shape=(
            jax.ShapeDtypeStruct(values.shape, jnp.float32),
            jax.ShapeDtypeStruct(side_values.shape, jnp.float32),
        ),
        in_specs=[pl.BlockSpec(memory_space=pltpu.VMEM)] * 2,
        out_specs=(pl.BlockSpec(memory_space=pltpu.VMEM),) * 2,
        scratch_shapes=recvs + sums + [pltpu.VMEM((rows, 128), jnp.float32)] + semaphores + side_scratch,
        compiler_params=pltpu.CompilerParams(collective_id=collective_id, has_side_effects=True),
    )(values, side_values)


def halo_kernel(n_blk, n_leaf, x_ref, o_ref, land, send_sem, recv_sem):
    own_blk = lax.axis_index("blk")
    own_leaf = lax.axis_index("leaf")
    targets = []
    for d in (-1, 1):
        for leaf in range(n_leaf):
            targets.append(((own_blk + d + n_blk) % n_blk, leaf, (1 - d) * n_leaf + own_leaf))
    for k in range(1, n_leaf):
        targets.append((own_blk, (own_leaf + k) % n_leaf, n_leaf + own_leaf))
    barrier = pltpu.get_barrier_semaphore()
    for blk, leaf, _ in targets:
        pl.semaphore_signal(
            barrier,
            1,
            device_id={"blk": blk, "leaf": leaf},
            device_id_type=pl.DeviceIdType.MESH,
        )
    pl.semaphore_wait(barrier, len(targets))
    copies = []
    for i, (blk, leaf, segment) in enumerate(targets):
        copy = pltpu.make_async_remote_copy(
            src_ref=x_ref,
            dst_ref=land.at[segment],
            send_sem=send_sem.at[i],
            recv_sem=recv_sem.at[segment],
            device_id={"blk": blk, "leaf": leaf},
            device_id_type=pl.DeviceIdType.MESH,
        )
        copy.start()
        copies.append(copy)
    land[n_leaf + own_leaf] = x_ref[...]
    incoming = [((own_blk - 1 + n_blk) % n_blk, s, s) for s in range(n_leaf)]
    incoming += [((own_blk + 1) % n_blk, s, 2 * n_leaf + s) for s in range(n_leaf)]
    for k in range(1, n_leaf):
        leaf = (own_leaf + k) % n_leaf
        incoming.append((own_blk, leaf, n_leaf + leaf))
    for copy in copies:
        copy.wait_send()
    for blk, leaf, segment in incoming:
        pltpu.make_async_remote_copy(
            src_ref=x_ref,
            dst_ref=land.at[segment],
            send_sem=send_sem.at[0],
            recv_sem=recv_sem.at[segment],
            device_id={"blk": blk, "leaf": leaf},
            device_id_type=pl.DeviceIdType.MESH,
        ).wait_recv()
    o_ref[...] = land[...]


def halo_gather(values, collective_id):
    n_blk = lax.axis_size("blk")
    n_leaf = lax.axis_size("leaf")
    segments = 3 * n_leaf
    return pl.pallas_call(
        lambda *refs: halo_kernel(n_blk, n_leaf, *refs),
        out_shape=jax.ShapeDtypeStruct((segments,) + values.shape, jnp.float32),
        in_specs=[pl.BlockSpec(memory_space=pltpu.VMEM)],
        out_specs=pl.BlockSpec(memory_space=pltpu.VMEM),
        scratch_shapes=[
            pltpu.VMEM((segments,) + values.shape, jnp.float32),
            pltpu.SemaphoreType.DMA((segments,)),
            pltpu.SemaphoreType.DMA((segments,)),
        ],
        compiler_params=pltpu.CompilerParams(collective_id=collective_id, has_side_effects=True),
    )(values)


def lower_solve(factor, values):
    return lax.linalg.triangular_solve(factor, values, left_side=True, lower=True)


def local(points, neighbors, omega, observed, prior_draws):
    blk_dev = neighbors.shape[0]
    cycle_count = lax.axis_size("blk")
    slab_blocks = blk_dev * lax.axis_size("leaf")
    period = 2.0 * cycle_count
    own_slab = lax.axis_index("blk")
    n_samp = lax.axis_size("samp")
    samp_idx = lax.axis_index("samp")
    usable = neighbors >= 0
    relative = jnp.mod(neighbors // slab_blocks - own_slab + 1, cycle_count)
    chosen = jnp.where(usable, relative * slab_blocks + jnp.mod(neighbors, slab_blocks), 0)
    usable_weight = usable.astype(jnp.float32)
    reach_blocks = halo_gather(points, 4)
    row_blocks = points.reshape(3, blk_dev, PB).transpose(1, 0, 2)

    segments = 3 * slab_blocks
    listed = jnp.zeros((segments,), jnp.float32).at[chosen[0]].max(usable_weight[0])
    kernel_tile = wendland(row_blocks[0], reach_blocks, period) * listed[:, None, None]

    def apply_kernel(values, wide=False):
        width = values.shape[0]
        if wide:
            slab_values = lax.all_gather(values, "leaf", axis=1, tiled=True)
            parts = (shifted(slab_values, 1), slab_values, shifted(slab_values, -1))
            out = None
            for i, part in enumerate(parts):
                tile = kernel_tile[i * slab_blocks : (i + 1) * slab_blocks]
                term = jnp.einsum(
                    "cnj,nij->ci",
                    part.reshape(width, slab_blocks, PB),
                    tile,
                    precision=lax.Precision.HIGHEST,
                )
                out = term if out is None else out + term
            return out
        reach = halo_gather(values, 6)
        return jnp.einsum("ncj,nij->ci", reach, kernel_tile, precision=lax.Precision.HIGHEST)

    def slot(x):
        zeros = jnp.zeros((n_samp,) + x.shape, x.dtype)
        return lax.dynamic_update_index_in_dim(zeros, x, samp_idx, 0)

    def unslot(xs):
        return lax.dynamic_index_in_dim(xs, samp_idx, 0, keepdims=False)

    def total_per_samp(values):
        return jax.tree.map(unslot, lax.psum(jax.tree.map(slot, values), ALL_AXES))

    sketch_rows = omega.shape[0]
    omega_rows = lax.dynamic_slice_in_dim(omega, samp_idx * (sketch_rows // n_samp), sketch_rows // n_samp)
    sketch = apply_kernel(omega_rows, wide=True) + sketch_shift * omega_rows
    sketch = lax.all_gather(sketch, "samp", axis=0, tiled=True)
    rhs = observed[None, :] - prior_draws
    half = PB // n_samp
    omega_half = lax.dynamic_slice_in_dim(omega, samp_idx * half, half, axis=1)
    sketch_half = lax.dynamic_slice_in_dim(sketch, samp_idx * half, half, axis=1)
    core_part = high_dot(omega_half, sketch_half.T)
    square_part = high_dot(sketch_half, sketch_half.T)
    joint_part = 0.5 * (core_part + core_part.T) + 0.5 * (square_part + square_part.T)
    gram_rows = joint_part.shape[0]
    width = rhs.shape[0]
    rhs_proj = high_dot(sketch, rhs.T).reshape(gram_rows * width // 128, 128)
    joint_gram, rhs_proj = gram_sum(joint_part.reshape(gram_rows * gram_rows // 128, 128), rhs_proj, 2)
    joint_gram = joint_gram.reshape(gram_rows, gram_rows)
    rhs_proj = rhs_proj.reshape(gram_rows, width)

    joint_factor = jnp.linalg.cholesky(joint_gram)

    def precond_from(vectors, projected):
        first_solve = lower_solve(joint_factor, projected)
        solved = lax.linalg.triangular_solve(
            joint_factor, first_solve, left_side=True, lower=True, transpose_a=True
        )
        return (vectors - high_dot(solved.T, sketch)) / noise_variance, solved

    residual = rhs
    projected = rhs_proj
    precond, _ = precond_from(residual, projected)
    direction = precond
    weights = jnp.zeros_like(rhs)

    sketch_rows = sketch.shape[0]

    def pack_scalars(*vectors):
        rows = jnp.stack(vectors)
        return jnp.pad(rows, ((0, 8 - rows.shape[0]), (0, 128 - width)))

    image = apply_kernel(direction) + noise_variance * direction
    image_proj = high_dot(sketch, image.T).reshape(sketch_rows * width // 128, 128)
    packed = jnp.concatenate(
        [
            image_proj,
            pack_scalars(
                jnp.sum(residual * precond, axis=1),
                jnp.sum(direction * image, axis=1),
                jnp.sum(residual * residual, axis=1),
                jnp.sum(residual * image, axis=1),
                jnp.sum(image * image, axis=1),
            ),
        ]
    )
    packed = group_sum(packed, 0)
    image_proj = packed[:-8].reshape(sketch_rows, width)
    inner_now = packed[-8, :width]
    curvature = packed[-7, :width]
    residual_sq, residual_image, image_sq = packed[-6, :width], packed[-5, :width], packed[-4, :width]
    step_size = inner_now / curvature
    weights = weights + step_size[:, None] * direction
    residual = residual - step_size[:, None] * image
    projected = projected - step_size[None, :] * image_proj
    precond, solved = precond_from(residual, projected)
    residual_sq = residual_sq - 2.0 * step_size * residual_image + step_size * step_size * image_sq
    inner_next = (residual_sq - jnp.sum(projected * solved, axis=0)) / noise_variance
    direction = precond + (inner_next / inner_now)[:, None] * direction
    inner_now = inner_next

    image = apply_kernel(direction) + noise_variance * direction
    curvature = group_sum(pack_scalars(jnp.sum(direction * image, axis=1)), 1)[0, :width]
    step_size = inner_now / curvature
    weights = weights + step_size[:, None] * direction
    residual = residual - step_size[:, None] * image
    return (weights, residual)


def solution(mesh):
    in_specs = (
        P(None, ("blk", "leaf")),
        P(("blk", "leaf"), None),
        P(None, ("blk", "leaf")),
        P(("blk", "leaf")),
        P("samp", ("blk", "leaf")),
    )
    out_specs = (P("samp", ("blk", "leaf")), P("samp", ("blk", "leaf")))
    return jax.shard_map(local, mesh=mesh, in_specs=in_specs, out_specs=out_specs, check_vma=False)
```

```python
import jax
import jax.numpy as jnp
from jax import lax
from jax.sharding import PartitionSpec as P
from jax.experimental import pallas as pl
from jax.experimental.pallas import tpu as pltpu

PB = 256
ITERS = 2


support_radius = 0.8
noise_variance = 1.0
sketch_shift = 1.0

ALL_AXES = ("blk", "leaf", "samp")


def shifted_2(block, axis, distance):
    devices = range(lax.axis_size(axis))
    route = [((i - distance) % len(devices), i) for i in devices]
    return lax.ppermute(block, axis, route)


def wendland(row_points, column_points, period):
    offset = row_points[None, :, :, None] - column_points[:, :, None, :]
    half_period = 0.5 * period
    along_x = jnp.mod(offset[:, 0] + half_period, period) - half_period
    squared = along_x * along_x + offset[:, 1] * offset[:, 1] + offset[:, 2] * offset[:, 2]
    radius = jnp.sqrt(squared) / support_radius
    remain = jnp.maximum(1.0 - radius, 0.0)
    return remain**4 * (4.0 * radius + 1.0)


def high_dot(left, right):
    return jnp.dot(left, right, precision=lax.Precision.HIGHEST, preferred_element_type=jnp.float32)


def shifted(values, offset_by):
    return shifted_2(values, "blk", offset_by)


def beside_all(values):
    slab_values = lax.all_gather(values, "leaf", axis=1, tiled=True)
    return jnp.concatenate([shifted(slab_values, 1), slab_values, shifted(slab_values, -1)], axis=1)


def blk_split(n_blk):
    if n_blk % 8 == 0 and n_blk > 8:
        return (8, n_blk // 8)
    return (n_blk, 1)


def reduce_phases():
    inner, outer = blk_split(lax.axis_size("blk"))
    phases = [("leaf", lax.axis_size("leaf"), 1), ("blk", inner, 1)]
    if outer > 1:
        phases.append(("blk", outer, inner))
    return tuple(p for p in phases if p[1] > 1)


def group_peer(axis, n, stride, k):
    idx = lax.axis_index(axis)
    own = (idx // stride) % n
    return own, idx + ((own + k) % n - own) * stride


def sum_kernel(phases, x_ref, o_ref, recv, send_sem, recv_sem):
    barrier = pltpu.get_barrier_semaphore()
    greeted = 0
    for axis, n, stride in phases:
        for k in range(1, n):
            _, peer = group_peer(axis, n, stride, k)
            pl.semaphore_signal(
                barrier, 1, device_id={axis: peer}, device_id_type=pl.DeviceIdType.MESH
            )
            greeted += 1
    pl.semaphore_wait(barrier, greeted)
    acc = x_ref[...]
    for p, (axis, n, stride) in enumerate(phases):
        recv[p, 0] = acc
        copies = []
        for k in range(1, n):
            own, peer = group_peer(axis, n, stride, k)
            copy = pltpu.make_async_remote_copy(
                src_ref=x_ref if p == 0 else recv.at[p, 0],
                dst_ref=recv.at[p, k],
                send_sem=send_sem.at[p, k],
                recv_sem=recv_sem.at[p, k],
                device_id={axis: peer},
                device_id_type=pl.DeviceIdType.MESH,
            )
            copy.start()
            copies.append(copy)
        for copy in copies:
            copy.wait()
        own, _ = group_peer(axis, n, stride, 0)
        terms = [recv[p, (own - j) % n] for j in range(n)]
        acc = terms[0]
        for term in terms[1:]:
            acc = acc + term
    o_ref[...] = acc


def group_sum(values, collective_id):
    phases = reduce_phases()
    rows = values.shape[0]
    widest = max(n for _, n, _ in phases)
    return pl.pallas_call(
        lambda *refs: sum_kernel(phases, *refs),
        out_shape=jax.ShapeDtypeStruct(values.shape, jnp.float32),
        in_specs=[pl.BlockSpec(memory_space=pltpu.VMEM)],
        out_specs=pl.BlockSpec(memory_space=pltpu.VMEM),
        scratch_shapes=[
            pltpu.VMEM((len(phases), widest, rows, 128), jnp.float32),
            pltpu.SemaphoreType.DMA((len(phases), widest)),
            pltpu.SemaphoreType.DMA((len(phases), widest)),
        ],
        compiler_params=pltpu.CompilerParams(collective_id=collective_id, has_side_effects=True),
    )(values)


def gram_kernel(phases, x_ref, y_ref, o_ref, z_ref, *scratch):
    count = len(phases)
    recvs = scratch[:count]
    sums = scratch[count : 2 * count - 1]
    full = scratch[2 * count - 1]
    rs_send, rs_recv, ag_send, ag_recv, side, side_send, side_recv = scratch[2 * count :]
    side_acc = y_ref[...]
    barrier = pltpu.get_barrier_semaphore()
    greeted = 0
    for axis, n, stride in phases:
        for k in range(1, n):
            _, peer = group_peer(axis, n, stride, k)
            pl.semaphore_signal(
                barrier, 1, device_id={axis: peer}, device_id_type=pl.DeviceIdType.MESH
            )
            greeted += 1
    pl.semaphore_wait(barrier, greeted)
    source = x_ref
    length = x_ref.shape[0]
    offset = 0
    for p, (axis, n, stride) in enumerate(phases):
        own, _ = group_peer(axis, n, stride, 0)
        part = length // n
        recv = recvs[p]
        recv[0] = source[pl.ds(pl.multiple_of(own * part, 8), part)]
        copies = []
        if axis != "samp":
            side[p, 0] = side_acc
            for k in range(1, n):
                _, peer = group_peer(axis, n, stride, k)
                copy = pltpu.make_async_remote_copy(
                    src_ref=side.at[p, 0],
                    dst_ref=side.at[p, k],
                    send_sem=side_send.at[p, k],
                    recv_sem=side_recv.at[p, k],
                    device_id={axis: peer},
                    device_id_type=pl.DeviceIdType.MESH,
                )
                copy.start()
                copies.append(copy)
        for k in range(1, n):
            _, peer = group_peer(axis, n, stride, k)
            chunk = (own + k) % n
            copy = pltpu.make_async_remote_copy(
                src_ref=source.at[pl.ds(pl.multiple_of(chunk * part, 8), part)],
                dst_ref=recv.at[k],
                send_sem=rs_send.at[p, k],
                recv_sem=rs_recv.at[p, k],
                device_id={axis: peer},
                device_id_type=pl.DeviceIdType.MESH,
            )
            copy.start()
            copies.append(copy)
        for copy in copies:
            copy.wait()
        acc = recv[own % n]
        for j in range(1, n):
            acc = acc + recv[(own - j) % n]
        if axis != "samp":
            side_acc = side[p, own % n]
            for j in range(1, n):
                side_acc = side_acc + side[p, (own - j) % n]
        offset = offset + own * part
        length = part
        if p < count - 1:
            sums[p][...] = acc
            source = sums[p]
        else:
            full[pl.ds(pl.multiple_of(offset, 8), part)] = acc
    for p in reversed(range(count)):
        axis, n, stride = phases[p]
        own, _ = group_peer(axis, n, stride, 0)
        here = full.at[pl.ds(pl.multiple_of(offset, 8), length)]
        copies = []
        for k in range(1, n):
            _, peer = group_peer(axis, n, stride, k)
            copy = pltpu.make_async_remote_copy(
                src_ref=here,
                dst_ref=here,
                send_sem=ag_send.at[p, k],
                recv_sem=ag_recv.at[p, k],
                device_id={axis: peer},
                device_id_type=pl.DeviceIdType.MESH,
            )
            copy.start()
            copies.append(copy)
        for copy in copies:
            copy.wait()
        offset = offset - own * length
        length = length * n
    o_ref[...] = full[...]
    z_ref[...] = side_acc


def gram_sum(values, side_values, collective_id):
    phases = (("samp", lax.axis_size("samp"), 1),) + reduce_phases()
    phases = tuple(p for p in phases if p[1] > 1)
    rows = values.shape[0]
    widest = max(n for _, n, _ in phases)
    recvs, sums = [], []
    length = rows
    for p, (_, n, _) in enumerate(phases):
        length //= n
        recvs.append(pltpu.VMEM((n, length, 128), jnp.float32))
        if p < len(phases) - 1:
            sums.append(pltpu.VMEM((length, 128), jnp.float32))
    semaphores = [pltpu.SemaphoreType.DMA((len(phases), widest)) for _ in range(4)]
    side_scratch = [
        pltpu.VMEM((len(phases), widest) + side_values.shape, jnp.float32),
        pltpu.SemaphoreType.DMA((len(phases), widest)),
        pltpu.SemaphoreType.DMA((len(phases), widest)),
    ]
    return pl.pallas_call(
        lambda *refs: gram_kernel(phases, *refs),
        out_shape=(
            jax.ShapeDtypeStruct(values.shape, jnp.float32),
            jax.ShapeDtypeStruct(side_values.shape, jnp.float32),
        ),
        in_specs=[pl.BlockSpec(memory_space=pltpu.VMEM)] * 2,
        out_specs=(pl.BlockSpec(memory_space=pltpu.VMEM),) * 2,
        scratch_shapes=recvs + sums + [pltpu.VMEM((rows, 128), jnp.float32)] + semaphores + side_scratch,
        compiler_params=pltpu.CompilerParams(collective_id=collective_id, has_side_effects=True),
    )(values, side_values)


def halo_kernel(n_blk, n_leaf, x_ref, o_ref, land, send_sem, recv_sem):
    own_blk = lax.axis_index("blk")
    own_leaf = lax.axis_index("leaf")
    targets = []
    for d in (-1, 1):
        for leaf in range(n_leaf):
            targets.append(((own_blk + d + n_blk) % n_blk, leaf, (1 - d) * n_leaf + own_leaf))
    for k in range(1, n_leaf):
        targets.append((own_blk, (own_leaf + k) % n_leaf, n_leaf + own_leaf))
    barrier = pltpu.get_barrier_semaphore()
    for blk, leaf, _ in targets:
        pl.semaphore_signal(
            barrier,
            1,
            device_id={"blk": blk, "leaf": leaf},
            device_id_type=pl.DeviceIdType.MESH,
        )
    pl.semaphore_wait(barrier, len(targets))
    copies = []
    for i, (blk, leaf, segment) in enumerate(targets):
        copy = pltpu.make_async_remote_copy(
            src_ref=x_ref,
            dst_ref=land.at[segment],
            send_sem=send_sem.at[i],
            recv_sem=recv_sem.at[segment],
            device_id={"blk": blk, "leaf": leaf},
            device_id_type=pl.DeviceIdType.MESH,
        )
        copy.start()
        copies.append(copy)
    land[n_leaf + own_leaf] = x_ref[...]
    incoming = [((own_blk - 1 + n_blk) % n_blk, s, s) for s in range(n_leaf)]
    incoming += [((own_blk + 1) % n_blk, s, 2 * n_leaf + s) for s in range(n_leaf)]
    for k in range(1, n_leaf):
        leaf = (own_leaf + k) % n_leaf
        incoming.append((own_blk, leaf, n_leaf + leaf))
    for copy in copies:
        copy.wait_send()
    for blk, leaf, segment in incoming:
        pltpu.make_async_remote_copy(
            src_ref=x_ref,
            dst_ref=land.at[segment],
            send_sem=send_sem.at[0],
            recv_sem=recv_sem.at[segment],
            device_id={"blk": blk, "leaf": leaf},
            device_id_type=pl.DeviceIdType.MESH,
        ).wait_recv()
    o_ref[...] = land[...]


def halo_gather(values, collective_id):
    n_blk = lax.axis_size("blk")
    n_leaf = lax.axis_size("leaf")
    segments = 3 * n_leaf
    return pl.pallas_call(
        lambda *refs: halo_kernel(n_blk, n_leaf, *refs),
        out_shape=jax.ShapeDtypeStruct((segments,) + values.shape, jnp.float32),
        in_specs=[pl.BlockSpec(memory_space=pltpu.VMEM)],
        out_specs=pl.BlockSpec(memory_space=pltpu.VMEM),
        scratch_shapes=[
            pltpu.VMEM((segments,) + values.shape, jnp.float32),
            pltpu.SemaphoreType.DMA((segments,)),
            pltpu.SemaphoreType.DMA((segments,)),
        ],
        compiler_params=pltpu.CompilerParams(collective_id=collective_id, has_side_effects=True),
    )(values)


def blocked_factor(gram, block=128):
    count = gram.shape[0] // block
    eye = jnp.eye(block, dtype=jnp.float32)
    inverses, panels = [], []
    rest = gram
    for k in range(count):
        diagonal = lax.linalg.cholesky(rest[:block, :block])
        inverse = lax.linalg.triangular_solve(diagonal, eye, left_side=True, lower=True)
        inverses.append(inverse)
        if k < count - 1:
            panel = high_dot(rest[block:, :block], inverse.T)
            panels.append(panel)
            rest = rest[block:, block:] - high_dot(panel, panel.T)
    return inverses, panels


def blocked_solve(inverses, panels, values):
    block = inverses[0].shape[0]
    count = len(inverses)
    lower = []
    rest = values
    for k in range(count):
        part = high_dot(inverses[k], rest[:block])
        lower.append(part)
        if k < count - 1:
            rest = rest[block:] - high_dot(panels[k], part)
    upper = [None] * count
    for k in reversed(range(count)):
        rhs = lower[k]
        if k < count - 1:
            rhs = rhs - high_dot(panels[k].T, jnp.concatenate(upper[k + 1 :]))
        upper[k] = high_dot(inverses[k].T, rhs)
    return jnp.concatenate(upper)


def lower_solve(factor, values):
    return lax.linalg.triangular_solve(factor, values, left_side=True, lower=True)


def local(points, neighbors, omega, observed, prior_draws):
    blk_dev = neighbors.shape[0]
    cycle_count = lax.axis_size("blk")
    slab_blocks = blk_dev * lax.axis_size("leaf")
    period = 2.0 * cycle_count
    own_slab = lax.axis_index("blk")
    n_samp = lax.axis_size("samp")
    samp_idx = lax.axis_index("samp")
    usable = neighbors >= 0
    relative = jnp.mod(neighbors // slab_blocks - own_slab + 1, cycle_count)
    chosen = jnp.where(usable, relative * slab_blocks + jnp.mod(neighbors, slab_blocks), 0)
    usable_weight = usable.astype(jnp.float32)
    reach_blocks = halo_gather(points, 4)
    row_blocks = points.reshape(3, blk_dev, PB).transpose(1, 0, 2)

    segments = 3 * slab_blocks
    listed = jnp.zeros((segments,), jnp.float32).at[chosen[0]].max(usable_weight[0])
    kernel_tile = wendland(row_blocks[0], reach_blocks, period) * listed[:, None, None]

    def apply_kernel(values, wide=False):
        width = values.shape[0]
        if wide:
            slab_values = lax.all_gather(values, "leaf", axis=1, tiled=True)
            parts = (shifted(slab_values, 1), slab_values, shifted(slab_values, -1))
            out = None
            for i, part in enumerate(parts):
                tile = kernel_tile[i * slab_blocks : (i + 1) * slab_blocks]
                term = jnp.einsum(
                    "cnj,nij->ci",
                    part.reshape(width, slab_blocks, PB),
                    tile,
                    precision=lax.Precision.HIGHEST,
                )
                out = term if out is None else out + term
            return out
        reach = halo_gather(values, 6)
        return jnp.einsum("ncj,nij->ci", reach, kernel_tile, precision=lax.Precision.HIGHEST)

    def slot(x):
        zeros = jnp.zeros((n_samp,) + x.shape, x.dtype)
        return lax.dynamic_update_index_in_dim(zeros, x, samp_idx, 0)

    def unslot(xs):
        return lax.dynamic_index_in_dim(xs, samp_idx, 0, keepdims=False)

    def total_per_samp(values):
        return jax.tree.map(unslot, lax.psum(jax.tree.map(slot, values), ALL_AXES))

    sketch_rows = omega.shape[0]
    omega_rows = lax.dynamic_slice_in_dim(omega, samp_idx * (sketch_rows // n_samp), sketch_rows // n_samp)
    sketch = apply_kernel(omega_rows, wide=True) + sketch_shift * omega_rows
    sketch = lax.all_gather(sketch, "samp", axis=0, tiled=True)
    rhs = observed[None, :] - prior_draws
    half = PB // n_samp
    omega_half = lax.dynamic_slice_in_dim(omega, samp_idx * half, half, axis=1)
    sketch_half = lax.dynamic_slice_in_dim(sketch, samp_idx * half, half, axis=1)
    core_part = high_dot(omega_half, sketch_half.T)
    square_part = high_dot(sketch_half, sketch_half.T)
    joint_part = 0.5 * (core_part + core_part.T) + 0.5 * (square_part + square_part.T)
    gram_rows = joint_part.shape[0]
    width = rhs.shape[0]
    rhs_proj = high_dot(sketch, rhs.T).reshape(gram_rows * width // 128, 128)
    joint_gram, rhs_proj = gram_sum(joint_part.reshape(gram_rows * gram_rows // 128, 128), rhs_proj, 2)
    joint_gram = joint_gram.reshape(gram_rows, gram_rows)
    rhs_proj = rhs_proj.reshape(gram_rows, width)

    inverses, panels = blocked_factor(joint_gram)

    def precond_from(vectors, projected):
        solved = blocked_solve(inverses, panels, projected)
        return (vectors - high_dot(solved.T, sketch)) / noise_variance, solved

    residual = rhs
    projected = rhs_proj
    precond, _ = precond_from(residual, projected)
    direction = precond
    weights = jnp.zeros_like(rhs)

    sketch_rows = sketch.shape[0]

    def pack_scalars(*vectors):
        rows = jnp.stack(vectors)
        return jnp.pad(rows, ((0, 8 - rows.shape[0]), (0, 128 - width)))

    image = apply_kernel(direction) + noise_variance * direction
    image_proj = high_dot(sketch, image.T).reshape(sketch_rows * width // 128, 128)
    packed = jnp.concatenate(
        [
            image_proj,
            pack_scalars(
                jnp.sum(residual * precond, axis=1),
                jnp.sum(direction * image, axis=1),
                jnp.sum(residual * residual, axis=1),
                jnp.sum(residual * image, axis=1),
                jnp.sum(image * image, axis=1),
            ),
        ]
    )
    packed = group_sum(packed, 0)
    image_proj = packed[:-8].reshape(sketch_rows, width)
    inner_now = packed[-8, :width]
    curvature = packed[-7, :width]
    residual_sq, residual_image, image_sq = packed[-6, :width], packed[-5, :width], packed[-4, :width]
    step_size = inner_now / curvature
    weights = weights + step_size[:, None] * direction
    residual = residual - step_size[:, None] * image
    projected = projected - step_size[None, :] * image_proj
    precond, solved = precond_from(residual, projected)
    residual_sq = residual_sq - 2.0 * step_size * residual_image + step_size * step_size * image_sq
    inner_next = (residual_sq - jnp.sum(projected * solved, axis=0)) / noise_variance
    direction = precond + (inner_next / inner_now)[:, None] * direction
    inner_now = inner_next

    image = apply_kernel(direction) + noise_variance * direction
    curvature = group_sum(pack_scalars(jnp.sum(direction * image, axis=1)), 1)[0, :width]
    step_size = inner_now / curvature
    weights = weights + step_size[:, None] * direction
    residual = residual - step_size[:, None] * image
    return (weights, residual)


def solution(mesh):
    in_specs = (
        P(None, ("blk", "leaf")),
        P(("blk", "leaf"), None),
        P(None, ("blk", "leaf")),
        P(("blk", "leaf")),
        P("samp", ("blk", "leaf")),
    )
    out_specs = (P("samp", ("blk", "leaf")), P("samp", ("blk", "leaf")))
    return jax.shard_map(local, mesh=mesh, in_specs=in_specs, out_specs=out_specs, check_vma=False)
```

```python
import jax
import jax.numpy as jnp
from jax import lax
from jax.sharding import PartitionSpec as P
from jax.experimental import pallas as pl
from jax.experimental.pallas import tpu as pltpu

PB = 256
ITERS = 2


support_radius = 0.8
noise_variance = 1.0
sketch_shift = 1.0

ALL_AXES = ("blk", "leaf", "samp")


def shifted_2(block, axis, distance):
    devices = range(lax.axis_size(axis))
    route = [((i - distance) % len(devices), i) for i in devices]
    return lax.ppermute(block, axis, route)


def wendland(row_points, column_points, period):
    offset = row_points[None, :, :, None] - column_points[:, :, None, :]
    half_period = 0.5 * period
    along_x = jnp.mod(offset[:, 0] + half_period, period) - half_period
    squared = along_x * along_x + offset[:, 1] * offset[:, 1] + offset[:, 2] * offset[:, 2]
    radius = jnp.sqrt(squared) / support_radius
    remain = jnp.maximum(1.0 - radius, 0.0)
    return remain**4 * (4.0 * radius + 1.0)


def high_dot(left, right):
    return jnp.dot(left, right, precision=lax.Precision.HIGHEST, preferred_element_type=jnp.float32)


def shifted(values, offset_by):
    return shifted_2(values, "blk", offset_by)


def beside_all(values):
    slab_values = lax.all_gather(values, "leaf", axis=1, tiled=True)
    return jnp.concatenate([shifted(slab_values, 1), slab_values, shifted(slab_values, -1)], axis=1)


def blk_split(n_blk):
    if n_blk % 8 == 0 and n_blk > 8:
        return (8, n_blk // 8)
    return (n_blk, 1)


def reduce_phases():
    inner, outer = blk_split(lax.axis_size("blk"))
    phases = [("leaf", lax.axis_size("leaf"), 1), ("blk", inner, 1)]
    if outer > 1:
        phases.append(("blk", outer, inner))
    return tuple(p for p in phases if p[1] > 1)


def group_peer(axis, n, stride, k):
    if axis == "slab":
        inner = n // lax.axis_size("leaf")
        blk = lax.axis_index("blk")
        own = lax.axis_index("leaf") * inner + blk % inner
        other = (own + k) % n
        return own, (blk - blk % inner + other % inner, other // inner)
    idx = lax.axis_index(axis)
    own = (idx // stride) % n
    return own, idx + ((own + k) % n - own) * stride


def device_of(axis, peer):
    if axis == "slab":
        return {"blk": peer[0], "leaf": peer[1]}
    return {axis: peer}


def sum_kernel(phases, x_ref, o_ref, recv, send_sem, recv_sem):
    barrier = pltpu.get_barrier_semaphore()
    greeted = 0
    for axis, n, stride in phases:
        for k in range(1, n):
            _, peer = group_peer(axis, n, stride, k)
            pl.semaphore_signal(
                barrier, 1, device_id=device_of(axis, peer), device_id_type=pl.DeviceIdType.MESH
            )
            greeted += 1
    pl.semaphore_wait(barrier, greeted)
    acc = x_ref[...]
    for p, (axis, n, stride) in enumerate(phases):
        recv[p, 0] = acc
        copies = []
        for k in range(1, n):
            own, peer = group_peer(axis, n, stride, k)
            copy = pltpu.make_async_remote_copy(
                src_ref=x_ref if p == 0 else recv.at[p, 0],
                dst_ref=recv.at[p, k],
                send_sem=send_sem.at[p, k],
                recv_sem=recv_sem.at[p, k],
                device_id=device_of(axis, peer),
                device_id_type=pl.DeviceIdType.MESH,
            )
            copy.start()
            copies.append(copy)
        for copy in copies:
            copy.wait()
        own, _ = group_peer(axis, n, stride, 0)
        terms = [recv[p, (own - j) % n] for j in range(n)]
        acc = terms[0]
        for term in terms[1:]:
            acc = acc + term
    o_ref[...] = acc


def group_sum(values, collective_id, merged=False):
    phases = reduce_phases()
    if merged and len(phases) == 3:
        phases = (("slab", phases[0][1] * phases[1][1], 1), phases[2])
    rows = values.shape[0]
    widest = max(n for _, n, _ in phases)
    return pl.pallas_call(
        lambda *refs: sum_kernel(phases, *refs),
        out_shape=jax.ShapeDtypeStruct(values.shape, jnp.float32),
        in_specs=[pl.BlockSpec(memory_space=pltpu.VMEM)],
        out_specs=pl.BlockSpec(memory_space=pltpu.VMEM),
        scratch_shapes=[
            pltpu.VMEM((len(phases), widest, rows, 128), jnp.float32),
            pltpu.SemaphoreType.DMA((len(phases), widest)),
            pltpu.SemaphoreType.DMA((len(phases), widest)),
        ],
        compiler_params=pltpu.CompilerParams(collective_id=collective_id, has_side_effects=True),
    )(values)


def gram_kernel(phases, x_ref, y_ref, o_ref, z_ref, *scratch):
    count = len(phases)
    recvs = scratch[:count]
    sums = scratch[count : 2 * count - 1]
    full = scratch[2 * count - 1]
    rs_send, rs_recv, ag_send, ag_recv, side, side_send, side_recv = scratch[2 * count :]
    side_acc = y_ref[...]
    barrier = pltpu.get_barrier_semaphore()
    greeted = 0
    for axis, n, stride in phases:
        for k in range(1, n):
            _, peer = group_peer(axis, n, stride, k)
            pl.semaphore_signal(
                barrier, 1, device_id={axis: peer}, device_id_type=pl.DeviceIdType.MESH
            )
            greeted += 1
    pl.semaphore_wait(barrier, greeted)
    source = x_ref
    length = x_ref.shape[0]
    offset = 0
    for p, (axis, n, stride) in enumerate(phases):
        own, _ = group_peer(axis, n, stride, 0)
        part = length // n
        recv = recvs[p]
        recv[0] = source[pl.ds(pl.multiple_of(own * part, 8), part)]
        copies = []
        if axis != "samp":
            side[p, 0] = side_acc
            for k in range(1, n):
                _, peer = group_peer(axis, n, stride, k)
                copy = pltpu.make_async_remote_copy(
                    src_ref=side.at[p, 0],
                    dst_ref=side.at[p, k],
                    send_sem=side_send.at[p, k],
                    recv_sem=side_recv.at[p, k],
                    device_id={axis: peer},
                    device_id_type=pl.DeviceIdType.MESH,
                )
                copy.start()
                copies.append(copy)
        for k in range(1, n):
            _, peer = group_peer(axis, n, stride, k)
            chunk = (own + k) % n
            copy = pltpu.make_async_remote_copy(
                src_ref=source.at[pl.ds(pl.multiple_of(chunk * part, 8), part)],
                dst_ref=recv.at[k],
                send_sem=rs_send.at[p, k],
                recv_sem=rs_recv.at[p, k],
                device_id={axis: peer},
                device_id_type=pl.DeviceIdType.MESH,
            )
            copy.start()
            copies.append(copy)
        for copy in copies:
            copy.wait()
        acc = recv[own % n]
        for j in range(1, n):
            acc = acc + recv[(own - j) % n]
        if axis != "samp":
            side_acc = side[p, own % n]
            for j in range(1, n):
                side_acc = side_acc + side[p, (own - j) % n]
        offset = offset + own * part
        length = part
        if p < count - 1:
            sums[p][...] = acc
            source = sums[p]
        else:
            full[pl.ds(pl.multiple_of(offset, 8), part)] = acc
    for p in reversed(range(count)):
        axis, n, stride = phases[p]
        own, _ = group_peer(axis, n, stride, 0)
        here = full.at[pl.ds(pl.multiple_of(offset, 8), length)]
        copies = []
        for k in range(1, n):
            _, peer = group_peer(axis, n, stride, k)
            copy = pltpu.make_async_remote_copy(
                src_ref=here,
                dst_ref=here,
                send_sem=ag_send.at[p, k],
                recv_sem=ag_recv.at[p, k],
                device_id={axis: peer},
                device_id_type=pl.DeviceIdType.MESH,
            )
            copy.start()
            copies.append(copy)
        for copy in copies:
            copy.wait()
        offset = offset - own * length
        length = length * n
    o_ref[...] = full[...]
    z_ref[...] = side_acc


def gram_sum(values, side_values, collective_id):
    phases = (("samp", lax.axis_size("samp"), 1),) + reduce_phases()
    phases = tuple(p for p in phases if p[1] > 1)
    rows = values.shape[0]
    widest = max(n for _, n, _ in phases)
    recvs, sums = [], []
    length = rows
    for p, (_, n, _) in enumerate(phases):
        length //= n
        recvs.append(pltpu.VMEM((n, length, 128), jnp.float32))
        if p < len(phases) - 1:
            sums.append(pltpu.VMEM((length, 128), jnp.float32))
    semaphores = [pltpu.SemaphoreType.DMA((len(phases), widest)) for _ in range(4)]
    side_scratch = [
        pltpu.VMEM((len(phases), widest) + side_values.shape, jnp.float32),
        pltpu.SemaphoreType.DMA((len(phases), widest)),
        pltpu.SemaphoreType.DMA((len(phases), widest)),
    ]
    return pl.pallas_call(
        lambda *refs: gram_kernel(phases, *refs),
        out_shape=(
            jax.ShapeDtypeStruct(values.shape, jnp.float32),
            jax.ShapeDtypeStruct(side_values.shape, jnp.float32),
        ),
        in_specs=[pl.BlockSpec(memory_space=pltpu.VMEM)] * 2,
        out_specs=(pl.BlockSpec(memory_space=pltpu.VMEM),) * 2,
        scratch_shapes=recvs + sums + [pltpu.VMEM((rows, 128), jnp.float32)] + semaphores + side_scratch,
        compiler_params=pltpu.CompilerParams(collective_id=collective_id, has_side_effects=True),
    )(values, side_values)


def halo_kernel(n_blk, n_leaf, x_ref, o_ref, land, send_sem, recv_sem):
    own_blk = lax.axis_index("blk")
    own_leaf = lax.axis_index("leaf")
    targets = []
    for d in (-1, 1):
        for leaf in range(n_leaf):
            targets.append(((own_blk + d + n_blk) % n_blk, leaf, (1 - d) * n_leaf + own_leaf))
    for k in range(1, n_leaf):
        targets.append((own_blk, (own_leaf + k) % n_leaf, n_leaf + own_leaf))
    barrier = pltpu.get_barrier_semaphore()
    for blk, leaf, _ in targets:
        pl.semaphore_signal(
            barrier,
            1,
            device_id={"blk": blk, "leaf": leaf},
            device_id_type=pl.DeviceIdType.MESH,
        )
    pl.semaphore_wait(barrier, len(targets))
    copies = []
    for i, (blk, leaf, segment) in enumerate(targets):
        copy = pltpu.make_async_remote_copy(
            src_ref=x_ref,
            dst_ref=land.at[segment],
            send_sem=send_sem.at[i],
            recv_sem=recv_sem.at[segment],
            device_id={"blk": blk, "leaf": leaf},
            device_id_type=pl.DeviceIdType.MESH,
        )
        copy.start()
        copies.append(copy)
    land[n_leaf + own_leaf] = x_ref[...]
    incoming = [((own_blk - 1 + n_blk) % n_blk, s, s) for s in range(n_leaf)]
    incoming += [((own_blk + 1) % n_blk, s, 2 * n_leaf + s) for s in range(n_leaf)]
    for k in range(1, n_leaf):
        leaf = (own_leaf + k) % n_leaf
        incoming.append((own_blk, leaf, n_leaf + leaf))
    for copy in copies:
        copy.wait_send()
    for blk, leaf, segment in incoming:
        pltpu.make_async_remote_copy(
            src_ref=x_ref,
            dst_ref=land.at[segment],
            send_sem=send_sem.at[0],
            recv_sem=recv_sem.at[segment],
            device_id={"blk": blk, "leaf": leaf},
            device_id_type=pl.DeviceIdType.MESH,
        ).wait_recv()
    o_ref[...] = land[...]


def halo_gather(values, collective_id):
    n_blk = lax.axis_size("blk")
    n_leaf = lax.axis_size("leaf")
    segments = 3 * n_leaf
    return pl.pallas_call(
        lambda *refs: halo_kernel(n_blk, n_leaf, *refs),
        out_shape=jax.ShapeDtypeStruct((segments,) + values.shape, jnp.float32),
        in_specs=[pl.BlockSpec(memory_space=pltpu.VMEM)],
        out_specs=pl.BlockSpec(memory_space=pltpu.VMEM),
        scratch_shapes=[
            pltpu.VMEM((segments,) + values.shape, jnp.float32),
            pltpu.SemaphoreType.DMA((segments,)),
            pltpu.SemaphoreType.DMA((segments,)),
        ],
        compiler_params=pltpu.CompilerParams(collective_id=collective_id, has_side_effects=True),
    )(values)


def blocked_factor(gram, block=128):
    count = gram.shape[0] // block
    eye = jnp.eye(block, dtype=jnp.float32)
    inverses, panels = [], []
    rest = gram
    for k in range(count):
        diagonal = lax.linalg.cholesky(rest[:block, :block])
        inverse = lax.linalg.triangular_solve(diagonal, eye, left_side=True, lower=True)
        inverses.append(inverse)
        if k < count - 1:
            panel = high_dot(rest[block:, :block], inverse.T)
            panels.append(panel)
            rest = rest[block:, block:] - high_dot(panel, panel.T)
    return inverses, panels


def blocked_solve(inverses, panels, values):
    block = inverses[0].shape[0]
    count = len(inverses)
    lower = []
    rest = values
    for k in range(count):
        part = high_dot(inverses[k], rest[:block])
        lower.append(part)
        if k < count - 1:
            rest = rest[block:] - high_dot(panels[k], part)
    upper = [None] * count
    for k in reversed(range(count)):
        rhs = lower[k]
        if k < count - 1:
            rhs = rhs - high_dot(panels[k].T, jnp.concatenate(upper[k + 1 :]))
        upper[k] = high_dot(inverses[k].T, rhs)
    return jnp.concatenate(upper)


def lower_solve(factor, values):
    return lax.linalg.triangular_solve(factor, values, left_side=True, lower=True)


def local(points, neighbors, omega, observed, prior_draws):
    blk_dev = neighbors.shape[0]
    cycle_count = lax.axis_size("blk")
    slab_blocks = blk_dev * lax.axis_size("leaf")
    period = 2.0 * cycle_count
    own_slab = lax.axis_index("blk")
    n_samp = lax.axis_size("samp")
    samp_idx = lax.axis_index("samp")
    usable = neighbors >= 0
    relative = jnp.mod(neighbors // slab_blocks - own_slab + 1, cycle_count)
    chosen = jnp.where(usable, relative * slab_blocks + jnp.mod(neighbors, slab_blocks), 0)
    usable_weight = usable.astype(jnp.float32)
    reach_blocks = halo_gather(points, 4)
    row_blocks = points.reshape(3, blk_dev, PB).transpose(1, 0, 2)

    segments = 3 * slab_blocks
    listed = jnp.zeros((segments,), jnp.float32).at[chosen[0]].max(usable_weight[0])
    kernel_tile = wendland(row_blocks[0], reach_blocks, period) * listed[:, None, None]

    def apply_kernel(values, wide=False):
        width = values.shape[0]
        if wide:
            slab_values = lax.all_gather(values, "leaf", axis=1, tiled=True)
            parts = (shifted(slab_values, 1), slab_values, shifted(slab_values, -1))
            out = None
            for i, part in enumerate(parts):
                tile = kernel_tile[i * slab_blocks : (i + 1) * slab_blocks]
                term = jnp.einsum(
                    "cnj,nij->ci",
                    part.reshape(width, slab_blocks, PB),
                    tile,
                    precision=lax.Precision.HIGHEST,
                )
                out = term if out is None else out + term
            return out
        reach = halo_gather(values, 6)
        return jnp.einsum("ncj,nij->ci", reach, kernel_tile, precision=lax.Precision.HIGHEST)

    def slot(x):
        zeros = jnp.zeros((n_samp,) + x.shape, x.dtype)
        return lax.dynamic_update_index_in_dim(zeros, x, samp_idx, 0)

    def unslot(xs):
        return lax.dynamic_index_in_dim(xs, samp_idx, 0, keepdims=False)

    def total_per_samp(values):
        return jax.tree.map(unslot, lax.psum(jax.tree.map(slot, values), ALL_AXES))

    sketch_rows = omega.shape[0]
    omega_rows = lax.dynamic_slice_in_dim(omega, samp_idx * (sketch_rows // n_samp), sketch_rows // n_samp)
    sketch = apply_kernel(omega_rows, wide=True) + sketch_shift * omega_rows
    sketch = lax.all_gather(sketch, "samp", axis=0, tiled=True)
    rhs = observed[None, :] - prior_draws
    half = PB // n_samp
    omega_half = lax.dynamic_slice_in_dim(omega, samp_idx * half, half, axis=1)
    sketch_half = lax.dynamic_slice_in_dim(sketch, samp_idx * half, half, axis=1)
    core_part = high_dot(omega_half, sketch_half.T)
    square_part = high_dot(sketch_half, sketch_half.T)
    joint_part = 0.5 * (core_part + core_part.T) + 0.5 * (square_part + square_part.T)
    gram_rows = joint_part.shape[0]
    width = rhs.shape[0]
    rhs_proj = high_dot(sketch, rhs.T).reshape(gram_rows * width // 128, 128)
    joint_gram, rhs_proj = gram_sum(joint_part.reshape(gram_rows * gram_rows // 128, 128), rhs_proj, 2)
    joint_gram = joint_gram.reshape(gram_rows, gram_rows)
    rhs_proj = rhs_proj.reshape(gram_rows, width)

    inverses, panels = blocked_factor(joint_gram)

    def precond_from(vectors, projected):
        solved = blocked_solve(inverses, panels, projected)
        return (vectors - high_dot(solved.T, sketch)) / noise_variance, solved

    residual = rhs
    projected = rhs_proj
    precond, _ = precond_from(residual, projected)
    direction = precond
    weights = jnp.zeros_like(rhs)

    sketch_rows = sketch.shape[0]

    def pack_scalars(*vectors):
        rows = jnp.stack(vectors)
        return jnp.pad(rows, ((0, 8 - rows.shape[0]), (0, 128 - width)))

    image = apply_kernel(direction) + noise_variance * direction
    image_proj = high_dot(sketch, image.T).reshape(sketch_rows * width // 128, 128)
    packed = jnp.concatenate(
        [
            image_proj,
            pack_scalars(
                jnp.sum(residual * precond, axis=1),
                jnp.sum(direction * image, axis=1),
                jnp.sum(residual * residual, axis=1),
                jnp.sum(residual * image, axis=1),
                jnp.sum(image * image, axis=1),
            ),
        ]
    )
    packed = group_sum(packed, 0)
    image_proj = packed[:-8].reshape(sketch_rows, width)
    inner_now = packed[-8, :width]
    curvature = packed[-7, :width]
    residual_sq, residual_image, image_sq = packed[-6, :width], packed[-5, :width], packed[-4, :width]
    step_size = inner_now / curvature
    weights = weights + step_size[:, None] * direction
    residual = residual - step_size[:, None] * image
    projected = projected - step_size[None, :] * image_proj
    precond, solved = precond_from(residual, projected)
    residual_sq = residual_sq - 2.0 * step_size * residual_image + step_size * step_size * image_sq
    inner_next = (residual_sq - jnp.sum(projected * solved, axis=0)) / noise_variance
    direction = precond + (inner_next / inner_now)[:, None] * direction
    inner_now = inner_next

    image = apply_kernel(direction) + noise_variance * direction
    curvature = group_sum(pack_scalars(jnp.sum(direction * image, axis=1)), 1, merged=True)[0, :width]
    step_size = inner_now / curvature
    weights = weights + step_size[:, None] * direction
    residual = residual - step_size[:, None] * image
    return (weights, residual)


def solution(mesh):
    in_specs = (
        P(None, ("blk", "leaf")),
        P(("blk", "leaf"), None),
        P(None, ("blk", "leaf")),
        P(("blk", "leaf")),
        P("samp", ("blk", "leaf")),
    )
    out_specs = (P("samp", ("blk", "leaf")), P("samp", ("blk", "leaf")))
    return jax.shard_map(local, mesh=mesh, in_specs=in_specs, out_specs=out_specs, check_vma=False)
```

```python
import jax
import jax.numpy as jnp
from jax import lax
from jax.sharding import PartitionSpec as P
from jax.experimental import pallas as pl
from jax.experimental.pallas import tpu as pltpu

PB = 256
ITERS = 2


support_radius = 0.8
noise_variance = 1.0
sketch_shift = 1.0

ALL_AXES = ("blk", "leaf", "samp")


def shifted_2(block, axis, distance):
    devices = range(lax.axis_size(axis))
    route = [((i - distance) % len(devices), i) for i in devices]
    return lax.ppermute(block, axis, route)


def wendland(row_points, column_points, period):
    offset = row_points[None, :, :, None] - column_points[:, :, None, :]
    half_period = 0.5 * period
    along_x = jnp.mod(offset[:, 0] + half_period, period) - half_period
    squared = along_x * along_x + offset[:, 1] * offset[:, 1] + offset[:, 2] * offset[:, 2]
    radius = jnp.sqrt(squared) / support_radius
    remain = jnp.maximum(1.0 - radius, 0.0)
    return remain**4 * (4.0 * radius + 1.0)


def high_dot(left, right):
    return jnp.dot(left, right, precision=lax.Precision.HIGHEST, preferred_element_type=jnp.float32)


def shifted(values, offset_by):
    return shifted_2(values, "blk", offset_by)


def beside_all(values):
    slab_values = lax.all_gather(values, "leaf", axis=1, tiled=True)
    return jnp.concatenate([shifted(slab_values, 1), slab_values, shifted(slab_values, -1)], axis=1)


def blk_split(n_blk):
    if n_blk % 8 == 0 and n_blk > 8:
        return (8, n_blk // 8)
    return (n_blk, 1)


def reduce_phases():
    inner, outer = blk_split(lax.axis_size("blk"))
    phases = [("leaf", lax.axis_size("leaf"), 1), ("blk", inner, 1)]
    if outer > 1:
        phases.append(("blk", outer, inner))
    return tuple(p for p in phases if p[1] > 1)


def group_peer(axis, n, stride, k):
    idx = lax.axis_index(axis)
    own = (idx // stride) % n
    return own, idx + ((own + k) % n - own) * stride


def sum_kernel(phases, x_ref, o_ref, recv, send_sem, recv_sem):
    barrier = pltpu.get_barrier_semaphore()
    greeted = 0
    for axis, n, stride in phases:
        for k in range(1, n):
            _, peer = group_peer(axis, n, stride, k)
            pl.semaphore_signal(
                barrier, 1, device_id={axis: peer}, device_id_type=pl.DeviceIdType.MESH
            )
            greeted += 1
    pl.semaphore_wait(barrier, greeted)
    acc = x_ref[...]
    for p, (axis, n, stride) in enumerate(phases):
        recv[p, 0] = acc
        copies = []
        for k in range(1, n):
            own, peer = group_peer(axis, n, stride, k)
            copy = pltpu.make_async_remote_copy(
                src_ref=x_ref if p == 0 else recv.at[p, 0],
                dst_ref=recv.at[p, k],
                send_sem=send_sem.at[p, k],
                recv_sem=recv_sem.at[p, k],
                device_id={axis: peer},
                device_id_type=pl.DeviceIdType.MESH,
            )
            copy.start()
            copies.append(copy)
        for copy in copies:
            copy.wait()
        own, _ = group_peer(axis, n, stride, 0)
        terms = [recv[p, (own - j) % n] for j in range(n)]
        acc = terms[0]
        for term in terms[1:]:
            acc = acc + term
    o_ref[...] = acc


def group_sum(values, collective_id):
    phases = reduce_phases()
    rows = values.shape[0]
    widest = max(n for _, n, _ in phases)
    return pl.pallas_call(
        lambda *refs: sum_kernel(phases, *refs),
        out_shape=jax.ShapeDtypeStruct(values.shape, jnp.float32),
        in_specs=[pl.BlockSpec(memory_space=pltpu.VMEM)],
        out_specs=pl.BlockSpec(memory_space=pltpu.VMEM),
        scratch_shapes=[
            pltpu.VMEM((len(phases), widest, rows, 128), jnp.float32),
            pltpu.SemaphoreType.DMA((len(phases), widest)),
            pltpu.SemaphoreType.DMA((len(phases), widest)),
        ],
        compiler_params=pltpu.CompilerParams(collective_id=collective_id, has_side_effects=True),
    )(values)


def gram_kernel(phases, x_ref, y_ref, o_ref, z_ref, *scratch):
    count = len(phases)
    recvs = scratch[: count - 1]
    sums = scratch[count - 1 : 2 * count - 3]
    full = scratch[2 * count - 3]
    rs_send, rs_recv, ag_send, ag_recv, side, side_send, side_recv = scratch[2 * count - 2 :]
    side_acc = y_ref[...]
    outer_own, _ = group_peer(*phases[0], 0)
    barrier = pltpu.get_barrier_semaphore()
    greeted = 0
    for axis, n, stride in phases:
        for k in range(1, n):
            _, peer = group_peer(axis, n, stride, k)
            pl.semaphore_signal(
                barrier, 1, device_id={axis: peer}, device_id_type=pl.DeviceIdType.MESH
            )
            greeted += 1
    pl.semaphore_wait(barrier, greeted)
    source = x_ref
    length = x_ref.shape[0]
    offset = outer_own * length
    for p, (axis, n, stride) in enumerate(phases):
        if p == 0:
            continue
        own, _ = group_peer(axis, n, stride, 0)
        part = length // n
        recv = recvs[p - 1]
        recv[0] = source[pl.ds(pl.multiple_of(own * part, 8), part)]
        copies = []
        if axis != "samp":
            side[p, 0] = side_acc
            for k in range(1, n):
                _, peer = group_peer(axis, n, stride, k)
                copy = pltpu.make_async_remote_copy(
                    src_ref=side.at[p, 0],
                    dst_ref=side.at[p, k],
                    send_sem=side_send.at[p, k],
                    recv_sem=side_recv.at[p, k],
                    device_id={axis: peer},
                    device_id_type=pl.DeviceIdType.MESH,
                )
                copy.start()
                copies.append(copy)
        for k in range(1, n):
            _, peer = group_peer(axis, n, stride, k)
            chunk = (own + k) % n
            copy = pltpu.make_async_remote_copy(
                src_ref=source.at[pl.ds(pl.multiple_of(chunk * part, 8), part)],
                dst_ref=recv.at[k],
                send_sem=rs_send.at[p, k],
                recv_sem=rs_recv.at[p, k],
                device_id={axis: peer},
                device_id_type=pl.DeviceIdType.MESH,
            )
            copy.start()
            copies.append(copy)
        for copy in copies:
            copy.wait()
        acc = recv[own % n]
        for j in range(1, n):
            acc = acc + recv[(own - j) % n]
        if axis != "samp":
            side_acc = side[p, own % n]
            for j in range(1, n):
                side_acc = side_acc + side[p, (own - j) % n]
        offset = offset + own * part
        length = part
        if p < count - 1:
            sums[p - 1][...] = acc
            source = sums[p - 1]
        else:
            full[pl.ds(pl.multiple_of(offset, 8), part)] = acc
    for p in reversed(range(count)):
        axis, n, stride = phases[p]
        own, _ = group_peer(axis, n, stride, 0)
        here = full.at[pl.ds(pl.multiple_of(offset, 8), length)]
        copies = []
        for k in range(1, n):
            _, peer = group_peer(axis, n, stride, k)
            copy = pltpu.make_async_remote_copy(
                src_ref=here,
                dst_ref=here,
                send_sem=ag_send.at[p, k],
                recv_sem=ag_recv.at[p, k],
                device_id={axis: peer},
                device_id_type=pl.DeviceIdType.MESH,
            )
            copy.start()
            copies.append(copy)
        for copy in copies:
            copy.wait()
        offset = offset - own * length
        length = length * n
    o_ref[...] = full[...]
    z_ref[...] = side_acc


def gram_sum(values, side_values, collective_id):
    phases = (("samp", lax.axis_size("samp"), 1),) + reduce_phases()
    rows = values.shape[0]
    widest = max(n for _, n, _ in phases)
    recvs, sums = [], []
    length = rows
    for p, (_, n, _) in enumerate(phases):
        if p == 0:
            continue
        length //= n
        recvs.append(pltpu.VMEM((n, length, 128), jnp.float32))
        if p < len(phases) - 1:
            sums.append(pltpu.VMEM((length, 128), jnp.float32))
    rows = rows * phases[0][1]
    semaphores = [pltpu.SemaphoreType.DMA((len(phases), widest)) for _ in range(4)]
    side_scratch = [
        pltpu.VMEM((len(phases), widest) + side_values.shape, jnp.float32),
        pltpu.SemaphoreType.DMA((len(phases), widest)),
        pltpu.SemaphoreType.DMA((len(phases), widest)),
    ]
    return pl.pallas_call(
        lambda *refs: gram_kernel(phases, *refs),
        out_shape=(
            jax.ShapeDtypeStruct((rows, 128), jnp.float32),
            jax.ShapeDtypeStruct(side_values.shape, jnp.float32),
        ),
        in_specs=[pl.BlockSpec(memory_space=pltpu.VMEM)] * 2,
        out_specs=(pl.BlockSpec(memory_space=pltpu.VMEM),) * 2,
        scratch_shapes=recvs + sums + [pltpu.VMEM((rows, 128), jnp.float32)] + semaphores + side_scratch,
        compiler_params=pltpu.CompilerParams(collective_id=collective_id, has_side_effects=True),
    )(values, side_values)


def halo_kernel(n_blk, n_leaf, x_ref, o_ref, land, send_sem, recv_sem):
    own_blk = lax.axis_index("blk")
    own_leaf = lax.axis_index("leaf")
    targets = []
    for d in (-1, 1):
        for leaf in range(n_leaf):
            targets.append(((own_blk + d + n_blk) % n_blk, leaf, (1 - d) * n_leaf + own_leaf))
    for k in range(1, n_leaf):
        targets.append((own_blk, (own_leaf + k) % n_leaf, n_leaf + own_leaf))
    barrier = pltpu.get_barrier_semaphore()
    for blk, leaf, _ in targets:
        pl.semaphore_signal(
            barrier,
            1,
            device_id={"blk": blk, "leaf": leaf},
            device_id_type=pl.DeviceIdType.MESH,
        )
    pl.semaphore_wait(barrier, len(targets))
    copies = []
    for i, (blk, leaf, segment) in enumerate(targets):
        copy = pltpu.make_async_remote_copy(
            src_ref=x_ref,
            dst_ref=land.at[segment],
            send_sem=send_sem.at[i],
            recv_sem=recv_sem.at[segment],
            device_id={"blk": blk, "leaf": leaf},
            device_id_type=pl.DeviceIdType.MESH,
        )
        copy.start()
        copies.append(copy)
    land[n_leaf + own_leaf] = x_ref[...]
    incoming = [((own_blk - 1 + n_blk) % n_blk, s, s) for s in range(n_leaf)]
    incoming += [((own_blk + 1) % n_blk, s, 2 * n_leaf + s) for s in range(n_leaf)]
    for k in range(1, n_leaf):
        leaf = (own_leaf + k) % n_leaf
        incoming.append((own_blk, leaf, n_leaf + leaf))
    for copy in copies:
        copy.wait_send()
    for blk, leaf, segment in incoming:
        pltpu.make_async_remote_copy(
            src_ref=x_ref,
            dst_ref=land.at[segment],
            send_sem=send_sem.at[0],
            recv_sem=recv_sem.at[segment],
            device_id={"blk": blk, "leaf": leaf},
            device_id_type=pl.DeviceIdType.MESH,
        ).wait_recv()
    o_ref[...] = land[...]


def halo_gather(values, collective_id):
    n_blk = lax.axis_size("blk")
    n_leaf = lax.axis_size("leaf")
    segments = 3 * n_leaf
    return pl.pallas_call(
        lambda *refs: halo_kernel(n_blk, n_leaf, *refs),
        out_shape=jax.ShapeDtypeStruct((segments,) + values.shape, jnp.float32),
        in_specs=[pl.BlockSpec(memory_space=pltpu.VMEM)],
        out_specs=pl.BlockSpec(memory_space=pltpu.VMEM),
        scratch_shapes=[
            pltpu.VMEM((segments,) + values.shape, jnp.float32),
            pltpu.SemaphoreType.DMA((segments,)),
            pltpu.SemaphoreType.DMA((segments,)),
        ],
        compiler_params=pltpu.CompilerParams(collective_id=collective_id, has_side_effects=True),
    )(values)


def blocked_factor(gram, block=128):
    count = gram.shape[0] // block
    eye = jnp.eye(block, dtype=jnp.float32)
    inverses, panels = [], []
    rest = gram
    for k in range(count):
        diagonal = lax.linalg.cholesky(rest[:block, :block])
        inverse = lax.linalg.triangular_solve(diagonal, eye, left_side=True, lower=True)
        inverses.append(inverse)
        if k < count - 1:
            panel = high_dot(rest[block:, :block], inverse.T)
            panels.append(panel)
            rest = rest[block:, block:] - high_dot(panel, panel.T)
    return inverses, panels


def blocked_solve(inverses, panels, values):
    block = inverses[0].shape[0]
    count = len(inverses)
    lower = []
    rest = values
    for k in range(count):
        part = high_dot(inverses[k], rest[:block])
        lower.append(part)
        if k < count - 1:
            rest = rest[block:] - high_dot(panels[k], part)
    upper = [None] * count
    for k in reversed(range(count)):
        rhs = lower[k]
        if k < count - 1:
            rhs = rhs - high_dot(panels[k].T, jnp.concatenate(upper[k + 1 :]))
        upper[k] = high_dot(inverses[k].T, rhs)
    return jnp.concatenate(upper)


def lower_solve(factor, values):
    return lax.linalg.triangular_solve(factor, values, left_side=True, lower=True)


def local(points, neighbors, omega, observed, prior_draws):
    blk_dev = neighbors.shape[0]
    cycle_count = lax.axis_size("blk")
    slab_blocks = blk_dev * lax.axis_size("leaf")
    period = 2.0 * cycle_count
    own_slab = lax.axis_index("blk")
    n_samp = lax.axis_size("samp")
    samp_idx = lax.axis_index("samp")
    usable = neighbors >= 0
    relative = jnp.mod(neighbors // slab_blocks - own_slab + 1, cycle_count)
    chosen = jnp.where(usable, relative * slab_blocks + jnp.mod(neighbors, slab_blocks), 0)
    usable_weight = usable.astype(jnp.float32)
    reach_blocks = halo_gather(points, 4)
    row_blocks = points.reshape(3, blk_dev, PB).transpose(1, 0, 2)

    segments = 3 * slab_blocks
    listed = jnp.zeros((segments,), jnp.float32).at[chosen[0]].max(usable_weight[0])
    kernel_tile = wendland(row_blocks[0], reach_blocks, period) * listed[:, None, None]

    def apply_kernel(values, wide=False):
        width = values.shape[0]
        if wide:
            slab_values = lax.all_gather(values, "leaf", axis=1, tiled=True)
            parts = (shifted(slab_values, 1), slab_values, shifted(slab_values, -1))
            out = None
            for i, part in enumerate(parts):
                tile = kernel_tile[i * slab_blocks : (i + 1) * slab_blocks]
                term = jnp.einsum(
                    "cnj,nij->ci",
                    part.reshape(width, slab_blocks, PB),
                    tile,
                    precision=lax.Precision.HIGHEST,
                )
                out = term if out is None else out + term
            return out
        reach = halo_gather(values, 6)
        return jnp.einsum("ncj,nij->ci", reach, kernel_tile, precision=lax.Precision.HIGHEST)

    def slot(x):
        zeros = jnp.zeros((n_samp,) + x.shape, x.dtype)
        return lax.dynamic_update_index_in_dim(zeros, x, samp_idx, 0)

    def unslot(xs):
        return lax.dynamic_index_in_dim(xs, samp_idx, 0, keepdims=False)

    def total_per_samp(values):
        return jax.tree.map(unslot, lax.psum(jax.tree.map(slot, values), ALL_AXES))

    sketch_rows = omega.shape[0]
    omega_rows = lax.dynamic_slice_in_dim(omega, samp_idx * (sketch_rows // n_samp), sketch_rows // n_samp)
    sketch_own = apply_kernel(omega_rows, wide=True) + sketch_shift * omega_rows
    sketch = lax.all_gather(sketch_own, "samp", axis=0, tiled=True)
    rhs = observed[None, :] - prior_draws
    joint_part = 0.5 * (high_dot(omega_rows, sketch.T) + high_dot(sketch_own, omega.T)) + high_dot(
        sketch_own, sketch.T
    )
    gram_rows = joint_part.shape[1]
    width = rhs.shape[0]
    rhs_proj = high_dot(sketch, rhs.T).reshape(gram_rows * width // 128, 128)
    joint_gram, rhs_proj = gram_sum(joint_part.reshape(-1, 128), rhs_proj, 2)
    joint_gram = joint_gram.reshape(gram_rows, gram_rows)
    rhs_proj = rhs_proj.reshape(gram_rows, width)

    inverses, panels = blocked_factor(joint_gram)

    def precond_from(vectors, projected):
        solved = blocked_solve(inverses, panels, projected)
        return (vectors - high_dot(solved.T, sketch)) / noise_variance, solved

    residual = rhs
    projected = rhs_proj
    precond, _ = precond_from(residual, projected)
    direction = precond
    weights = jnp.zeros_like(rhs)

    sketch_rows = sketch.shape[0]

    def pack_scalars(*vectors):
        rows = jnp.stack(vectors)
        return jnp.pad(rows, ((0, 8 - rows.shape[0]), (0, 128 - width)))

    image = apply_kernel(direction) + noise_variance * direction
    image_proj = high_dot(sketch, image.T).reshape(sketch_rows * width // 128, 128)
    packed = jnp.concatenate(
        [
            image_proj,
            pack_scalars(
                jnp.sum(residual * precond, axis=1),
                jnp.sum(direction * image, axis=1),
                jnp.sum(residual * residual, axis=1),
                jnp.sum(residual * image, axis=1),
                jnp.sum(image * image, axis=1),
            ),
        ]
    )
    packed = group_sum(packed, 0)
    image_proj = packed[:-8].reshape(sketch_rows, width)
    inner_now = packed[-8, :width]
    curvature = packed[-7, :width]
    residual_sq, residual_image, image_sq = packed[-6, :width], packed[-5, :width], packed[-4, :width]
    step_size = inner_now / curvature
    weights = weights + step_size[:, None] * direction
    residual = residual - step_size[:, None] * image
    projected = projected - step_size[None, :] * image_proj
    precond, solved = precond_from(residual, projected)
    residual_sq = residual_sq - 2.0 * step_size * residual_image + step_size * step_size * image_sq
    inner_next = (residual_sq - jnp.sum(projected * solved, axis=0)) / noise_variance
    direction = precond + (inner_next / inner_now)[:, None] * direction
    inner_now = inner_next

    image = apply_kernel(direction) + noise_variance * direction
    curvature = group_sum(pack_scalars(jnp.sum(direction * image, axis=1)), 1)[0, :width]
    step_size = inner_now / curvature
    weights = weights + step_size[:, None] * direction
    residual = residual - step_size[:, None] * image
    return (weights, residual)


def solution(mesh):
    in_specs = (
        P(None, ("blk", "leaf")),
        P(("blk", "leaf"), None),
        P(None, ("blk", "leaf")),
        P(("blk", "leaf")),
        P("samp", ("blk", "leaf")),
    )
    out_specs = (P("samp", ("blk", "leaf")), P("samp", ("blk", "leaf")))
    return jax.shard_map(local, mesh=mesh, in_specs=in_specs, out_specs=out_specs, check_vma=False)
```

```python
import jax
import jax.numpy as jnp
from jax import lax
from jax.sharding import PartitionSpec as P
from jax.experimental import pallas as pl
from jax.experimental.pallas import tpu as pltpu

PB = 256
ITERS = 2


support_radius = 0.8
noise_variance = 1.0
sketch_shift = 1.0

ALL_AXES = ("blk", "leaf", "samp")


def shifted_2(block, axis, distance):
    devices = range(lax.axis_size(axis))
    route = [((i - distance) % len(devices), i) for i in devices]
    return lax.ppermute(block, axis, route)


def wendland(row_points, column_points, period):
    offset = row_points[None, :, :, None] - column_points[:, :, None, :]
    half_period = 0.5 * period
    along_x = jnp.mod(offset[:, 0] + half_period, period) - half_period
    squared = along_x * along_x + offset[:, 1] * offset[:, 1] + offset[:, 2] * offset[:, 2]
    radius = jnp.sqrt(squared) / support_radius
    remain = jnp.maximum(1.0 - radius, 0.0)
    return remain**4 * (4.0 * radius + 1.0)


def high_dot(left, right):
    return jnp.dot(left, right, precision=lax.Precision.HIGHEST, preferred_element_type=jnp.float32)


def shifted(values, offset_by):
    return shifted_2(values, "blk", offset_by)


def beside_all(values):
    slab_values = lax.all_gather(values, "leaf", axis=1, tiled=True)
    return jnp.concatenate([shifted(slab_values, 1), slab_values, shifted(slab_values, -1)], axis=1)


def blk_split(n_blk):
    if n_blk % 8 == 0 and n_blk > 8:
        return (8, n_blk // 8)
    return (n_blk, 1)


def reduce_phases():
    inner, outer = blk_split(lax.axis_size("blk"))
    phases = [("leaf", lax.axis_size("leaf"), 1), ("blk", inner, 1)]
    if outer > 1:
        phases.append(("blk", outer, inner))
    return tuple(p for p in phases if p[1] > 1)


def group_peer(axis, n, stride, k):
    idx = lax.axis_index(axis)
    own = (idx // stride) % n
    return own, idx + ((own + k) % n - own) * stride


def sum_kernel(phases, x_ref, o_ref, recv, send_sem, recv_sem):
    barrier = pltpu.get_barrier_semaphore()
    greeted = 0
    for axis, n, stride in phases:
        for k in range(1, n):
            _, peer = group_peer(axis, n, stride, k)
            pl.semaphore_signal(
                barrier, 1, device_id={axis: peer}, device_id_type=pl.DeviceIdType.MESH
            )
            greeted += 1
    pl.semaphore_wait(barrier, greeted)
    acc = x_ref[...]
    for p, (axis, n, stride) in enumerate(phases):
        recv[p, 0] = acc
        copies = []
        for k in range(1, n):
            own, peer = group_peer(axis, n, stride, k)
            copy = pltpu.make_async_remote_copy(
                src_ref=x_ref if p == 0 else recv.at[p, 0],
                dst_ref=recv.at[p, k],
                send_sem=send_sem.at[p, k],
                recv_sem=recv_sem.at[p, k],
                device_id={axis: peer},
                device_id_type=pl.DeviceIdType.MESH,
            )
            copy.start()
            copies.append(copy)
        for copy in copies:
            copy.wait()
        own, _ = group_peer(axis, n, stride, 0)
        terms = [recv[p, (own - j) % n] for j in range(n)]
        acc = terms[0]
        for term in terms[1:]:
            acc = acc + term
    o_ref[...] = acc


def group_sum(values, collective_id):
    phases = reduce_phases()
    rows = values.shape[0]
    widest = max(n for _, n, _ in phases)
    return pl.pallas_call(
        lambda *refs: sum_kernel(phases, *refs),
        out_shape=jax.ShapeDtypeStruct(values.shape, jnp.float32),
        in_specs=[pl.BlockSpec(memory_space=pltpu.VMEM)],
        out_specs=pl.BlockSpec(memory_space=pltpu.VMEM),
        scratch_shapes=[
            pltpu.VMEM((len(phases), widest, rows, 128), jnp.float32),
            pltpu.SemaphoreType.DMA((len(phases), widest)),
            pltpu.SemaphoreType.DMA((len(phases), widest)),
        ],
        compiler_params=pltpu.CompilerParams(collective_id=collective_id, has_side_effects=True),
    )(values)


def gram_kernel(phases, x_ref, y_ref, o_ref, z_ref, *scratch):
    count = len(phases)
    recvs = scratch[: count - 1]
    sums = scratch[count - 1 : 2 * count - 3]
    full = scratch[2 * count - 3]
    rs_send, rs_recv, ag_send, ag_recv, side, side_send, side_recv = scratch[2 * count - 2 :]
    side_acc = y_ref[...]
    outer_own, _ = group_peer(*phases[0], 0)
    barrier = pltpu.get_barrier_semaphore()
    greeted = 0
    for axis, n, stride in phases:
        for k in range(1, n):
            _, peer = group_peer(axis, n, stride, k)
            pl.semaphore_signal(
                barrier, 1, device_id={axis: peer}, device_id_type=pl.DeviceIdType.MESH
            )
            greeted += 1
    pl.semaphore_wait(barrier, greeted)
    source = x_ref
    length = x_ref.shape[0]
    offset = outer_own * length
    for p, (axis, n, stride) in enumerate(phases):
        if p == 0:
            continue
        own, _ = group_peer(axis, n, stride, 0)
        part = length // n
        recv = recvs[p - 1]
        recv[0] = source[pl.ds(pl.multiple_of(own * part, 8), part)]
        copies = []
        if axis != "samp":
            side[p, 0] = side_acc
            for k in range(1, n):
                _, peer = group_peer(axis, n, stride, k)
                copy = pltpu.make_async_remote_copy(
                    src_ref=side.at[p, 0],
                    dst_ref=side.at[p, k],
                    send_sem=side_send.at[p, k],
                    recv_sem=side_recv.at[p, k],
                    device_id={axis: peer},
                    device_id_type=pl.DeviceIdType.MESH,
                )
                copy.start()
                copies.append(copy)
        for k in range(1, n):
            _, peer = group_peer(axis, n, stride, k)
            chunk = (own + k) % n
            copy = pltpu.make_async_remote_copy(
                src_ref=source.at[pl.ds(pl.multiple_of(chunk * part, 8), part)],
                dst_ref=recv.at[k],
                send_sem=rs_send.at[p, k],
                recv_sem=rs_recv.at[p, k],
                device_id={axis: peer},
                device_id_type=pl.DeviceIdType.MESH,
            )
            copy.start()
            copies.append(copy)
        for copy in copies:
            copy.wait()
        acc = recv[own % n]
        for j in range(1, n):
            acc = acc + recv[(own - j) % n]
        if axis != "samp":
            side_acc = side[p, own % n]
            for j in range(1, n):
                side_acc = side_acc + side[p, (own - j) % n]
        offset = offset + own * part
        length = part
        if p < count - 1:
            sums[p - 1][...] = acc
            source = sums[p - 1]
        else:
            full[pl.ds(pl.multiple_of(offset, 8), part)] = acc
    for p in reversed(range(count)):
        axis, n, stride = phases[p]
        own, _ = group_peer(axis, n, stride, 0)
        here = full.at[pl.ds(pl.multiple_of(offset, 8), length)]
        copies = []
        for k in range(1, n):
            _, peer = group_peer(axis, n, stride, k)
            copy = pltpu.make_async_remote_copy(
                src_ref=here,
                dst_ref=here,
                send_sem=ag_send.at[p, k],
                recv_sem=ag_recv.at[p, k],
                device_id={axis: peer},
                device_id_type=pl.DeviceIdType.MESH,
            )
            copy.start()
            copies.append(copy)
        for copy in copies:
            copy.wait()
        offset = offset - own * length
        length = length * n
    o_ref[...] = full[...]
    z_ref[...] = side_acc


def gram_sum(values, side_values, collective_id):
    phases = (("samp", lax.axis_size("samp"), 1),) + reduce_phases()
    rows = values.shape[0]
    widest = max(n for _, n, _ in phases)
    recvs, sums = [], []
    length = rows
    for p, (_, n, _) in enumerate(phases):
        if p == 0:
            continue
        length //= n
        recvs.append(pltpu.VMEM((n, length, 128), jnp.float32))
        if p < len(phases) - 1:
            sums.append(pltpu.VMEM((length, 128), jnp.float32))
    rows = rows * phases[0][1]
    semaphores = [pltpu.SemaphoreType.DMA((len(phases), widest)) for _ in range(4)]
    side_scratch = [
        pltpu.VMEM((len(phases), widest) + side_values.shape, jnp.float32),
        pltpu.SemaphoreType.DMA((len(phases), widest)),
        pltpu.SemaphoreType.DMA((len(phases), widest)),
    ]
    return pl.pallas_call(
        lambda *refs: gram_kernel(phases, *refs),
        out_shape=(
            jax.ShapeDtypeStruct((rows, 128), jnp.float32),
            jax.ShapeDtypeStruct(side_values.shape, jnp.float32),
        ),
        in_specs=[pl.BlockSpec(memory_space=pltpu.VMEM)] * 2,
        out_specs=(pl.BlockSpec(memory_space=pltpu.VMEM),) * 2,
        scratch_shapes=recvs + sums + [pltpu.VMEM((rows, 128), jnp.float32)] + semaphores + side_scratch,
        compiler_params=pltpu.CompilerParams(collective_id=collective_id, has_side_effects=True),
    )(values, side_values)


def halo_kernel(n_blk, n_leaf, x_ref, o_ref, land, send_sem, recv_sem):
    own_blk = lax.axis_index("blk")
    own_leaf = lax.axis_index("leaf")
    targets = []
    for d in (-1, 1):
        for leaf in range(n_leaf):
            targets.append(((own_blk + d + n_blk) % n_blk, leaf, (1 - d) * n_leaf + own_leaf))
    for k in range(1, n_leaf):
        targets.append((own_blk, (own_leaf + k) % n_leaf, n_leaf + own_leaf))
    barrier = pltpu.get_barrier_semaphore()
    for blk, leaf, _ in targets:
        pl.semaphore_signal(
            barrier,
            1,
            device_id={"blk": blk, "leaf": leaf},
            device_id_type=pl.DeviceIdType.MESH,
        )
    pl.semaphore_wait(barrier, len(targets))
    copies = []
    for i, (blk, leaf, segment) in enumerate(targets):
        copy = pltpu.make_async_remote_copy(
            src_ref=x_ref,
            dst_ref=land.at[segment],
            send_sem=send_sem.at[i],
            recv_sem=recv_sem.at[segment],
            device_id={"blk": blk, "leaf": leaf},
            device_id_type=pl.DeviceIdType.MESH,
        )
        copy.start()
        copies.append(copy)
    land[n_leaf + own_leaf] = x_ref[...]
    incoming = [((own_blk - 1 + n_blk) % n_blk, s, s) for s in range(n_leaf)]
    incoming += [((own_blk + 1) % n_blk, s, 2 * n_leaf + s) for s in range(n_leaf)]
    for k in range(1, n_leaf):
        leaf = (own_leaf + k) % n_leaf
        incoming.append((own_blk, leaf, n_leaf + leaf))
    for copy in copies:
        copy.wait_send()
    for blk, leaf, segment in incoming:
        pltpu.make_async_remote_copy(
            src_ref=x_ref,
            dst_ref=land.at[segment],
            send_sem=send_sem.at[0],
            recv_sem=recv_sem.at[segment],
            device_id={"blk": blk, "leaf": leaf},
            device_id_type=pl.DeviceIdType.MESH,
        ).wait_recv()
    o_ref[...] = land[...]


def halo_gather(values, collective_id):
    n_blk = lax.axis_size("blk")
    n_leaf = lax.axis_size("leaf")
    segments = 3 * n_leaf
    return pl.pallas_call(
        lambda *refs: halo_kernel(n_blk, n_leaf, *refs),
        out_shape=jax.ShapeDtypeStruct((segments,) + values.shape, jnp.float32),
        in_specs=[pl.BlockSpec(memory_space=pltpu.VMEM)],
        out_specs=pl.BlockSpec(memory_space=pltpu.VMEM),
        scratch_shapes=[
            pltpu.VMEM((segments,) + values.shape, jnp.float32),
            pltpu.SemaphoreType.DMA((segments,)),
            pltpu.SemaphoreType.DMA((segments,)),
        ],
        compiler_params=pltpu.CompilerParams(collective_id=collective_id, has_side_effects=True),
    )(values)


def blocked_factor(gram, block=128):
    count = gram.shape[0] // block
    eye = jnp.eye(block, dtype=jnp.float32)
    inverses, panels = [], []
    rest = gram
    for k in range(count):
        diagonal = lax.linalg.cholesky(rest[:block, :block])
        inverse = lax.linalg.triangular_solve(diagonal, eye, left_side=True, lower=True)
        inverses.append(inverse)
        if k < count - 1:
            panel = high_dot(rest[block:, :block], inverse.T)
            panels.append(panel)
            rest = rest[block:, block:] - high_dot(panel, panel.T)
    return inverses, panels


def blocked_solve(inverses, panels, values):
    block = inverses[0].shape[0]
    count = len(inverses)
    lower = []
    rest = values
    for k in range(count):
        part = high_dot(inverses[k], rest[:block])
        lower.append(part)
        if k < count - 1:
            rest = rest[block:] - high_dot(panels[k], part)
    upper = [None] * count
    for k in reversed(range(count)):
        rhs = lower[k]
        if k < count - 1:
            rhs = rhs - high_dot(panels[k].T, jnp.concatenate(upper[k + 1 :]))
        upper[k] = high_dot(inverses[k].T, rhs)
    return jnp.concatenate(upper)


def lower_solve(factor, values):
    return lax.linalg.triangular_solve(factor, values, left_side=True, lower=True)


def local(points, neighbors, omega, observed, prior_draws):
    blk_dev = neighbors.shape[0]
    cycle_count = lax.axis_size("blk")
    slab_blocks = blk_dev * lax.axis_size("leaf")
    period = 2.0 * cycle_count
    own_slab = lax.axis_index("blk")
    n_samp = lax.axis_size("samp")
    samp_idx = lax.axis_index("samp")
    usable = neighbors >= 0
    relative = jnp.mod(neighbors // slab_blocks - own_slab + 1, cycle_count)
    chosen = jnp.where(usable, relative * slab_blocks + jnp.mod(neighbors, slab_blocks), 0)
    usable_weight = usable.astype(jnp.float32)
    reach_blocks = halo_gather(points, 4)
    row_blocks = points.reshape(3, blk_dev, PB).transpose(1, 0, 2)

    segments = 3 * slab_blocks
    listed = jnp.zeros((segments,), jnp.float32).at[chosen[0]].max(usable_weight[0])
    kernel_tile = wendland(row_blocks[0], reach_blocks, period) * listed[:, None, None]

    flat_tile = kernel_tile.transpose(0, 2, 1).reshape(-1, PB)

    def apply_kernel(values, wide=False):
        width = values.shape[0]
        if wide:
            slab_values = lax.all_gather(values, "leaf", axis=1, tiled=True)
            parts = (shifted(slab_values, 1), slab_values, shifted(slab_values, -1))
            out = None
            for i, part in enumerate(parts):
                tile = kernel_tile[i * slab_blocks : (i + 1) * slab_blocks]
                term = jnp.einsum(
                    "cnj,nij->ci",
                    part.reshape(width, slab_blocks, PB),
                    tile,
                    precision=lax.Precision.HIGHEST,
                )
                out = term if out is None else out + term
            return out
        reach = halo_gather(values, 6)
        return high_dot(reach.transpose(1, 0, 2).reshape(width, -1), flat_tile)

    def slot(x):
        zeros = jnp.zeros((n_samp,) + x.shape, x.dtype)
        return lax.dynamic_update_index_in_dim(zeros, x, samp_idx, 0)

    def unslot(xs):
        return lax.dynamic_index_in_dim(xs, samp_idx, 0, keepdims=False)

    def total_per_samp(values):
        return jax.tree.map(unslot, lax.psum(jax.tree.map(slot, values), ALL_AXES))

    sketch_rows = omega.shape[0]
    omega_rows = lax.dynamic_slice_in_dim(omega, samp_idx * (sketch_rows // n_samp), sketch_rows // n_samp)
    sketch_own = apply_kernel(omega_rows, wide=True) + sketch_shift * omega_rows
    sketch = lax.all_gather(sketch_own, "samp", axis=0, tiled=True)
    rhs = observed[None, :] - prior_draws
    joint_part = 0.5 * (high_dot(omega_rows, sketch.T) + high_dot(sketch_own, omega.T)) + high_dot(
        sketch_own, sketch.T
    )
    gram_rows = joint_part.shape[1]
    width = rhs.shape[0]
    rhs_proj = high_dot(sketch, rhs.T).reshape(gram_rows * width // 128, 128)
    joint_gram, rhs_proj = gram_sum(joint_part.reshape(-1, 128), rhs_proj, 2)
    joint_gram = joint_gram.reshape(gram_rows, gram_rows)
    rhs_proj = rhs_proj.reshape(gram_rows, width)

    inverses, panels = blocked_factor(joint_gram)

    def precond_from(vectors, projected):
        solved = blocked_solve(inverses, panels, projected)
        return (vectors - high_dot(solved.T, sketch)) / noise_variance, solved

    residual = rhs
    projected = rhs_proj
    precond, _ = precond_from(residual, projected)
    direction = precond
    weights = jnp.zeros_like(rhs)

    sketch_rows = sketch.shape[0]

    def pack_scalars(*vectors):
        rows = jnp.stack(vectors)
        return jnp.pad(rows, ((0, 8 - rows.shape[0]), (0, 128 - width)))

    image = apply_kernel(direction) + noise_variance * direction
    image_proj = high_dot(sketch, image.T).reshape(sketch_rows * width // 128, 128)
    packed = jnp.concatenate(
        [
            image_proj,
            pack_scalars(
                jnp.sum(residual * precond, axis=1),
                jnp.sum(direction * image, axis=1),
                jnp.sum(residual * residual, axis=1),
                jnp.sum(residual * image, axis=1),
                jnp.sum(image * image, axis=1),
            ),
        ]
    )
    packed = group_sum(packed, 0)
    image_proj = packed[:-8].reshape(sketch_rows, width)
    inner_now = packed[-8, :width]
    curvature = packed[-7, :width]
    residual_sq, residual_image, image_sq = packed[-6, :width], packed[-5, :width], packed[-4, :width]
    step_size = inner_now / curvature
    weights = weights + step_size[:, None] * direction
    residual = residual - step_size[:, None] * image
    projected = projected - step_size[None, :] * image_proj
    precond, solved = precond_from(residual, projected)
    residual_sq = residual_sq - 2.0 * step_size * residual_image + step_size * step_size * image_sq
    inner_next = (residual_sq - jnp.sum(projected * solved, axis=0)) / noise_variance
    direction = precond + (inner_next / inner_now)[:, None] * direction
    inner_now = inner_next

    image = apply_kernel(direction) + noise_variance * direction
    curvature = group_sum(pack_scalars(jnp.sum(direction * image, axis=1)), 1)[0, :width]
    step_size = inner_now / curvature
    weights = weights + step_size[:, None] * direction
    residual = residual - step_size[:, None] * image
    return (weights, residual)


def solution(mesh):
    in_specs = (
        P(None, ("blk", "leaf")),
        P(("blk", "leaf"), None),
        P(None, ("blk", "leaf")),
        P(("blk", "leaf")),
        P("samp", ("blk", "leaf")),
    )
    out_specs = (P("samp", ("blk", "leaf")), P("samp", ("blk", "leaf")))
    return jax.shard_map(local, mesh=mesh, in_specs=in_specs, out_specs=out_specs, check_vma=False)
```

```python
import jax
import jax.numpy as jnp
from jax import lax
from jax.sharding import PartitionSpec as P
from jax.experimental import pallas as pl
from jax.experimental.pallas import tpu as pltpu

PB = 256
ITERS = 2


support_radius = 0.8
noise_variance = 1.0
sketch_shift = 1.0

ALL_AXES = ("blk", "leaf", "samp")


def shifted_2(block, axis, distance):
    devices = range(lax.axis_size(axis))
    route = [((i - distance) % len(devices), i) for i in devices]
    return lax.ppermute(block, axis, route)


def wendland(row_points, column_points, period):
    offset = row_points[None, :, :, None] - column_points[:, :, None, :]
    half_period = 0.5 * period
    along_x = jnp.mod(offset[:, 0] + half_period, period) - half_period
    squared = along_x * along_x + offset[:, 1] * offset[:, 1] + offset[:, 2] * offset[:, 2]
    radius = jnp.sqrt(squared) / support_radius
    remain = jnp.maximum(1.0 - radius, 0.0)
    return remain**4 * (4.0 * radius + 1.0)


def high_dot(left, right):
    return jnp.dot(left, right, precision=lax.Precision.HIGHEST, preferred_element_type=jnp.float32)


def shifted(values, offset_by):
    return shifted_2(values, "blk", offset_by)


def beside_all(values):
    slab_values = lax.all_gather(values, "leaf", axis=1, tiled=True)
    return jnp.concatenate([shifted(slab_values, 1), slab_values, shifted(slab_values, -1)], axis=1)


def blk_split(n_blk):
    if n_blk % 8 == 0 and n_blk > 8:
        return (8, n_blk // 8)
    return (n_blk, 1)


def reduce_phases():
    inner, outer = blk_split(lax.axis_size("blk"))
    phases = [("leaf", lax.axis_size("leaf"), 1), ("blk", inner, 1)]
    if outer > 1:
        phases.append(("blk", outer, inner))
    return tuple(p for p in phases if p[1] > 1)


def group_peer(axis, n, stride, k):
    idx = lax.axis_index(axis)
    own = (idx // stride) % n
    return own, idx + ((own + k) % n - own) * stride


def sum_kernel(phases, x_ref, o_ref, recv, send_sem, recv_sem):
    barrier = pltpu.get_barrier_semaphore()
    greeted = 0
    for axis, n, stride in phases:
        for k in range(1, n):
            _, peer = group_peer(axis, n, stride, k)
            pl.semaphore_signal(
                barrier, 1, device_id={axis: peer}, device_id_type=pl.DeviceIdType.MESH
            )
            greeted += 1
    pl.semaphore_wait(barrier, greeted)
    acc = x_ref[...]
    for p, (axis, n, stride) in enumerate(phases):
        recv[p, 0] = acc
        copies = []
        for k in range(1, n):
            own, peer = group_peer(axis, n, stride, k)
            copy = pltpu.make_async_remote_copy(
                src_ref=x_ref if p == 0 else recv.at[p, 0],
                dst_ref=recv.at[p, k],
                send_sem=send_sem.at[p, k],
                recv_sem=recv_sem.at[p, k],
                device_id={axis: peer},
                device_id_type=pl.DeviceIdType.MESH,
            )
            copy.start()
            copies.append(copy)
        for copy in copies:
            copy.wait()
        own, _ = group_peer(axis, n, stride, 0)
        terms = [recv[p, (own - j) % n] for j in range(n)]
        acc = terms[0]
        for term in terms[1:]:
            acc = acc + term
    o_ref[...] = acc


def group_sum(values, collective_id):
    phases = reduce_phases()
    rows = values.shape[0]
    widest = max(n for _, n, _ in phases)
    return pl.pallas_call(
        lambda *refs: sum_kernel(phases, *refs),
        out_shape=jax.ShapeDtypeStruct(values.shape, jnp.float32),
        in_specs=[pl.BlockSpec(memory_space=pltpu.VMEM)],
        out_specs=pl.BlockSpec(memory_space=pltpu.VMEM),
        scratch_shapes=[
            pltpu.VMEM((len(phases), widest, rows, 128), jnp.float32),
            pltpu.SemaphoreType.DMA((len(phases), widest)),
            pltpu.SemaphoreType.DMA((len(phases), widest)),
        ],
        compiler_params=pltpu.CompilerParams(collective_id=collective_id, has_side_effects=True),
    )(values)


def gram_kernel(phases, x_ref, y_ref, o_ref, z_ref, *scratch):
    count = len(phases)
    recvs = scratch[: count - 1]
    sums = scratch[count - 1 : 2 * count - 3]
    full = scratch[2 * count - 3]
    rs_send, rs_recv, ag_send, ag_recv, side, side_send, side_recv = scratch[2 * count - 2 :]
    side_acc = y_ref[...]
    outer_own, _ = group_peer(*phases[0], 0)
    barrier = pltpu.get_barrier_semaphore()
    greeted = 0
    for axis, n, stride in phases:
        for k in range(1, n):
            _, peer = group_peer(axis, n, stride, k)
            pl.semaphore_signal(
                barrier, 1, device_id={axis: peer}, device_id_type=pl.DeviceIdType.MESH
            )
            greeted += 1
    pl.semaphore_wait(barrier, greeted)
    source = x_ref
    length = x_ref.shape[0]
    offset = outer_own * length
    for p, (axis, n, stride) in enumerate(phases):
        if p == 0:
            continue
        own, _ = group_peer(axis, n, stride, 0)
        part = length // n
        recv = recvs[p - 1]
        recv[0] = source[pl.ds(pl.multiple_of(own * part, 8), part)]
        copies = []
        if axis != "samp":
            side[p, 0] = side_acc
            for k in range(1, n):
                _, peer = group_peer(axis, n, stride, k)
                copy = pltpu.make_async_remote_copy(
                    src_ref=side.at[p, 0],
                    dst_ref=side.at[p, k],
                    send_sem=side_send.at[p, k],
                    recv_sem=side_recv.at[p, k],
                    device_id={axis: peer},
                    device_id_type=pl.DeviceIdType.MESH,
                )
                copy.start()
                copies.append(copy)
        for k in range(1, n):
            _, peer = group_peer(axis, n, stride, k)
            chunk = (own + k) % n
            copy = pltpu.make_async_remote_copy(
                src_ref=source.at[pl.ds(pl.multiple_of(chunk * part, 8), part)],
                dst_ref=recv.at[k],
                send_sem=rs_send.at[p, k],
                recv_sem=rs_recv.at[p, k],
                device_id={axis: peer},
                device_id_type=pl.DeviceIdType.MESH,
            )
            copy.start()
            copies.append(copy)
        for copy in copies:
            copy.wait()
        acc = recv[own % n]
        for j in range(1, n):
            acc = acc + recv[(own - j) % n]
        if axis != "samp":
            side_acc = side[p, own % n]
            for j in range(1, n):
                side_acc = side_acc + side[p, (own - j) % n]
        offset = offset + own * part
        length = part
        if p < count - 1:
            sums[p - 1][...] = acc
            source = sums[p - 1]
        else:
            full[pl.ds(pl.multiple_of(offset, 8), part)] = acc
    for p in reversed(range(count)):
        axis, n, stride = phases[p]
        own, _ = group_peer(axis, n, stride, 0)
        here = full.at[pl.ds(pl.multiple_of(offset, 8), length)]
        copies = []
        for k in range(1, n):
            _, peer = group_peer(axis, n, stride, k)
            copy = pltpu.make_async_remote_copy(
                src_ref=here,
                dst_ref=here,
                send_sem=ag_send.at[p, k],
                recv_sem=ag_recv.at[p, k],
                device_id={axis: peer},
                device_id_type=pl.DeviceIdType.MESH,
            )
            copy.start()
            copies.append(copy)
        for copy in copies:
            copy.wait()
        offset = offset - own * length
        length = length * n
    o_ref[...] = full[...]
    z_ref[...] = side_acc


def gram_sum(values, side_values, collective_id):
    phases = (("samp", lax.axis_size("samp"), 1),) + reduce_phases()
    rows = values.shape[0]
    widest = max(n for _, n, _ in phases)
    recvs, sums = [], []
    length = rows
    for p, (_, n, _) in enumerate(phases):
        if p == 0:
            continue
        length //= n
        recvs.append(pltpu.VMEM((n, length, 128), jnp.float32))
        if p < len(phases) - 1:
            sums.append(pltpu.VMEM((length, 128), jnp.float32))
    rows = rows * phases[0][1]
    semaphores = [pltpu.SemaphoreType.DMA((len(phases), widest)) for _ in range(4)]
    side_scratch = [
        pltpu.VMEM((len(phases), widest) + side_values.shape, jnp.float32),
        pltpu.SemaphoreType.DMA((len(phases), widest)),
        pltpu.SemaphoreType.DMA((len(phases), widest)),
    ]
    return pl.pallas_call(
        lambda *refs: gram_kernel(phases, *refs),
        out_shape=(
            jax.ShapeDtypeStruct((rows, 128), jnp.float32),
            jax.ShapeDtypeStruct(side_values.shape, jnp.float32),
        ),
        in_specs=[pl.BlockSpec(memory_space=pltpu.VMEM)] * 2,
        out_specs=(pl.BlockSpec(memory_space=pltpu.VMEM),) * 2,
        scratch_shapes=recvs + sums + [pltpu.VMEM((rows, 128), jnp.float32)] + semaphores + side_scratch,
        compiler_params=pltpu.CompilerParams(collective_id=collective_id, has_side_effects=True),
    )(values, side_values)


def halo_kernel(n_blk, n_leaf, wide, x_ref, o_ref, land, send_sem, recv_sem):
    own_blk = lax.axis_index("blk")
    own_leaf = lax.axis_index("leaf")
    centre = n_leaf if wide else 0
    targets = []
    for d in (-1, 1) if wide else ():
        for leaf in range(n_leaf):
            targets.append(((own_blk + d + n_blk) % n_blk, leaf, (1 - d) * n_leaf + own_leaf))
    for k in range(1, n_leaf):
        targets.append((own_blk, (own_leaf + k) % n_leaf, centre + own_leaf))
    barrier = pltpu.get_barrier_semaphore()
    for blk, leaf, _ in targets:
        pl.semaphore_signal(
            barrier,
            1,
            device_id={"blk": blk, "leaf": leaf},
            device_id_type=pl.DeviceIdType.MESH,
        )
    pl.semaphore_wait(barrier, len(targets))
    copies = []
    for i, (blk, leaf, segment) in enumerate(targets):
        copy = pltpu.make_async_remote_copy(
            src_ref=x_ref,
            dst_ref=land.at[segment],
            send_sem=send_sem.at[i],
            recv_sem=recv_sem.at[segment],
            device_id={"blk": blk, "leaf": leaf},
            device_id_type=pl.DeviceIdType.MESH,
        )
        copy.start()
        copies.append(copy)
    land[centre + own_leaf] = x_ref[...]
    incoming = []
    if wide:
        incoming += [((own_blk - 1 + n_blk) % n_blk, s, s) for s in range(n_leaf)]
        incoming += [((own_blk + 1) % n_blk, s, 2 * n_leaf + s) for s in range(n_leaf)]
    for k in range(1, n_leaf):
        leaf = (own_leaf + k) % n_leaf
        incoming.append((own_blk, leaf, centre + leaf))
    for copy in copies:
        copy.wait_send()
    for blk, leaf, segment in incoming:
        pltpu.make_async_remote_copy(
            src_ref=x_ref,
            dst_ref=land.at[segment],
            send_sem=send_sem.at[0],
            recv_sem=recv_sem.at[segment],
            device_id={"blk": blk, "leaf": leaf},
            device_id_type=pl.DeviceIdType.MESH,
        ).wait_recv()
    o_ref[...] = land[...]


def halo_gather(values, collective_id, wide=True):
    n_blk = lax.axis_size("blk")
    n_leaf = lax.axis_size("leaf")
    segments = (3 if wide else 1) * n_leaf
    return pl.pallas_call(
        lambda *refs: halo_kernel(n_blk, n_leaf, wide, *refs),
        out_shape=jax.ShapeDtypeStruct((segments,) + values.shape, jnp.float32),
        in_specs=[pl.BlockSpec(memory_space=pltpu.VMEM)],
        out_specs=pl.BlockSpec(memory_space=pltpu.VMEM),
        scratch_shapes=[
            pltpu.VMEM((segments,) + values.shape, jnp.float32),
            pltpu.SemaphoreType.DMA((segments,)),
            pltpu.SemaphoreType.DMA((segments,)),
        ],
        compiler_params=pltpu.CompilerParams(collective_id=collective_id, has_side_effects=True),
    )(values)


def blocked_factor(gram, block=128):
    count = gram.shape[0] // block
    eye = jnp.eye(block, dtype=jnp.float32)
    inverses, panels = [], []
    rest = gram
    for k in range(count):
        diagonal = lax.linalg.cholesky(rest[:block, :block])
        inverse = lax.linalg.triangular_solve(diagonal, eye, left_side=True, lower=True)
        inverses.append(inverse)
        if k < count - 1:
            panel = high_dot(rest[block:, :block], inverse.T)
            panels.append(panel)
            rest = rest[block:, block:] - high_dot(panel, panel.T)
    return inverses, panels


def blocked_solve(inverses, panels, values):
    block = inverses[0].shape[0]
    count = len(inverses)
    lower = []
    rest = values
    for k in range(count):
        part = high_dot(inverses[k], rest[:block])
        lower.append(part)
        if k < count - 1:
            rest = rest[block:] - high_dot(panels[k], part)
    upper = [None] * count
    for k in reversed(range(count)):
        rhs = lower[k]
        if k < count - 1:
            rhs = rhs - high_dot(panels[k].T, jnp.concatenate(upper[k + 1 :]))
        upper[k] = high_dot(inverses[k].T, rhs)
    return jnp.concatenate(upper)


def lower_solve(factor, values):
    return lax.linalg.triangular_solve(factor, values, left_side=True, lower=True)


def local(points, neighbors, omega, observed, prior_draws):
    blk_dev = neighbors.shape[0]
    cycle_count = lax.axis_size("blk")
    slab_blocks = blk_dev * lax.axis_size("leaf")
    period = 2.0 * cycle_count
    own_slab = lax.axis_index("blk")
    n_samp = lax.axis_size("samp")
    samp_idx = lax.axis_index("samp")
    usable = neighbors >= 0
    relative = jnp.mod(neighbors // slab_blocks - own_slab + 1, cycle_count)
    chosen = jnp.where(usable, relative * slab_blocks + jnp.mod(neighbors, slab_blocks), 0)
    usable_weight = usable.astype(jnp.float32)
    reach_blocks = halo_gather(points, 4)
    row_blocks = points.reshape(3, blk_dev, PB).transpose(1, 0, 2)

    segments = 3 * slab_blocks
    listed = jnp.zeros((segments,), jnp.float32).at[chosen[0]].max(usable_weight[0])
    kernel_tile = wendland(row_blocks[0], reach_blocks, period) * listed[:, None, None]

    def apply_kernel(values, wide=False):
        width = values.shape[0]
        if wide:
            slab_values = halo_gather(values, 5, wide=False)
            parts = (shifted(slab_values, 1), slab_values, shifted(slab_values, -1))
            out = None
            for i, part in enumerate(parts):
                tile = kernel_tile[i * slab_blocks : (i + 1) * slab_blocks]
                term = jnp.einsum("ncj,nij->ci", part, tile, precision=lax.Precision.HIGHEST)
                out = term if out is None else out + term
            return out
        reach = halo_gather(values, 6)
        return jnp.einsum("ncj,nij->ci", reach, kernel_tile, precision=lax.Precision.HIGHEST)

    def slot(x):
        zeros = jnp.zeros((n_samp,) + x.shape, x.dtype)
        return lax.dynamic_update_index_in_dim(zeros, x, samp_idx, 0)

    def unslot(xs):
        return lax.dynamic_index_in_dim(xs, samp_idx, 0, keepdims=False)

    def total_per_samp(values):
        return jax.tree.map(unslot, lax.psum(jax.tree.map(slot, values), ALL_AXES))

    sketch_rows = omega.shape[0]
    omega_rows = lax.dynamic_slice_in_dim(omega, samp_idx * (sketch_rows // n_samp), sketch_rows // n_samp)
    sketch_own = apply_kernel(omega_rows, wide=True) + sketch_shift * omega_rows
    sketch = lax.all_gather(sketch_own, "samp", axis=0, tiled=True)
    rhs = observed[None, :] - prior_draws
    joint_part = 0.5 * (high_dot(omega_rows, sketch.T) + high_dot(sketch_own, omega.T)) + high_dot(
        sketch_own, sketch.T
    )
    gram_rows = joint_part.shape[1]
    width = rhs.shape[0]
    rhs_proj = high_dot(sketch, rhs.T).reshape(gram_rows * width // 128, 128)
    joint_gram, rhs_proj = gram_sum(joint_part.reshape(-1, 128), rhs_proj, 2)
    joint_gram = joint_gram.reshape(gram_rows, gram_rows)
    rhs_proj = rhs_proj.reshape(gram_rows, width)

    inverses, panels = blocked_factor(joint_gram)

    def precond_from(vectors, projected):
        solved = blocked_solve(inverses, panels, projected)
        return (vectors - high_dot(solved.T, sketch)) / noise_variance, solved

    residual = rhs
    projected = rhs_proj
    precond, _ = precond_from(residual, projected)
    direction = precond
    weights = jnp.zeros_like(rhs)

    sketch_rows = sketch.shape[0]

    def pack_scalars(*vectors):
        rows = jnp.stack(vectors)
        return jnp.pad(rows, ((0, 8 - rows.shape[0]), (0, 128 - width)))

    image = apply_kernel(direction) + noise_variance * direction
    image_proj = high_dot(sketch, image.T).reshape(sketch_rows * width // 128, 128)
    packed = jnp.concatenate(
        [
            image_proj,
            pack_scalars(
                jnp.sum(residual * precond, axis=1),
                jnp.sum(direction * image, axis=1),
                jnp.sum(residual * residual, axis=1),
                jnp.sum(residual * image, axis=1),
                jnp.sum(image * image, axis=1),
            ),
        ]
    )
    packed = group_sum(packed, 0)
    image_proj = packed[:-8].reshape(sketch_rows, width)
    inner_now = packed[-8, :width]
    curvature = packed[-7, :width]
    residual_sq, residual_image, image_sq = packed[-6, :width], packed[-5, :width], packed[-4, :width]
    step_size = inner_now / curvature
    weights = weights + step_size[:, None] * direction
    residual = residual - step_size[:, None] * image
    projected = projected - step_size[None, :] * image_proj
    precond, solved = precond_from(residual, projected)
    residual_sq = residual_sq - 2.0 * step_size * residual_image + step_size * step_size * image_sq
    inner_next = (residual_sq - jnp.sum(projected * solved, axis=0)) / noise_variance
    direction = precond + (inner_next / inner_now)[:, None] * direction
    inner_now = inner_next

    image = apply_kernel(direction) + noise_variance * direction
    curvature = group_sum(pack_scalars(jnp.sum(direction * image, axis=1)), 1)[0, :width]
    step_size = inner_now / curvature
    weights = weights + step_size[:, None] * direction
    residual = residual - step_size[:, None] * image
    return (weights, residual)


def solution(mesh):
    in_specs = (
        P(None, ("blk", "leaf")),
        P(("blk", "leaf"), None),
        P(None, ("blk", "leaf")),
        P(("blk", "leaf")),
        P("samp", ("blk", "leaf")),
    )
    out_specs = (P("samp", ("blk", "leaf")), P("samp", ("blk", "leaf")))
    return jax.shard_map(local, mesh=mesh, in_specs=in_specs, out_specs=out_specs, check_vma=False)
```

```python
import jax
import jax.numpy as jnp
from jax import lax
from jax.sharding import PartitionSpec as P
from jax.experimental import pallas as pl
from jax.experimental.pallas import tpu as pltpu

PB = 256
ITERS = 2


support_radius = 0.8
noise_variance = 1.0
sketch_shift = 1.0

ALL_AXES = ("blk", "leaf", "samp")


def shifted_2(block, axis, distance):
    devices = range(lax.axis_size(axis))
    route = [((i - distance) % len(devices), i) for i in devices]
    return lax.ppermute(block, axis, route)


def wendland(row_points, column_points, period):
    offset = row_points[None, :, :, None] - column_points[:, :, None, :]
    half_period = 0.5 * period
    along_x = jnp.mod(offset[:, 0] + half_period, period) - half_period
    squared = along_x * along_x + offset[:, 1] * offset[:, 1] + offset[:, 2] * offset[:, 2]
    radius = jnp.sqrt(squared) / support_radius
    remain = jnp.maximum(1.0 - radius, 0.0)
    return remain**4 * (4.0 * radius + 1.0)


def high_dot(left, right):
    return jnp.dot(left, right, precision=lax.Precision.HIGHEST, preferred_element_type=jnp.float32)


def shifted(values, offset_by):
    return shifted_2(values, "blk", offset_by)


def beside_all(values):
    slab_values = lax.all_gather(values, "leaf", axis=1, tiled=True)
    return jnp.concatenate([shifted(slab_values, 1), slab_values, shifted(slab_values, -1)], axis=1)


def blk_split(n_blk):
    if n_blk % 8 == 0 and n_blk > 8:
        return (8, n_blk // 8)
    return (n_blk, 1)


def reduce_phases():
    inner, outer = blk_split(lax.axis_size("blk"))
    phases = [("leaf", lax.axis_size("leaf"), 1), ("blk", inner, 1)]
    if outer > 1:
        phases.append(("blk", outer, inner))
    return tuple(p for p in phases if p[1] > 1)


def group_peer(axis, n, stride, k):
    idx = lax.axis_index(axis)
    own = (idx // stride) % n
    return own, idx + ((own + k) % n - own) * stride


def sum_kernel(phases, x_ref, o_ref, recv, send_sem, recv_sem):
    barrier = pltpu.get_barrier_semaphore()
    greeted = 0
    for axis, n, stride in phases:
        for k in range(1, n):
            _, peer = group_peer(axis, n, stride, k)
            pl.semaphore_signal(
                barrier, 1, device_id={axis: peer}, device_id_type=pl.DeviceIdType.MESH
            )
            greeted += 1
    pl.semaphore_wait(barrier, greeted)
    acc = x_ref[...]
    for p, (axis, n, stride) in enumerate(phases):
        recv[p, 0] = acc
        copies = []
        for k in range(1, n):
            own, peer = group_peer(axis, n, stride, k)
            copy = pltpu.make_async_remote_copy(
                src_ref=x_ref if p == 0 else recv.at[p, 0],
                dst_ref=recv.at[p, k],
                send_sem=send_sem.at[p, k],
                recv_sem=recv_sem.at[p, k],
                device_id={axis: peer},
                device_id_type=pl.DeviceIdType.MESH,
            )
            copy.start()
            copies.append(copy)
        for copy in copies:
            copy.wait()
        own, _ = group_peer(axis, n, stride, 0)
        terms = [recv[p, (own - j) % n] for j in range(n)]
        acc = terms[0]
        for term in terms[1:]:
            acc = acc + term
    o_ref[...] = acc


def group_sum(values, collective_id):
    phases = reduce_phases()
    rows = values.shape[0]
    widest = max(n for _, n, _ in phases)
    return pl.pallas_call(
        lambda *refs: sum_kernel(phases, *refs),
        out_shape=jax.ShapeDtypeStruct(values.shape, jnp.float32),
        in_specs=[pl.BlockSpec(memory_space=pltpu.VMEM)],
        out_specs=pl.BlockSpec(memory_space=pltpu.VMEM),
        scratch_shapes=[
            pltpu.VMEM((len(phases), widest, rows, 128), jnp.float32),
            pltpu.SemaphoreType.DMA((len(phases), widest)),
            pltpu.SemaphoreType.DMA((len(phases), widest)),
        ],
        compiler_params=pltpu.CompilerParams(collective_id=collective_id, has_side_effects=True),
    )(values)


def gram_kernel(phases, x_ref, y_ref, o_ref, z_ref, *scratch):
    count = len(phases)
    recvs = scratch[: count - 1]
    sums = scratch[count - 1 : 2 * count - 3]
    full = scratch[2 * count - 3]
    rs_send, rs_recv, ag_send, ag_recv, side, side_send, side_recv = scratch[2 * count - 2 :]
    side_acc = y_ref[...]
    outer_own, _ = group_peer(*phases[0], 0)
    barrier = pltpu.get_barrier_semaphore()
    greeted = 0
    for axis, n, stride in phases:
        for k in range(1, n):
            _, peer = group_peer(axis, n, stride, k)
            pl.semaphore_signal(
                barrier, 1, device_id={axis: peer}, device_id_type=pl.DeviceIdType.MESH
            )
            greeted += 1
    pl.semaphore_wait(barrier, greeted)
    source = x_ref
    length = x_ref.shape[0]
    offset = outer_own * length
    for p, (axis, n, stride) in enumerate(phases):
        if p == 0:
            continue
        own, _ = group_peer(axis, n, stride, 0)
        part = length // n
        recv = recvs[p - 1]
        recv[0] = source[pl.ds(pl.multiple_of(own * part, 8), part)]
        copies = []
        if axis != "samp":
            side[p, 0] = side_acc
            for k in range(1, n):
                _, peer = group_peer(axis, n, stride, k)
                copy = pltpu.make_async_remote_copy(
                    src_ref=side.at[p, 0],
                    dst_ref=side.at[p, k],
                    send_sem=side_send.at[p, k],
                    recv_sem=side_recv.at[p, k],
                    device_id={axis: peer},
                    device_id_type=pl.DeviceIdType.MESH,
                )
                copy.start()
                copies.append(copy)
        for k in range(1, n):
            _, peer = group_peer(axis, n, stride, k)
            chunk = (own + k) % n
            copy = pltpu.make_async_remote_copy(
                src_ref=source.at[pl.ds(pl.multiple_of(chunk * part, 8), part)],
                dst_ref=recv.at[k],
                send_sem=rs_send.at[p, k],
                recv_sem=rs_recv.at[p, k],
                device_id={axis: peer},
                device_id_type=pl.DeviceIdType.MESH,
            )
            copy.start()
            copies.append(copy)
        for copy in copies:
            copy.wait()
        acc = recv[own % n]
        for j in range(1, n):
            acc = acc + recv[(own - j) % n]
        if axis != "samp":
            side_acc = side[p, own % n]
            for j in range(1, n):
                side_acc = side_acc + side[p, (own - j) % n]
        offset = offset + own * part
        length = part
        if p < count - 1:
            sums[p - 1][...] = acc
            source = sums[p - 1]
        else:
            full[pl.ds(pl.multiple_of(offset, 8), part)] = acc
    for p in reversed(range(count)):
        axis, n, stride = phases[p]
        own, _ = group_peer(axis, n, stride, 0)
        here = full.at[pl.ds(pl.multiple_of(offset, 8), length)]
        copies = []
        for k in range(1, n):
            _, peer = group_peer(axis, n, stride, k)
            copy = pltpu.make_async_remote_copy(
                src_ref=here,
                dst_ref=here,
                send_sem=ag_send.at[p, k],
                recv_sem=ag_recv.at[p, k],
                device_id={axis: peer},
                device_id_type=pl.DeviceIdType.MESH,
            )
            copy.start()
            copies.append(copy)
        for copy in copies:
            copy.wait()
        offset = offset - own * length
        length = length * n
    o_ref[...] = full[...]
    z_ref[...] = side_acc


def gram_sum(values, side_values, collective_id):
    phases = (("samp", lax.axis_size("samp"), 1),) + reduce_phases()
    rows = values.shape[0]
    widest = max(n for _, n, _ in phases)
    recvs, sums = [], []
    length = rows
    for p, (_, n, _) in enumerate(phases):
        if p == 0:
            continue
        length //= n
        recvs.append(pltpu.VMEM((n, length, 128), jnp.float32))
        if p < len(phases) - 1:
            sums.append(pltpu.VMEM((length, 128), jnp.float32))
    rows = rows * phases[0][1]
    semaphores = [pltpu.SemaphoreType.DMA((len(phases), widest)) for _ in range(4)]
    side_scratch = [
        pltpu.VMEM((len(phases), widest) + side_values.shape, jnp.float32),
        pltpu.SemaphoreType.DMA((len(phases), widest)),
        pltpu.SemaphoreType.DMA((len(phases), widest)),
    ]
    return pl.pallas_call(
        lambda *refs: gram_kernel(phases, *refs),
        out_shape=(
            jax.ShapeDtypeStruct((rows, 128), jnp.float32),
            jax.ShapeDtypeStruct(side_values.shape, jnp.float32),
        ),
        in_specs=[pl.BlockSpec(memory_space=pltpu.VMEM)] * 2,
        out_specs=(pl.BlockSpec(memory_space=pltpu.VMEM),) * 2,
        scratch_shapes=recvs + sums + [pltpu.VMEM((rows, 128), jnp.float32)] + semaphores + side_scratch,
        compiler_params=pltpu.CompilerParams(collective_id=collective_id, has_side_effects=True),
    )(values, side_values)


def halo_kernel(n_blk, n_leaf, wide, x_ref, o_ref, land, send_sem, recv_sem):
    own_blk = lax.axis_index("blk")
    own_leaf = lax.axis_index("leaf")
    centre = n_leaf if wide else 0
    targets = []
    for d in (-1, 1) if wide else ():
        for leaf in range(n_leaf):
            targets.append(((own_blk + d + n_blk) % n_blk, leaf, (1 - d) * n_leaf + own_leaf))
    for k in range(1, n_leaf):
        targets.append((own_blk, (own_leaf + k) % n_leaf, centre + own_leaf))
    barrier = pltpu.get_barrier_semaphore()
    for blk, leaf, _ in targets:
        pl.semaphore_signal(
            barrier,
            1,
            device_id={"blk": blk, "leaf": leaf},
            device_id_type=pl.DeviceIdType.MESH,
        )
    pl.semaphore_wait(barrier, len(targets))
    copies = []
    for i, (blk, leaf, segment) in enumerate(targets):
        copy = pltpu.make_async_remote_copy(
            src_ref=x_ref,
            dst_ref=land.at[segment],
            send_sem=send_sem.at[i],
            recv_sem=recv_sem.at[segment],
            device_id={"blk": blk, "leaf": leaf},
            device_id_type=pl.DeviceIdType.MESH,
        )
        copy.start()
        copies.append(copy)
    land[centre + own_leaf] = x_ref[...]
    incoming = []
    if wide:
        incoming += [((own_blk - 1 + n_blk) % n_blk, s, s) for s in range(n_leaf)]
        incoming += [((own_blk + 1) % n_blk, s, 2 * n_leaf + s) for s in range(n_leaf)]
    for k in range(1, n_leaf):
        leaf = (own_leaf + k) % n_leaf
        incoming.append((own_blk, leaf, centre + leaf))
    for copy in copies:
        copy.wait_send()
    for blk, leaf, segment in incoming:
        pltpu.make_async_remote_copy(
            src_ref=x_ref,
            dst_ref=land.at[segment],
            send_sem=send_sem.at[0],
            recv_sem=recv_sem.at[segment],
            device_id={"blk": blk, "leaf": leaf},
            device_id_type=pl.DeviceIdType.MESH,
        ).wait_recv()
    o_ref[...] = land[...]


def halo_gather(values, collective_id, wide=True):
    n_blk = lax.axis_size("blk")
    n_leaf = lax.axis_size("leaf")
    segments = (3 if wide else 1) * n_leaf
    return pl.pallas_call(
        lambda *refs: halo_kernel(n_blk, n_leaf, wide, *refs),
        out_shape=jax.ShapeDtypeStruct((segments,) + values.shape, jnp.float32),
        in_specs=[pl.BlockSpec(memory_space=pltpu.VMEM)],
        out_specs=pl.BlockSpec(memory_space=pltpu.VMEM),
        scratch_shapes=[
            pltpu.VMEM((segments,) + values.shape, jnp.float32),
            pltpu.SemaphoreType.DMA((segments,)),
            pltpu.SemaphoreType.DMA((segments,)),
        ],
        compiler_params=pltpu.CompilerParams(collective_id=collective_id, has_side_effects=True),
    )(values)


def blocked_factor(gram, block=128):
    count = gram.shape[0] // block
    eye = jnp.eye(block, dtype=jnp.float32)
    inverses, panels = [], []
    rest = gram
    for k in range(count):
        diagonal = lax.linalg.cholesky(rest[:block, :block])
        inverse = lax.linalg.triangular_solve(diagonal, eye, left_side=True, lower=True)
        inverses.append(inverse)
        if k < count - 1:
            panel = high_dot(rest[block:, :block], inverse.T)
            panels.append(panel)
            rest = rest[block:, block:] - high_dot(panel, panel.T)
    return inverses, panels


def blocked_solve(inverses, panels, values):
    block = inverses[0].shape[0]
    count = len(inverses)
    lower = []
    rest = values
    for k in range(count):
        part = high_dot(inverses[k], rest[:block])
        lower.append(part)
        if k < count - 1:
            rest = rest[block:] - high_dot(panels[k], part)
    upper = [None] * count
    for k in reversed(range(count)):
        rhs = lower[k]
        if k < count - 1:
            rhs = rhs - high_dot(panels[k].T, jnp.concatenate(upper[k + 1 :]))
        upper[k] = high_dot(inverses[k].T, rhs)
    return jnp.concatenate(upper)


def lower_solve(factor, values):
    return lax.linalg.triangular_solve(factor, values, left_side=True, lower=True)


def local(points, neighbors, omega, observed, prior_draws):
    blk_dev = neighbors.shape[0]
    cycle_count = lax.axis_size("blk")
    slab_blocks = blk_dev * lax.axis_size("leaf")
    period = 2.0 * cycle_count
    own_slab = lax.axis_index("blk")
    n_samp = lax.axis_size("samp")
    samp_idx = lax.axis_index("samp")
    usable = neighbors >= 0
    relative = jnp.mod(neighbors // slab_blocks - own_slab + 1, cycle_count)
    chosen = jnp.where(usable, relative * slab_blocks + jnp.mod(neighbors, slab_blocks), 0)
    usable_weight = usable.astype(jnp.float32)
    reach_blocks = halo_gather(points, 4)
    row_blocks = points.reshape(3, blk_dev, PB).transpose(1, 0, 2)

    segments = 3 * slab_blocks
    listed = jnp.zeros((segments,), jnp.float32).at[chosen[0]].max(usable_weight[0])
    kernel_tile = wendland(row_blocks[0], reach_blocks, period) * listed[:, None, None]

    def apply_kernel(values, wide=False):
        width = values.shape[0]
        if wide:
            slab_values = halo_gather(values, 5, wide=False)
            parts = (shifted(slab_values, 1), slab_values, shifted(slab_values, -1))
            out = None
            for i, part in enumerate(parts):
                tile = kernel_tile[i * slab_blocks : (i + 1) * slab_blocks]
                term = jnp.einsum("ncj,nij->ci", part, tile, precision=lax.Precision.HIGHEST)
                out = term if out is None else out + term
            return out
        reach = halo_gather(values, 6)
        return jnp.einsum("ncj,nij->ci", reach, kernel_tile, precision=lax.Precision.HIGHEST)

    def slot(x):
        zeros = jnp.zeros((n_samp,) + x.shape, x.dtype)
        return lax.dynamic_update_index_in_dim(zeros, x, samp_idx, 0)

    def unslot(xs):
        return lax.dynamic_index_in_dim(xs, samp_idx, 0, keepdims=False)

    def total_per_samp(values):
        return jax.tree.map(unslot, lax.psum(jax.tree.map(slot, values), ALL_AXES))

    sketch_rows = omega.shape[0]
    omega_rows = lax.dynamic_slice_in_dim(omega, samp_idx * (sketch_rows // n_samp), sketch_rows // n_samp)
    reach_blocks, omega_rows = lax.optimization_barrier((reach_blocks, omega_rows))
    sketch_own = apply_kernel(omega_rows, wide=True) + sketch_shift * omega_rows
    sketch = lax.all_gather(sketch_own, "samp", axis=0, tiled=True)
    rhs = observed[None, :] - prior_draws
    joint_part = 0.5 * (high_dot(omega_rows, sketch.T) + high_dot(sketch_own, omega.T)) + high_dot(
        sketch_own, sketch.T
    )
    gram_rows = joint_part.shape[1]
    width = rhs.shape[0]
    rhs_proj = high_dot(sketch, rhs.T).reshape(gram_rows * width // 128, 128)
    joint_gram, rhs_proj = gram_sum(joint_part.reshape(-1, 128), rhs_proj, 2)
    joint_gram = joint_gram.reshape(gram_rows, gram_rows)
    rhs_proj = rhs_proj.reshape(gram_rows, width)

    inverses, panels = blocked_factor(joint_gram)

    def precond_from(vectors, projected):
        solved = blocked_solve(inverses, panels, projected)
        return (vectors - high_dot(solved.T, sketch)) / noise_variance, solved

    residual = rhs
    projected = rhs_proj
    precond, _ = precond_from(residual, projected)
    direction = precond
    weights = jnp.zeros_like(rhs)

    sketch_rows = sketch.shape[0]

    def pack_scalars(*vectors):
        rows = jnp.stack(vectors)
        return jnp.pad(rows, ((0, 8 - rows.shape[0]), (0, 128 - width)))

    image = apply_kernel(direction) + noise_variance * direction
    image_proj = high_dot(sketch, image.T).reshape(sketch_rows * width // 128, 128)
    packed = jnp.concatenate(
        [
            image_proj,
            pack_scalars(
                jnp.sum(residual * precond, axis=1),
                jnp.sum(direction * image, axis=1),
                jnp.sum(residual * residual, axis=1),
                jnp.sum(residual * image, axis=1),
                jnp.sum(image * image, axis=1),
            ),
        ]
    )
    packed = group_sum(packed, 0)
    image_proj = packed[:-8].reshape(sketch_rows, width)
    inner_now = packed[-8, :width]
    curvature = packed[-7, :width]
    residual_sq, residual_image, image_sq = packed[-6, :width], packed[-5, :width], packed[-4, :width]
    step_size = inner_now / curvature
    weights = weights + step_size[:, None] * direction
    residual = residual - step_size[:, None] * image
    projected = projected - step_size[None, :] * image_proj
    precond, solved = precond_from(residual, projected)
    residual_sq = residual_sq - 2.0 * step_size * residual_image + step_size * step_size * image_sq
    inner_next = (residual_sq - jnp.sum(projected * solved, axis=0)) / noise_variance
    direction = precond + (inner_next / inner_now)[:, None] * direction
    inner_now = inner_next

    image = apply_kernel(direction) + noise_variance * direction
    curvature = group_sum(pack_scalars(jnp.sum(direction * image, axis=1)), 1)[0, :width]
    step_size = inner_now / curvature
    weights = weights + step_size[:, None] * direction
    residual = residual - step_size[:, None] * image
    return (weights, residual)


def solution(mesh):
    in_specs = (
        P(None, ("blk", "leaf")),
        P(("blk", "leaf"), None),
        P(None, ("blk", "leaf")),
        P(("blk", "leaf")),
        P("samp", ("blk", "leaf")),
    )
    out_specs = (P("samp", ("blk", "leaf")), P("samp", ("blk", "leaf")))
    return jax.shard_map(local, mesh=mesh, in_specs=in_specs, out_specs=out_specs, check_vma=False)
```
